32 devices in a mesh: dp: 8 (over z, x), fsdp: 4 (over y, core).
Axes of the slice: x: 2, y: 2, z: 4, core: 2. Of those that a mesh axis runs over, the one named last changes fastest.
Arguments:
- tokens: bfloat16 [12288, 1280], P(('dp', 'fsdp')), may hold values from -6 to 6
- teacher: bfloat16 [12288, 1280], P(('dp', 'fsdp')), may hold values from -6 to 6
- picture: int32 [12288], P(('dp', 'fsdp')), may hold values from 0 to 767, as said below
- places: int32 [12288, 2], P(('dp', 'fsdp')), may hold values from 0 to 15, as said below
- validity: int32 [12288], P(('dp', 'fsdp')), may hold values from 0 to 1, as said below
- first_gain: bfloat16 [1280], P('dp'), may hold values from 0.5 to 1.5
- first_shift: bfloat16 [1280], P('dp'), may hold values from -1.5 to 1.5
- mixer_weight: bfloat16 [1280, 3, 1280], P('dp', None, 'fsdp'), may hold values from -0.15625 to 0.15625
- mixer_bias: bfloat16 [3840], P('dp'), may hold values from -1.5 to 1.5
- output_weight: bfloat16 [1280, 1280], P('fsdp', 'dp'), may hold values from -0.625 to 0.625
- output_bias: bfloat16 [1280], P('dp'), may hold values from -1.5 to 1.5
- second_gain: bfloat16 [1280], P('dp'), may hold values from 0.5 to 1.5
- second_shift: bfloat16 [1280], P('dp'), may hold values from -1.5 to 1.5
- upward_weight: bfloat16 [1280, 5120], P('dp', 'fsdp'), may hold values from -0.15625 to 0.15625
- upward_bias: bfloat16 [5120], P('dp'), may hold values from -1.5 to 1.5
- downward_weight: bfloat16 [5120, 1280], P('fsdp', 'dp'), may hold values from -0.125 to 0.125
- downward_bias: bfloat16 [1280], P('dp'), may hold values from -1.5 to 1.5
Outputs:
- result: bfloat16 [12288, 1280], P(('dp', 'fsdp'))
- loss: float32 [], replicated
- grad_tokens: float32 [12288, 1280], P(('dp', 'fsdp'))
- grad_first_gain: float32 [1280], P('dp')
- grad_first_shift: float32 [1280], P('dp')
- grad_mixer_weight: float32 [1280, 3, 1280], P('dp', None, 'fsdp')
- grad_mixer_bias: float32 [2560], P('dp')
- grad_value_bias: float32 [1280], P('dp')
- grad_output_weight: float32 [1280, 1280], P('fsdp', 'dp')
- grad_output_bias: float32 [1280], P('dp')
- grad_second_gain: float32 [1280], P('dp')
- grad_second_shift: float32 [1280], P('dp')
- grad_upward_weight: float32 [1280, 5120], P('dp', 'fsdp')
- grad_upward_bias: float32 [5120], P('dp')
- grad_downward_weight: float32 [5120, 1280], P('fsdp', 'dp')
- grad_downward_bias: float32 [1280], P('dp')
The draws below stay inside these ranges and needn't reach their ends.
Inputs may be any that keep to these rules, and one draw needn't show every extreme that they name: Pictures never span rows; along a row the picture numbers never fall, each picture holds 16 to 64 patches except the one that the row's end cuts. A patch's places are its row and column in a picture of 4 to 16 columns, filled row by row; rows stay under 64 // 4 + 1. `validity`: padding only ends a row; every row has real patches.
All inputs are finite; a program needn't handle non-finite values.
Results may differ from the reference program's by a relative error of at most 0.014.
Values may be sent and summed in bfloat16 or wider, within the bound.
A program may use at most 192 MiB of HBM per device.

```python
import math
import jax
import jax.numpy as jnp
from jax import lax

D = 1280
HEADS = 16
HD = 80
FF = 5120
ROW_PATCHES = 128
TOTAL_PATCHES = 12288
PICMIN = 16
PICMAX = 64
MAXPICS = 8


def layout(key):
    rows_all = TOTAL_PATCHES // ROW_PATCHES
    base = jax.random.fold_in(key, 11)
    first, second, third = jax.random.split(base, 3)
    lengths = jax.random.randint(first, (rows_all, MAXPICS), PICMIN, PICMAX + 1)
    starts = jnp.cumsum(lengths, axis=1) - lengths
    widths = jax.random.randint(second, (rows_all, MAXPICS), 4, 17)
    slot_index = jnp.arange(ROW_PATCHES, dtype=jnp.int32)
    inside = (starts[:, None, :] <= slot_index[None, :, None]).astype(jnp.int32)
    member = jnp.sum(inside, axis=2) - 1
    start_here = jnp.take_along_axis(starts, member, axis=1)
    width_here = jnp.take_along_axis(widths, member, axis=1)
    offset = slot_index[None, :] - start_here
    row_index = jnp.arange(rows_all, dtype=jnp.int32)
    filler_slots = 2 * ROW_PATCHES // 3 * row_index // rows_all + jax.random.randint(third, (rows_all,), 0, ROW_PATCHES // 8 + 1)
    occupancy_flags = (slot_index[None, :] < (ROW_PATCHES - filler_slots)[:, None]).astype(jnp.int32)
    picture_labels = row_index[:, None] * MAXPICS + member
    positioned_patches = jnp.stack([offset // width_here, offset % width_here], axis=-1)
    return (picture_labels.reshape(TOTAL_PATCHES).astype(jnp.int32), positioned_patches.reshape(TOTAL_PATCHES, 2).astype(jnp.int32), occupancy_flags.reshape(TOTAL_PATCHES))


def draw_picture(key, part):
    return layout(key)[0]


def draw_places(key, part):
    return layout(key)[1]


def draw_validity(key, part):
    return layout(key)[2]


def level_of(rng, extent, cuts, least, largest):
    def one(dim, parts):
        draws = jax.random.uniform(jax.random.fold_in(jax.random.fold_in(rng, 6), dim), (parts,), jnp.float32, least / len(cuts), largest / len(cuts))
        return jnp.repeat(jnp.exp(draws), extent[dim] // parts).reshape((-1,) + (1,) * (len(extent) - dim - 1))

    gain = one(*cuts[0])
    for cut in cuts[1:]:
        gain = gain * one(*cut)
    return gain


def bell_draw(key, dims, spread, reach, shards=(), held_as=jnp.bfloat16):
    drawn = spread * jax.random.normal(key, dims, jnp.float32)
    if shards:
        drawn = drawn * level_of(key, dims, shards, -0.22, 0.18)
    return jnp.clip(drawn, -reach, reach).astype(held_as)


def setup_inputs(seed: int = 0) -> dict:
    streams_of = jax.random.split(jax.random.key(seed), 18)
    return {
        "tokens": bell_draw(streams_of[0], (TOTAL_PATCHES, D), 1.0, 6.0, ((0, 32),)),
        "teacher": bell_draw(streams_of[1], (TOTAL_PATCHES, D), 1.0, 6.0, ((0, 32),)),
        "picture": draw_picture(jax.random.fold_in(streams_of[17], 71), 0),
        "places": draw_places(jax.random.fold_in(streams_of[17], 71), 0),
        "validity": draw_validity(jax.random.fold_in(streams_of[17], 71), 0),
        "first_gain": jnp.clip(1.0 + 0.1 * jax.random.normal(streams_of[5], (D,), jnp.float32), 0.5, 1.5).astype(jnp.bfloat16),
        "first_shift": bell_draw(streams_of[6], (D,), 0.3, 1.5, ((0, 8),)),
        "mixer_weight": bell_draw(streams_of[7], (D, 3, D), D ** -0.5, 0.15625, ((0, 8), (2, 4))),
        "mixer_bias": bell_draw(streams_of[8], (3 * D,), 0.3, 1.5, ((0, 8),)),
        "output_weight": bell_draw(streams_of[9], (D, D), (D // 16) ** -0.5, 0.625, ((0, 4), (1, 8))),
        "output_bias": bell_draw(streams_of[10], (D,), 0.3, 1.5, ((0, 8),)),
        "second_gain": jnp.clip(1.0 + 0.1 * jax.random.normal(streams_of[11], (D,), jnp.float32), 0.5, 1.5).astype(jnp.bfloat16),
        "second_shift": bell_draw(streams_of[12], (D,), 0.3, 1.5, ((0, 8),)),
        "upward_weight": bell_draw(streams_of[13], (D, FF), D ** -0.5, 0.15625, ((0, 8), (1, 4))),
        "upward_bias": bell_draw(streams_of[14], (FF,), 0.3, 1.5, ((0, 8),)),
        "downward_weight": bell_draw(streams_of[15], (FF, D), (FF // 2) ** -0.5, 0.125, ((0, 4), (1, 8))),
        "downward_bias": bell_draw(streams_of[16], (D,), 0.3, 1.5, ((0, 8),)),
    }


@jax.custom_vjp
def low(v):
    return lax.optimization_barrier(v.astype(jnp.bfloat16)).astype(jnp.float32)

@jax.custom_vjp
def low_back(v):
    return v

def low_keep(v):
    return (low(v), None)

def low_pass(kept, grad):
    return (grad,)

def back_keep(v):
    return (v, None)

def back_low(kept, grad):
    return (low(grad),)
low.defvjp(low_keep, low_pass)
low_back.defvjp(back_keep, back_low)
EPSILON = 1e-06
HIGH = lax.Precision.HIGHEST

def norm_layer(values, scaler, offset):
    average = lax.optimization_barrier(jnp.mean(values, axis=-1, keepdims=True))
    centered = values - average
    variance = lax.optimization_barrier(jnp.mean(centered * centered, axis=-1, keepdims=True))
    return centered * lax.rsqrt(variance + EPSILON) * scaler + offset

def tables(places):
    quarter = HD // 4
    frequency = 1.0 / 10000.0 ** (jnp.arange(quarter, dtype=jnp.float32) * 4.0 / HD)
    row_angle = places[:, 0:1].astype(jnp.float32) * frequency
    col_angle = places[:, 1:2].astype(jnp.float32) * frequency
    angle_all = jnp.concatenate([row_angle, col_angle, row_angle, col_angle], axis=-1)
    return (jnp.cos(angle_all)[:, None, :], jnp.sin(angle_all)[:, None, :])

def rotate(values, cosine, sine):
    halfway = HD // 2
    flipped = jnp.concatenate([-values[..., halfway:], values[..., :halfway]], axis=-1)
    return values * cosine + flipped * sine

def group_pass(params, inputs, target, picture, places, validity):
    first_gain, first_shift, mixer_weight, mixer_bias, output_weight, output_bias, second_gain, second_shift, upward_weight, upward_bias, downward_weight, downward_bias = params
    count_rows = inputs.shape[0]
    normed_one = low(norm_layer(inputs, first_gain, first_shift))
    mixer_flat = mixer_weight.reshape(D, 3 * D)
    mixed = low_back(jnp.dot(normed_one, mixer_flat, precision=HIGH) + mixer_bias)
    mixed = mixed.reshape(count_rows, 3, HEADS, HD)
    cosine, sine = tables(places)
    query = low(rotate(mixed[:, 0], cosine, sine)).reshape(-1, ROW_PATCHES, HEADS, HD)
    key_rows = low(rotate(mixed[:, 1], cosine, sine)).reshape(-1, ROW_PATCHES, HEADS, HD)
    value_rows = low(mixed[:, 2]).reshape(-1, ROW_PATCHES, HEADS, HD)
    picture_rows = picture.reshape(-1, ROW_PATCHES)
    occupancy_flags = validity.reshape(-1, ROW_PATCHES) > 0
    shared_picture_mask = picture_rows[:, :, None] == picture_rows[:, None, :]
    self_pairs = jnp.eye(ROW_PATCHES, dtype=bool)[None]
    permitted_pairs = (shared_picture_mask & occupancy_flags[:, None, :] | self_pairs)[:, None]
    products = jnp.einsum('bqhd,bkhd->bhqk', query, key_rows, precision=HIGH) * HD ** (-0.5)
    scores = low_back(jnp.where(permitted_pairs, products, -1e+30))
    probs = low(jax.nn.softmax(scores, axis=-1))
    attended = jnp.einsum('bhqk,bkhd->bqhd', probs, value_rows, precision=HIGH).reshape(count_rows, D)
    attended = low(low_back(attended))
    branch = low_back(jnp.dot(attended, output_weight, precision=HIGH) + output_bias)
    middle = inputs + branch
    normed_two = low(norm_layer(middle, second_gain, second_shift))
    upper = low_back(jnp.dot(normed_two, upward_weight, precision=HIGH) + upward_bias)
    active = low(upper * jax.nn.sigmoid(1.702 * upper))
    lowered = low_back(jnp.dot(active, downward_weight, precision=HIGH) + downward_bias)
    result = middle + lowered
    difference = result - target
    errors = jnp.sum(validity.astype(jnp.float32)[:, None] * difference * difference)
    return (result, errors)

def reference(tokens, teacher, picture, places, validity, first_gain, first_shift, mixer_weight, mixer_bias, output_weight, output_bias, second_gain, second_shift, upward_weight, upward_bias, downward_weight, downward_bias):
    params = tuple((item.astype(jnp.float32) for item in (first_gain, first_shift, mixer_weight, mixer_bias, output_weight, output_bias, second_gain, second_shift, upward_weight, upward_bias, downward_weight, downward_bias)))
    inputs = tokens.astype(jnp.float32)
    target = teacher.astype(jnp.float32)
    token_tally = jnp.sum(validity).astype(jnp.float32)
    group_rows = math.gcd(TOTAL_PATCHES // ROW_PATCHES, max(1, 4096 // ROW_PATCHES)) * ROW_PATCHES
    groups = TOTAL_PATCHES // group_rows
    stepper = jax.checkpoint(group_pass)

    def whole(values, weights):

        def one_group(carry, pieces):
            result, errors = stepper(weights, pieces[0], pieces[1], pieces[2], pieces[3], pieces[4])
            return (carry + errors, result)
        pieces = (values.reshape(groups, group_rows, D), target.reshape(groups, group_rows, D), picture.reshape(groups, group_rows), places.reshape(groups, group_rows, 2), validity.reshape(groups, group_rows))
        total, result = lax.scan(one_group, jnp.zeros((), jnp.float32), pieces)
        return (result.reshape(TOTAL_PATCHES, D), total)
    (result, total), pullback = jax.vjp(whole, inputs, params)
    scaling = TOTAL_PATCHES / token_tally
    grad_inputs, grads = pullback((jnp.zeros_like(result), scaling))
    loss = total / (token_tally * D)
    return (result.astype(jnp.bfloat16), loss, grad_inputs, grads[0], grads[1], grads[2], grads[3][:2 * D], grads[3][2 * D:], grads[4], grads[5], grads[6], grads[7], grads[8], grads[9], grads[10], grads[11])
```

```python
import numpy as np
import jax
import jax.numpy as jnp
from jax import lax
from jax.experimental import pallas as pl
from jax.experimental.pallas import tpu as pltpu
from jax.sharding import PartitionSpec as P

D = 1280
HD = 80
FF = 5120
ROW_PATCHES = 128
MB = 3


EPSILON = 1e-06


def norm_forward(values, scaler, offset):
    average = jnp.mean(values, axis=-1, keepdims=True)
    centered = values - average
    reciprocal = lax.rsqrt(jnp.mean(centered * centered, axis=-1, keepdims=True) + EPSILON)
    normed = centered * reciprocal
    return (normed * scaler.astype(jnp.float32) + offset.astype(jnp.float32), normed, reciprocal)


def norm_backward(gradient, normed, reciprocal, scaler):
    scaled = gradient * scaler.astype(jnp.float32)
    adjusted = (
        scaled
        - jnp.mean(scaled, axis=-1, keepdims=True)
        - normed * jnp.mean(scaled * normed, axis=-1, keepdims=True)
    )
    return (adjusted * reciprocal, jnp.sum(gradient * normed, axis=0), jnp.sum(gradient, axis=0))


def tables(places):
    quarter = HD // 4
    frequency = 1.0 / 10000.0 ** (jnp.arange(quarter, dtype=jnp.float32) * 4.0 / HD)
    row_angle = places[:, 0:1].astype(jnp.float32) * frequency
    col_angle = places[:, 1:2].astype(jnp.float32) * frequency
    angle_all = jnp.concatenate([row_angle, col_angle, row_angle, col_angle], axis=-1)
    return (jnp.cos(angle_all)[:, None, :], jnp.sin(angle_all)[:, None, :])


def rotate(values, cosine, sine):
    halfway = HD // 2
    flipped = jnp.concatenate([-values[..., halfway:], values[..., :halfway]], axis=-1)
    return values * cosine + flipped * sine


def unrotate(gradient, cosine, sine):
    halfway = HD // 2
    shifted = gradient * sine
    return gradient * cosine + jnp.concatenate(
        [shifted[..., halfway:], -shifted[..., :halfway]], axis=-1
    )


def allowed_mask(picture, validity):
    picture_rows = picture.reshape(-1, ROW_PATCHES)
    occupancy_flags = validity.reshape(-1, ROW_PATCHES) > 0
    shared_picture_mask = picture_rows[:, :, None] == picture_rows[:, None, :]
    self_pairs = jnp.eye(ROW_PATCHES, dtype=bool)[None]
    return (shared_picture_mask & occupancy_flags[:, None, :] | self_pairs)[:, None]


def scores_of(query, key_rows, permitted_pairs):
    products = jnp.einsum(
        "bqhd,bkhd->bhqk", query, key_rows, preferred_element_type=jnp.float32
    ) * HD ** (-0.5)
    return jnp.where(permitted_pairs, products, -1e30)


def attend(query, key_rows, value_rows, permitted_pairs):
    scores = scores_of(query, key_rows, permitted_pairs)
    maximum = jnp.max(scores, axis=-1, keepdims=True)
    log_total = maximum + jnp.log(jnp.sum(jnp.exp(scores - maximum), axis=-1, keepdims=True))
    probs = jnp.exp(scores - log_total).astype(jnp.bfloat16)
    attended = jnp.einsum("bhqk,bkhd->bqhd", probs, value_rows, preferred_element_type=jnp.float32)
    return (attended, log_total)


def attend_back(grad_attended, query, key_rows, value_rows, permitted_pairs, log_total):
    scores = scores_of(query, key_rows, permitted_pairs)
    probs = jnp.exp(scores - log_total)
    grad_probs = jnp.einsum(
        "bqhd,bkhd->bhqk", grad_attended, value_rows, preferred_element_type=jnp.float32
    )
    delta = jnp.sum(grad_probs * probs, axis=-1, keepdims=True)
    grad_scores = (probs * (grad_probs - delta)).astype(jnp.bfloat16)
    scaling = HD ** (-0.5)
    grad_query = (
        jnp.einsum("bhqk,bkhd->bqhd", grad_scores, key_rows, preferred_element_type=jnp.float32)
        * scaling
    )
    grad_key = (
        jnp.einsum("bhqk,bqhd->bkhd", grad_scores, query, preferred_element_type=jnp.float32)
        * scaling
    )
    grad_value = jnp.einsum(
        "bhqk,bqhd->bkhd",
        probs.astype(jnp.bfloat16),
        grad_attended,
        preferred_element_type=jnp.float32,
    )
    return (grad_query, grad_key, grad_value)


def quick_gelu_grad(grad_active, upper):
    sigmoid_up = jax.nn.sigmoid(1.702 * upper)
    return (grad_active * (sigmoid_up + 1.702 * upper * sigmoid_up * (1.0 - sigmoid_up))).astype(
        jnp.bfloat16
    )


def own_slice(vector, data_index, data_ways):
    length = vector.shape[0] // data_ways
    return lax.dynamic_slice_in_dim(vector, data_index * length, length, 0)


def on_device(
    tokens,
    teacher,
    picture,
    places,
    validity,
    first_gain,
    first_shift,
    mixer_weight,
    mixer_bias,
    output_weight,
    output_bias,
    second_gain,
    second_shift,
    upward_weight,
    upward_bias,
    downward_weight,
    downward_bias,
):
    data_ways = lax.axis_size("dp")
    split_ways = lax.axis_size("fsdp")
    member = lax.axis_index("fsdp")
    data_index = lax.axis_index("dp")
    occupancy_flags = validity.astype(jnp.float32)
    token_tally = lax.psum(jnp.sum(occupancy_flags), ("dp", "fsdp"))
    factor = tokens.shape[0] * data_ways * split_ways / token_tally
    (
        mixer_local,
        output_local,
        upward_local,
        downward_local,
        gain_one,
        shift_one,
        mixer_shift,
        output_shift,
        gain_two,
        shift_two,
        upward_shift,
        downward_shift,
    ) = (
        lax.all_gather(mixer_weight, "dp", axis=0, tiled=True),
        lax.all_gather(output_weight, "dp", axis=1, tiled=True),
        lax.all_gather(upward_weight, "dp", axis=0, tiled=True),
        lax.all_gather(downward_weight, "dp", axis=1, tiled=True),
        lax.all_gather(first_gain, "dp", axis=0, tiled=True),
        lax.all_gather(first_shift, "dp", axis=0, tiled=True),
        lax.all_gather(mixer_bias, "dp", axis=0, tiled=True),
        lax.all_gather(output_bias, "dp", axis=0, tiled=True),
        lax.all_gather(second_gain, "dp", axis=0, tiled=True),
        lax.all_gather(second_shift, "dp", axis=0, tiled=True),
        lax.all_gather(upward_bias, "dp", axis=0, tiled=True),
        lax.all_gather(downward_bias, "dp", axis=0, tiled=True),
    )
    width_local = output_local.shape[0]
    heads_local = width_local // HD
    hidden_local = upward_local.shape[1]
    mixer_flat = mixer_local.reshape(D, 3 * width_local)
    mixer_piece = lax.dynamic_slice_in_dim(
        mixer_shift.reshape(3, D), member * width_local, width_local, 1
    )
    mixer_piece = mixer_piece.reshape(3 * width_local).astype(jnp.float32)
    upward_piece = lax.dynamic_slice_in_dim(
        upward_shift, member * hidden_local, hidden_local, 0
    ).astype(jnp.float32)
    packed_rows = tokens.shape[0] // MB
    errors = jnp.zeros((), jnp.float32)
    matrix_sums = None
    small_sums = None
    results = []
    input_grads = []
    for micro in range(MB):
        start_offset = micro * packed_rows
        inputs = tokens[start_offset : start_offset + packed_rows].astype(jnp.float32)
        target = teacher[start_offset : start_offset + packed_rows].astype(jnp.float32)
        occupied_rows = occupancy_flags[start_offset : start_offset + packed_rows]
        picture_rows = picture[start_offset : start_offset + packed_rows]
        local_picture = (picture_rows - picture_rows[0]).astype(jnp.bfloat16)
        place_rows = places[start_offset : start_offset + packed_rows].astype(jnp.bfloat16)
        live_marks = validity[start_offset : start_offset + packed_rows].astype(jnp.bfloat16)
        shifted_one, normed_one, recip_one = norm_forward(inputs, gain_one, shift_one)
        lowered_one = shifted_one.astype(jnp.bfloat16)
        group_one, group_picture, group_places, group_live = (
            lax.all_gather(lowered_one, "fsdp", axis=0, tiled=True),
            lax.all_gather(local_picture, "fsdp", axis=0, tiled=True),
            lax.all_gather(place_rows, "fsdp", axis=0, tiled=True),
            lax.all_gather(live_marks, "fsdp", axis=0, tiled=True),
        )
        group_rows = group_one.shape[0]
        mixed = jnp.dot(group_one, mixer_flat, preferred_element_type=jnp.float32) + mixer_piece
        mixed = mixed.reshape(group_rows, 3, heads_local, HD)
        cosine, sine = tables(group_places)
        query = (
            rotate(mixed[:, 0], cosine, sine)
            .astype(jnp.bfloat16)
            .reshape(-1, ROW_PATCHES, heads_local, HD)
        )
        key_rows = (
            rotate(mixed[:, 1], cosine, sine)
            .astype(jnp.bfloat16)
            .reshape(-1, ROW_PATCHES, heads_local, HD)
        )
        value_rows = mixed[:, 2].astype(jnp.bfloat16).reshape(-1, ROW_PATCHES, heads_local, HD)
        permitted_pairs = allowed_mask(group_picture, group_live)
        attended, log_total = attend(query, key_rows, value_rows, permitted_pairs)
        attended = attended.reshape(group_rows, width_local).astype(jnp.bfloat16)
        branch = lax.psum_scatter(
            jnp.dot(attended, output_local, preferred_element_type=jnp.float32).astype(
                jnp.bfloat16
            ),
            "fsdp",
            scatter_dimension=0,
            tiled=True,
        ).astype(jnp.float32)
        middle = inputs + branch + output_shift.astype(jnp.float32)
        shifted_two, normed_two, recip_two = norm_forward(middle, gain_two, shift_two)
        lowered_two = shifted_two.astype(jnp.bfloat16)
        group_two = lax.all_gather(lowered_two, "fsdp", axis=0, tiled=True)
        upper = jnp.dot(group_two, upward_local, preferred_element_type=jnp.float32) + upward_piece
        active = (upper * jax.nn.sigmoid(1.702 * upper)).astype(jnp.bfloat16)
        lowered = lax.psum_scatter(
            jnp.dot(active, downward_local, preferred_element_type=jnp.float32).astype(
                jnp.bfloat16
            ),
            "fsdp",
            scatter_dimension=0,
            tiled=True,
        ).astype(jnp.float32)
        outputs = middle + lowered + downward_shift.astype(jnp.float32)
        difference = outputs - target
        masked = occupied_rows[:, None] * difference
        errors = errors + jnp.sum(masked * difference)
        grad_out = 2.0 * factor * masked
        grad_low = grad_out.astype(jnp.bfloat16)
        down_bias_term = jnp.sum(grad_low.astype(jnp.float32), axis=0)
        group_grad = lax.all_gather(grad_low, "fsdp", axis=0, tiled=True)
        g_down = jnp.einsum("rf,rd->fd", active, group_grad, preferred_element_type=jnp.float32)
        grad_active = jnp.einsum(
            "rd,fd->rf", group_grad, downward_local, preferred_element_type=jnp.float32
        )
        grad_upper = quick_gelu_grad(grad_active, upper)
        g_up = jnp.einsum("rd,rf->df", group_two, grad_upper, preferred_element_type=jnp.float32)
        up_bias_term = lax.dynamic_update_slice_in_dim(
            jnp.zeros((FF,), jnp.float32),
            jnp.sum(grad_upper.astype(jnp.float32), axis=0),
            member * hidden_local,
            0,
        )
        grad_two = lax.psum_scatter(
            jnp.einsum(
                "rf,df->rd", grad_upper, upward_local, preferred_element_type=jnp.float32
            ).astype(jnp.bfloat16),
            "fsdp",
            scatter_dimension=0,
            tiled=True,
        ).astype(jnp.float32)
        back_two, g_gain_two, g_shift_two = norm_backward(grad_two, normed_two, recip_two, gain_two)
        grad_middle = grad_out + back_two
        grad_branch = grad_middle.astype(jnp.bfloat16)
        out_bias_term = jnp.sum(grad_branch.astype(jnp.float32), axis=0)
        group_branch = lax.all_gather(grad_branch, "fsdp", axis=0, tiled=True)
        g_output = jnp.einsum(
            "rd,re->de", attended, group_branch, preferred_element_type=jnp.float32
        )
        grad_attended = jnp.einsum(
            "re,de->rd", group_branch, output_local, preferred_element_type=jnp.float32
        )
        grad_attended = grad_attended.astype(jnp.bfloat16).reshape(-1, ROW_PATCHES, heads_local, HD)
        grad_query, grad_key, grad_value = attend_back(
            grad_attended, query, key_rows, value_rows, permitted_pairs, log_total
        )
        grad_mixed = jnp.stack(
            [
                unrotate(grad_query.reshape(group_rows, heads_local, HD), cosine, sine),
                unrotate(grad_key.reshape(group_rows, heads_local, HD), cosine, sine),
                grad_value.reshape(group_rows, heads_local, HD),
            ],
            axis=1,
        )
        grad_mixed = grad_mixed.reshape(group_rows, 3 * width_local).astype(jnp.bfloat16)
        g_mixer = jnp.einsum("rd,re->de", group_one, grad_mixed, preferred_element_type=jnp.float32)
        g_mixer = g_mixer.reshape(D, 3, width_local)
        mixer_bias_term = lax.dynamic_update_slice_in_dim(
            jnp.zeros((3, D), jnp.float32),
            jnp.sum(grad_mixed.astype(jnp.float32), axis=0).reshape(3, width_local),
            member * width_local,
            1,
        )
        mixer_bias_term = mixer_bias_term.reshape(3 * D)
        grad_one = lax.psum_scatter(
            jnp.einsum(
                "re,de->rd", grad_mixed, mixer_flat, preferred_element_type=jnp.float32
            ).astype(jnp.bfloat16),
            "fsdp",
            scatter_dimension=0,
            tiled=True,
        ).astype(jnp.float32)
        back_one, g_gain_one, g_shift_one = norm_backward(grad_one, normed_one, recip_one, gain_one)
        grad_inputs = grad_middle + back_one
        matrices = (g_mixer, g_output, g_up, g_down)
        smalls = (
            g_gain_one,
            g_shift_one,
            mixer_bias_term,
            out_bias_term,
            g_gain_two,
            g_shift_two,
            up_bias_term,
            down_bias_term,
        )
        matrix_sums = (
            matrices if matrix_sums is None else jax.tree.map(jnp.add, matrix_sums, matrices)
        )
        small_sums = smalls if small_sums is None else jax.tree.map(jnp.add, small_sums, smalls)
        results.append(outputs.astype(jnp.bfloat16))
        input_grads.append(grad_inputs)
    g_mixer_sum, g_output_sum, g_up_sum, g_down_sum = matrix_sums
    reduced = (
        lax.psum_scatter(
            g_mixer_sum.astype(jnp.bfloat16), "dp", scatter_dimension=0, tiled=True
        ).astype(jnp.float32),
        lax.psum_scatter(
            g_output_sum.astype(jnp.bfloat16), "dp", scatter_dimension=1, tiled=True
        ).astype(jnp.float32),
        lax.psum_scatter(
            g_up_sum.astype(jnp.bfloat16), "dp", scatter_dimension=0, tiled=True
        ).astype(jnp.float32),
        lax.psum_scatter(
            g_down_sum.astype(jnp.bfloat16), "dp", scatter_dimension=1, tiled=True
        ).astype(jnp.float32),
    )
    totals = lax.psum(
        (
            small_sums[0],
            small_sums[1],
            small_sums[2],
            small_sums[3],
            small_sums[4],
            small_sums[5],
            small_sums[6],
            small_sums[7],
            errors,
        ),
        ("dp", "fsdp"),
    )
    pieces = [own_slice(totals[index], data_index, data_ways) for index in range(8)]
    query_key_piece = own_slice(totals[2][: 2 * D], data_index, data_ways)
    value_piece = own_slice(totals[2][2 * D :], data_index, data_ways)
    loss = totals[8] / (token_tally * D)
    return (
        jnp.concatenate(results, axis=0),
        loss,
        jnp.concatenate(input_grads, axis=0),
        pieces[0],
        pieces[1],
        reduced[0],
        query_key_piece,
        value_piece,
        reduced[1],
        pieces[3],
        pieces[4],
        pieces[5],
        reduced[2],
        pieces[6],
        reduced[3],
        pieces[7],
    )


BF = jnp.bfloat16
F32 = jnp.float32
HEADS_LOCAL = 4
W = 320
F = 1280
R = 384
G = 1536
BLK = 160
MESH_ID = pl.DeviceIdType.MESH


def _nn(a, b):
    return lax.dot_general(a, b, (((1,), (0,)), ((), ())), preferred_element_type=F32)


def _nt(a, b):
    return lax.dot_general(a, b, (((1,), (1,)), ((), ())), preferred_element_type=F32)


def _tn(a, b):
    return lax.dot_general(a, b, (((0,), (0,)), ((), ())), preferred_element_type=F32)


def _rows(start, size, step):
    return pl.ds(pl.multiple_of(start, step), size)


class Place:
    def __init__(self):
        dp = lax.axis_index("dp")
        fs = lax.axis_index("fsdp")
        z, x = lax.div(dp, 2), lax.rem(dp, 2)
        y, c = lax.div(fs, 2), lax.rem(fs, 2)
        self.z, self.x, self.fs = z, x, fs
        self.core = (dp, 2 * y + 1 - c)
        self.ynb = (dp, 2 * (1 - y) + c)
        self.xnb = (2 * z + 1 - x, fs)
        self.zs = (z, z + 1 - 2 * lax.rem(z, 2), lax.rem(z + 2, 4), 3 - z)
        self.zn = tuple((2 * zk + x, fs) for zk in self.zs)

    def barrier(self):
        sem = pltpu.get_barrier_semaphore()
        for peer in (self.core, self.ynb, self.xnb) + self.zn[1:]:
            pl.semaphore_signal(sem, inc=1, device_id=peer, device_id_type=MESH_ID)
        pl.semaphore_wait(sem, 6)


def _send(src, dst, ss, rs, peer):
    return pltpu.make_async_remote_copy(
        src_ref=src, dst_ref=dst, send_sem=ss, recv_sem=rs, device_id=peer, device_id_type=MESH_ID
    )


class Gather:
    def __init__(self, place, buf, ss, rs):
        self.to_core = _send(
            buf.at[pl.ds(0, R), :], buf.at[pl.ds(R, R), :], ss.at[0], rs.at[0], place.core
        )
        self.to_y = [
            _send(
                buf.at[pl.ds(128 * i, 128), :],
                buf.at[pl.ds(2 * R + 128 * i, 128), :],
                ss.at[1 + i],
                rs.at[1 + i],
                place.ynb,
            )
            for i in range(3)
        ]
        self.on = [
            _send(
                buf.at[pl.ds(2 * R + 128 * i, 128), :],
                buf.at[pl.ds(3 * R + 128 * i, 128), :],
                ss.at[4 + i],
                rs.at[4 + i],
                place.core,
            )
            for i in range(3)
        ]

    def start_y(self, i):
        self.to_y[i].start()

    def start_core(self):
        self.to_core.start()

    def start(self):
        for copy in self.to_y:
            copy.start()
        self.to_core.start()

    def wait_core(self):
        self.to_core.wait_recv()

    def pass_on(self):
        for here, on in zip(self.to_y, self.on):
            here.wait_recv()
            on.start()

    def wait_diagonal(self):
        for on in self.on:
            on.wait_recv()

    def end(self):
        self.to_core.wait_send()
        for copy in self.to_y + self.on:
            copy.wait_send()


class Scatter:
    def __init__(self, place, sb, rb, ss, rs):
        self.sb, self.rb = sb, rb
        peers = (place.core, place.ynb, place.core)
        self.copies = [_send(sb.at[i], rb.at[i], ss.at[i], rs.at[i], peers[i]) for i in range(3)]

    def diagonal(self, term):
        self.sb[0] = term.astype(BF)
        self.copies[0].start()

    def over_y(self, term):
        self.copies[0].wait_recv()
        self.sb[1] = (term + self.rb[0].astype(F32)).astype(BF)
        self.copies[1].start()

    def other_core(self, term):
        self.sb[2] = term.astype(BF)
        self.copies[2].start()

    def wait(self):
        self.copies[2].wait_recv()
        self.copies[1].wait_recv()

    def rest(self, rows):
        return self.rb[2, rows, :].astype(F32) + self.rb[1, rows, :].astype(F32)

    def end(self):
        for copy in self.copies:
            copy.wait_send()


def _norm(values):
    average = jnp.mean(values, axis=-1, keepdims=True)
    centered = values - average
    reciprocal = lax.rsqrt(jnp.mean(centered * centered, axis=-1, keepdims=True) + EPSILON)
    return centered * reciprocal, reciprocal


def _head_rows(lanes, offset):
    lane = lax.broadcasted_iota(jnp.int32, (1, lanes), 1) - offset
    return [
        jnp.where((lane >= HD * h) & (lane < HD * h + HD), 1.0, 0.0).astype(BF)
        for h in range(HEADS_LOCAL)
    ]


def _stack(values, heads):
    return jnp.concatenate([values * head for head in heads], axis=0)


def _allowed(auxb):
    lane = lax.broadcasted_iota(jnp.int32, (1, 128), 1)
    picks = (lane >= 96) & (lane < 104)
    left = jnp.where(picks, auxb.astype(F32), jnp.where(lane == 104, 1.0, 0.0)).astype(BF)
    score = _nt(left, auxb)
    here = lax.broadcasted_iota(jnp.int32, (128, 128), 0)
    there = lax.broadcasted_iota(jnp.int32, (128, 128), 1)
    return (score > 1.5) | (here == there)


def _softmax(scores, allowed):
    probs = []
    for h in range(HEADS_LOCAL):
        part = jnp.where(allowed, scores[:, 128 * h : 128 * h + 128], -1e30)
        grown = jnp.exp(part - jnp.max(part, axis=-1, keepdims=True))
        probs.append(grown * (1.0 / jnp.sum(grown, axis=-1, keepdims=True)))
    return probs


def forward_kernel(
    tok_h, teach_h, aux_h, wa_h, wu_h, wd_h, vecs, mixb, tabs,
    res_h, gz_h, gy_h, mid_h, n1_h, n2_h, act_h, da_h, qk_h, v_h, o_h, aux_o, w_h, err_o,
    tok, teach, aux, w, wo, n1, n2, act, da, qk, v, o, mix, acc, mid, gy, sb, rb,
    ws, wr, ns, nr, xs, xr, ts, tr, ps, pr, ls, os_,
):
    place = Place()
    local = [
        pltpu.make_async_copy(src, dst, ls.at[i])
        for i, (src, dst) in enumerate(
            [
                (tok_h, tok),
                (aux_h, aux.at[pl.ds(0, R), :]),
                (teach_h, teach),
                (wa_h, w.at[0, _rows(BLK * (2 * place.z + place.x), BLK, 32), :]),
                (wu_h, w.at[1, _rows(BLK * (2 * place.z + place.x), BLK, 32), :]),
                (wd_h, w.at[2, _rows(BLK * (2 * place.z + place.x), BLK, 32), :]),
            ]
        )
    ]
    for copy in local:
        copy.start()
    place.barrier()

    shards = (wa_h, wu_h, wd_h)

    def at(chunk, zk, xk):
        return w.at[chunk, _rows(BLK * (2 * zk + xk), BLK, 32), :]

    def block(chunk, zk, xk):
        return wr.at[chunk, 2 * zk + xk]

    def first(chunk, k):
        z, x = place.z, place.x
        peer = place.xnb if k == 0 else place.zn[k]
        return _send(shards[chunk], at(chunk, z, x), ws.at[chunk, k], block(chunk, z, x), peer)

    def second(chunk, k):
        zk, x = place.zs[k], place.x
        return _send(
            at(chunk, zk, x), at(chunk, zk, x), ws.at[chunk, 3 + k], block(chunk, zk, x), place.xnb
        )

    def begin(chunk):
        for k in range(4):
            first(chunk, k).start()

    def onward(chunk, k):
        second(chunk, k).wait_recv()
        second(chunk, k).start()

    def complete(chunk):
        for zk in range(4):
            _send(
                at(chunk, zk, 1 - place.x),
                at(chunk, zk, 1 - place.x),
                ws.at[chunk, 0],
                block(chunk, zk, 1 - place.x),
                place.xnb,
            ).wait_recv()
        local[3 + chunk].wait()

    outs = []

    def out(src, dst):
        copy = pltpu.make_async_copy(src, dst, os_.at[len(outs)])
        copy.start()
        outs.append(copy)

    begin(0)
    local[0].wait()
    ag1 = Gather(place, n1, ns, nr)
    agx = Gather(place, aux, xs, xr)
    local[1].wait()
    agx.start()

    def first_norm(i, _):
        rows = _rows(32 * i, 32, 32)
        normed, _r = _norm(tok[rows, :].astype(F32))
        n1[rows, :] = (normed * vecs[0:1, :] + vecs[1:2, :]).astype(BF)
        return 0

    lax.fori_loop(0, R // 32, first_norm, 0)
    ag1.start()
    agx.pass_on()
    onward(0, 1)
    ag1.pass_on()
    onward(0, 3)
    onward(0, 2)
    begin(1)
    ag1.wait_core()
    ag1.wait_diagonal()
    agx.wait_core()
    agx.wait_diagonal()
    complete(0)
    wo[...] = w[0, :, 3 * W :]
    out(n1, n1_h)
    out(aux, aux_o)
    out(w.at[0], w_h.at[0])

    left = _head_rows(2 * W, 0)
    side = _head_rows(W, 0)
    rs1 = Scatter(place, sb, rb, ts, tr)

    def member(t, _):
        r = 3 - t
        mix[...] = (
            _nn(n1[_rows(R * r, R, 128), :], w[0, :, : 3 * W]) + mixb[...]
        )

        def attend_rows(i, _):
            mine = _rows(128 * i, 128, 128)
            rows = _rows(R * r + 128 * i, 128, 128)
            auxb = aux[rows, :]
            angle = _nn(auxb, tabs[...])
            raw = mix[mine, : 2 * W]
            turned = (
                raw * angle[:, : 2 * W]
                + pltpu.roll(raw, 2 * W - 40, 1) * angle[:, 2 * W : 4 * W]
                + pltpu.roll(raw, 40, 1) * angle[:, 4 * W :]
            )
            qkb = turned.astype(BF)
            kqb = pltpu.roll(turned, W, 1).astype(BF)
            vb = mix[mine, 2 * W :].astype(BF)
            qk[rows, :] = qkb
            v[rows, :] = vb
            scores = _nt(qkb, _stack(kqb, left)) * HD ** (-0.5)
            probs = _softmax(scores, _allowed(auxb))
            flat = jnp.concatenate([p.astype(BF) for p in probs], axis=1)
            o[rows, :] = _nn(flat, _stack(vb, side)).astype(BF)
            return 0

        lax.fori_loop(0, 3, attend_rows, 0)
        acc[...] = _nt(o[_rows(R * r, R, 128), :], wo[...])

        @pl.when(t == 0)
        def _():
            rs1.diagonal(acc[...])
            onward(1, 1)

        @pl.when(t == 1)
        def _():
            rs1.over_y(acc[...])
            onward(1, 3)

        @pl.when(t == 2)
        def _():
            rs1.other_core(acc[...])
            onward(1, 2)

        return 0

    lax.fori_loop(0, 4, member, 0)
    begin(2)
    out(qk, qk_h)
    out(v, v_h)
    out(o, o_h)
    rs1.wait()

    ns2 = Gather(place, n2, ns, nr)
    ag1.end()

    def second_norm(i, _):
        rows = _rows(32 * i, 32, 32)
        middle = tok[rows, :].astype(F32) + (acc[rows, :] + rs1.rest(rows)) + vecs[2:3, :]
        mid[rows, :] = middle
        normed, _r = _norm(middle)
        n2[rows, :] = (normed * vecs[3:4, :] + vecs[4:5, :]).astype(BF)
        return 0

    lax.fori_loop(0, R // 32, second_norm, 0)
    ns2.start()
    out(mid, mid_h)
    complete(1)
    out(w.at[1], w_h.at[1])

    def upward(r):
        rows = _rows(R * r, R, 128)
        acc[...] = _nn(n2[rows, :], w[1]) + vecs[6:7, :]

        def active_rows(i, _):
            sub = _rows(32 * i, 32, 32)
            rows = _rows(R * r + 32 * i, 32, 32)
            upper = acc[sub, :]
            gate = 1.0 / (1.0 + jnp.exp(-1.702 * upper))
            act[rows, :] = (upper * gate).astype(BF)
            da[rows, :] = (gate + 1.702 * upper * gate * (1.0 - gate)).astype(BF)
            return 0

        lax.fori_loop(0, R // 32, active_rows, 0)

    def up_members(r, _):
        @pl.when(r == 1)
        def _():
            ns2.wait_core()

        @pl.when(r == 2)
        def _():
            onward(2, 1)
            ns2.pass_on()

        @pl.when(r == 3)
        def _():
            onward(2, 3)
            ns2.wait_diagonal()

        upward(r)
        return 0

    lax.fori_loop(0, 4, up_members, 0)
    out(n2, n2_h)
    out(act, act_h)
    out(da, da_h)
    onward(2, 2)
    complete(2)
    out(w.at[2], w_h.at[2])
    rs1.end()
    rs2 = Scatter(place, sb, rb, ps, pr)

    def down_members(t, _):
        acc[...] = _nt(act[_rows(R * (3 - t), R, 128), :], w[2])

        @pl.when(t == 0)
        def _():
            rs2.diagonal(acc[...])

        @pl.when(t == 1)
        def _():
            rs2.over_y(acc[...])

        @pl.when(t == 2)
        def _():
            rs2.other_core(acc[...])

        return 0

    lax.fori_loop(0, 4, down_members, 0)
    local[2].wait()
    rs2.wait()
    agx.end()

    def finish(i, total):
        rows = _rows(32 * i, 32, 32)
        result = mid[rows, :] + (acc[rows, :] + rs2.rest(rows)) + vecs[5:6, :]
        real = aux[rows, 104:105].astype(F32)
        difference = result - teach[rows, :].astype(F32)
        masked = real * difference
        gout = vecs[7:8, :] * masked
        gy[rows, :] = gout
        tok[rows, :] = result.astype(BF)
        teach[rows, :] = gout.astype(BF)
        return total + jnp.sum(masked * difference, axis=0, keepdims=True)

    total = lax.fori_loop(0, R // 32, finish, jnp.zeros((1, D), F32))
    err_o[...] = jnp.broadcast_to(total, (8, D))
    out(tok, res_h)
    out(teach, gz_h)
    out(gy, gy_h)
    ns2.end()
    rs2.end()
    for chunk in range(3):
        for k in range(4):
            first(chunk, k).wait_send()
        for k in range(1, 4):
            second(chunk, k).wait_send()
    for copy in outs:
        copy.wait()


def _call(kernel, name, outs, ins, scratch, collective, limit):
    return pl.pallas_call(
        kernel,
        out_shape=[jax.ShapeDtypeStruct(shape, dtype) for shape, dtype, _ in outs],
        in_specs=[pl.BlockSpec(memory_space=space) for space in ins],
        out_specs=[pl.BlockSpec(memory_space=space) for _, _, space in outs],
        scratch_shapes=scratch,
        compiler_params=pltpu.CompilerParams(
            collective_id=collective, has_side_effects=True, vmem_limit_bytes=limit
        ),
        name=name,
    )


def forward_call(*operands):
    any_, vm = pl.ANY, pltpu.VMEM
    outs = [
        ((R, D), BF, any_),
        ((R, D), BF, any_),
        ((R, D), F32, any_),
        ((R, D), F32, any_),
        ((G, D), BF, any_),
        ((G, D), BF, any_),
        ((G, F), BF, any_),
        ((G, F), BF, any_),
        ((G, 2 * W), BF, any_),
        ((G, W), BF, any_),
        ((G, W), BF, any_),
        ((G, 128), BF, any_),
        ((3, D, D), BF, any_),
        ((8, D), F32, vm),
    ]
    dma = pltpu.SemaphoreType.DMA
    scratch = [
        vm((R, D), BF),
        vm((R, D), BF),
        vm((G, 128), BF),
        vm((3, D, D), BF),
        vm((D, W), BF),
        vm((G, D), BF),
        vm((G, D), BF),
        vm((G, F), BF),
        vm((G, F), BF),
        vm((G, 2 * W), BF),
        vm((G, W), BF),
        vm((G, W), BF),
        vm((R, 3 * W), F32),
        vm((R, D), F32),
        vm((R, D), F32),
        vm((R, D), F32),
        vm((3, R, D), BF),
        vm((3, R, D), BF),
        dma((3, 7)),
        dma((3, 8)),
        dma((7,)),
        dma((7,)),
        dma((7,)),
        dma((7,)),
        dma((3,)),
        dma((3,)),
        dma((3,)),
        dma((3,)),
        dma((6,)),
        dma((16,)),
    ]
    ins = [any_] * 6 + [vm] * 3
    return _call(forward_kernel, "forward", outs, ins, scratch, 1, 60 << 20)(*operands)


def backward_kernel(
    tok_h, gz_h, gy_h, mid_h, n1_h, n2_h, act_h, da_h, qk_h, v_h, o_h, aux_h, w_h, vecs, tabs, err,
    gtok_h, gw_h, small_o,
    tok, gy, mid, b1, b2, b3, b4, qk, v, o, go, aux, wd, wu, wo, gb, xin, zin, fin, acc, sb, rb,
    small, stage, came,
    ns, nr, ms, mr, ts, tr, ps, pr, xs, xr, zs, zr, ss, sr, ls, os_,
):
    place = Place()
    loads = [
        pltpu.make_async_copy(src, dst, ls.at[i])
        for i, (src, dst) in enumerate(
            [
                (gz_h, b1.at[pl.ds(0, R), :]),
                (w_h.at[2], wd),
                (da_h, b3),
                (act_h, b2),
                (w_h.at[1], wu),
                (n2_h, b4),
                (gy_h, gy),
                (mid_h, mid),
                (o_h, o),
                (qk_h, qk),
                (v_h, v),
                (aux_h, aux),
                (tok_h, tok),
            ]
        )
    ]
    for copy in loads:
        copy.start()
    place.barrier()
    loads[0].wait()
    gather = Gather(place, b1, ns, nr)
    gather.start()
    small[...] = jnp.zeros_like(small)
    small[6:7, :] = err[0:1, :]
    small[5:6, :] = jnp.sum(b1[pl.ds(0, R), :].astype(F32), axis=0, keepdims=True)
    loads[1].wait()
    loads[2].wait()

    def column_rows(i, total, r):
        sub = _rows(32 * i, 32, 32)
        rows = _rows(R * r + 32 * i, 32, 32)
        low = (acc[sub, :] * b3[rows, :].astype(F32)).astype(BF)
        b3[rows, :] = low
        return total + jnp.sum(low.astype(F32), axis=0, keepdims=True)

    def upper_grad(r, total):
        @pl.when(r == 1)
        def _():
            gather.wait_core()

        @pl.when(r == 2)
        def _():
            gather.pass_on()

        @pl.when(r == 3)
        def _():
            gather.wait_diagonal()

        acc[...] = _nn(b1[_rows(R * r, R, 128), :], wd[...])
        return lax.fori_loop(0, R // 32, lambda i, t: column_rows(i, t, r), total)

    up_total = lax.fori_loop(0, 4, upper_grad, jnp.zeros((1, F), F32))
    small[pl.ds(8 + place.fs, 1), :] = up_total

    far = 1 - lax.div(place.z, 2)
    near = lax.div(place.z, 2)

    def to_x(chunk, slot, k):
        rows = _rows(BLK * (2 * place.zs[k] + 1 - place.x), BLK, 32)
        return _send(gb.at[slot, rows, :], xin.at[chunk, k], xs.at[chunk, k], xr.at[chunk, k], place.xnb)

    def to_z(chunk, slot, k):
        rows = _rows(BLK * (2 * place.zs[k] + place.x), BLK, 32)
        return _send(
            gb.at[slot, rows, :], zin.at[chunk, k - 1], zs.at[chunk, k - 1], zr.at[chunk, k - 1], place.zn[k]
        )

    def tile(chunk, slot, lhs, rhs, half):
        rows = _rows(640 * half, 640, 128)
        gb[slot, rows, :] = _tn(lhs[:, rows], rhs[...]).astype(BF)

    def add_x(chunk, slot, k):
        to_x(chunk, slot, k).wait_recv()
        rows = _rows(BLK * (2 * place.zs[k] + place.x), BLK, 32)
        total = gb[slot, rows, :].astype(F32) + xin[chunk, k].astype(F32)
        if k == 0:
            fin[chunk] = total
        else:
            gb[slot, rows, :] = total.astype(BF)
            to_z(chunk, slot, k).start()

    outs = []

    def out(src, dst):
        copy = pltpu.make_async_copy(src, dst, os_.at[len(outs)])
        copy.start()
        outs.append(copy)

    def add_z(chunk, slot):
        for k in range(1, 4):
            to_z(chunk, slot, k).wait_recv()
        fin[chunk] = fin[chunk] + (
            zin[chunk, 0].astype(F32) + zin[chunk, 1].astype(F32) + zin[chunk, 2].astype(F32)
        )
        out(fin.at[chunk], gw_h.at[chunk])

    loads[3].wait()
    tile(2, 0, b1, b2, far)
    to_x(2, 0, 2).start()
    to_x(2, 0, 3).start()
    tile(2, 0, b1, b2, near)
    to_x(2, 0, 1).start()
    to_x(2, 0, 0).start()

    n1_load = pltpu.make_async_copy(n1_h, b2, ls.at[13])
    n1_load.start()
    wa_load = pltpu.make_async_copy(w_h.at[0], wd, ls.at[14])
    wa_load.start()

    loads[4].wait()
    gather.end()
    rs1 = Scatter(place, sb, rb, ts, tr)

    def lower_two(t, _):
        acc[...] = _nt(b3[_rows(R * (3 - t), R, 128), :], wu[...])

        @pl.when(t == 0)
        def _():
            rs1.diagonal(acc[...])

        @pl.when(t == 1)
        def _():
            rs1.over_y(acc[...])

        @pl.when(t == 2)
        def _():
            rs1.other_core(acc[...])

        return 0

    lax.fori_loop(0, 4, lower_two, 0)
    loads[5].wait()
    add_x(2, 0, 2)
    tile(1, 1, b4, b3, far)
    to_x(1, 1, 2).start()
    to_x(1, 1, 3).start()
    add_x(2, 0, 3)
    tile(1, 1, b4, b3, near)
    to_x(1, 1, 1).start()
    to_x(1, 1, 0).start()
    loads[6].wait()
    loads[7].wait()
    rs1.wait()
    gather2 = Gather(place, b1, ms, mr)

    def norm_rows(i, sums, values, gain, keep):
        rows = _rows(32 * i, 32, 32)
        grad = acc[rows, :] + keep.rest(rows)
        normed, reciprocal = _norm(values[rows, :].astype(F32))
        scaled = grad * gain
        back = (
            scaled
            - jnp.mean(scaled, axis=-1, keepdims=True)
            - normed * jnp.mean(scaled * normed, axis=-1, keepdims=True)
        ) * reciprocal
        total = gy[rows, :] + back
        gy[rows, :] = total
        return (
            rows,
            total,
            (
                sums[0] + jnp.sum(grad * normed, axis=0, keepdims=True),
                sums[1] + jnp.sum(grad, axis=0, keepdims=True),
            ),
        )

    zero = jnp.zeros((1, D), F32)

    def second_back(i, sums):
        rows, total, pair = norm_rows(i, sums[:2], mid, vecs[3:4, :], rs1)
        low = total.astype(BF)
        b1[rows, :] = low
        return pair + (sums[2] + jnp.sum(low.astype(F32), axis=0, keepdims=True),)

    gain2, shift2, outb = lax.fori_loop(0, R // 32, second_back, (zero, zero, zero))
    gather2.start()
    small[2:3, :] = outb
    small[3:4, :] = gain2
    small[4:5, :] = shift2
    add_x(2, 0, 1)
    add_x(2, 0, 0)
    for i in range(8, 12):
        loads[i].wait()
    wa_load.wait()
    wo[...] = wd[:, 3 * W :]

    left = _head_rows(2 * W, 0)
    right = _head_rows(2 * W, W)
    side = _head_rows(W, 0)

    def attend_grad(r, total):
        @pl.when(r == 1)
        def _():
            gather2.wait_core()

        @pl.when(r == 2)
        def _():
            gather2.pass_on()

        @pl.when(r == 3)
        def _():
            gather2.wait_diagonal()

        go[...] = _nn(b1[_rows(R * r, R, 128), :], wo[...]).astype(BF)

        def attend_rows(i, total):
            mine = _rows(128 * i, 128, 128)
            rows = _rows(R * r + 128 * i, 128, 128)
            auxb = aux[rows, :]
            angle = _nn(auxb, tabs[...])
            qkb = qk[rows, :]
            kqb = pltpu.roll(qkb.astype(F32), W, 1).astype(BF)
            vb = v[rows, :]
            gob = go[mine, :]
            keys = _stack(kqb, left)
            queries = _stack(kqb, right)
            scores = _nt(qkb, keys) * HD ** (-0.5)
            probs = _softmax(scores, _allowed(auxb))
            gprobs = _nt(gob, _stack(vb, side))
            gscores = []
            for h in range(HEADS_LOCAL):
                gp = gprobs[:, 128 * h : 128 * h + 128]
                delta = jnp.sum(gp * probs[h], axis=-1, keepdims=True)
                gscores.append((probs[h] * (gp - delta)).astype(BF))
            flat = jnp.concatenate(gscores, axis=1)
            tall = jnp.concatenate(gscores, axis=0)
            ptall = jnp.concatenate([p.astype(BF) for p in probs], axis=0)
            gqk = (_nn(flat, keys) + _tn(tall, queries)) * HD ** (-0.5)
            gv = _tn(ptall, _stack(gob, side))
            turned = (
                gqk * angle[:, : 2 * W]
                + pltpu.roll(gqk * angle[:, 4 * W :], 2 * W - 40, 1)
                + pltpu.roll(gqk * angle[:, 2 * W : 4 * W], 40, 1)
            )
            low = jnp.concatenate([turned, gv], axis=1).astype(BF)
            b3[rows, : 3 * W] = low
            return total + jnp.sum(low.astype(F32), axis=0, keepdims=True)

        return lax.fori_loop(0, 3, attend_rows, total)

    mix_total = lax.fori_loop(0, 4, attend_grad, jnp.zeros((1, 3 * W), F32))
    small[pl.ds(12 + place.fs, 1), : 3 * W] = mix_total

    for k in range(4):
        to_x(2, 0, k).wait_send()
    for k in range(1, 4):
        to_z(2, 0, k).wait_send()
    n1_load.wait()

    def last_tile(half):
        rows = _rows(640 * half, 640, 128)
        gb[0, rows, : 3 * W] = _tn(b2[:, rows], b3[:, : 3 * W]).astype(BF)
        gb[0, rows, 3 * W :] = _tn(b1[:, rows], o[...]).astype(BF)

    last_tile(far)
    to_x(0, 0, 2).start()
    to_x(0, 0, 3).start()
    last_tile(near)
    to_x(0, 0, 1).start()
    to_x(0, 0, 0).start()
    rs1.end()
    rs2 = Scatter(place, sb, rb, ps, pr)

    def lower_one(t, _):
        acc[...] = _nt(b3[_rows(R * (3 - t), R, 128), : 3 * W], wd[:, : 3 * W])

        @pl.when(t == 0)
        def _():
            rs2.diagonal(acc[...])

        @pl.when(t == 1)
        def _():
            rs2.over_y(acc[...])

        @pl.when(t == 2)
        def _():
            rs2.other_core(acc[...])

        return 0

    lax.fori_loop(0, 4, lower_one, 0)
    add_x(1, 1, 2)
    add_x(1, 1, 3)
    add_x(1, 1, 1)
    add_x(1, 1, 0)
    add_z(2, 0)
    loads[12].wait()
    rs2.wait()

    def first_back(i, sums):
        return norm_rows(i, sums, tok, vecs[0:1, :], rs2)[2]

    gain1, shift1 = lax.fori_loop(0, R // 32, first_back, (zero, zero))
    out(gy, gtok_h)
    small[0:1, :] = gain1
    small[1:2, :] = shift1

    hops = [
        _send(stage.at[i], came.at[i], ss.at[i], sr.at[i], peer)
        for i, peer in enumerate((place.core, place.ynb, place.xnb, place.zn[1], place.zn[2]))
    ]
    stage[0] = small[...]
    for i in range(5):
        hops[i].start()
        hops[i].wait_recv()
        total = stage[i] + came[i]
        if i < 4:
            stage[i + 1] = total
        else:
            small_o[...] = total

    add_z(1, 1)
    for k in (2, 3, 1, 0):
        add_x(0, 0, k)
    add_z(0, 0)

    gather2.end()
    rs2.end()
    for hop in hops:
        hop.wait_send()
    for chunk, slot in ((1, 1), (0, 0)):
        for k in range(4):
            to_x(chunk, slot, k).wait_send()
        for k in range(1, 4):
            to_z(chunk, slot, k).wait_send()
    for copy in outs:
        copy.wait()


def backward_call(*operands):
    any_, vm = pl.ANY, pltpu.VMEM
    outs = [((R, D), F32, any_), ((3, BLK, D), F32, any_), ((16, D), F32, vm)]
    dma = pltpu.SemaphoreType.DMA
    scratch = [
        vm((R, D), BF),
        vm((R, D), F32),
        vm((R, D), F32),
        vm((G, D), BF),
        vm((G, D), BF),
        vm((G, D), BF),
        vm((G, D), BF),
        vm((G, 2 * W), BF),
        vm((G, W), BF),
        vm((G, W), BF),
        vm((R, W), BF),
        vm((G, 128), BF),
        vm((D, D), BF),
        vm((D, D), BF),
        vm((D, W), BF),
        vm((2, D, D), BF),
        vm((3, 4, BLK, D), BF),
        vm((3, 3, BLK, D), BF),
        vm((3, BLK, D), F32),
        vm((R, D), F32),
        vm((3, R, D), BF),
        vm((3, R, D), BF),
        vm((16, D), F32),
        vm((5, 16, D), F32),
        vm((5, 16, D), F32),
        dma((7,)),
        dma((7,)),
        dma((7,)),
        dma((7,)),
        dma((3,)),
        dma((3,)),
        dma((3,)),
        dma((3,)),
        dma((3, 4)),
        dma((3, 4)),
        dma((3, 3)),
        dma((3, 3)),
        dma((5,)),
        dma((5,)),
        dma((15,)),
        dma((8,)),
    ]
    ins = [any_] * 13 + [vm] * 3
    return _call(backward_kernel, "backward", outs, ins, scratch, 2, 64 << 20)(*operands)


def turn_tables():
    import ml_dtypes

    quarter = HD // 4
    frequency = (1.0 / np.float32(10000.0) ** (np.arange(quarter, dtype=np.float32) * 4.0 / HD)).astype(np.float32)
    angle = (np.arange(16, dtype=np.float32)[:, None] * frequency[None, :]).astype(np.float32)
    cosine, sine = np.cos(angle.astype(np.float64)), np.sin(angle.astype(np.float64))
    zero = np.zeros_like(cosine)

    def head(first, second):
        top = np.concatenate([first, zero, second, zero], axis=1)
        low = np.concatenate([zero, first, zero, second], axis=1)
        return np.tile(np.concatenate([top, low], axis=0), (1, 2 * HEADS_LOCAL))

    full = np.concatenate([head(cosine, cosine), head(-sine, zero), head(zero, sine)], axis=1).astype(np.float32)
    terms = []
    rest = full
    for _ in range(3):
        term = rest.astype(ml_dtypes.bfloat16)
        terms.append(term)
        rest = rest - term.astype(np.float32)
    terms.append(np.zeros((32, full.shape[1]), ml_dtypes.bfloat16))
    return jnp.asarray(np.concatenate(terms, axis=0))


def row_marks(picture, places, validity):
    spots = jnp.arange(16, dtype=jnp.int32)
    row_spot = places[:, 0:1] == spots
    col_spot = places[:, 1:2] == spots
    pictures = picture.reshape(-1, ROW_PATCHES)
    change = (pictures[:, 1:] != pictures[:, :-1]).astype(BF)
    change = jnp.pad(change, ((0, 0), (1, 0)))
    upto = jnp.triu(jnp.ones((ROW_PATCHES, ROW_PATCHES), BF))
    rank = jnp.dot(change, upto, preferred_element_type=F32).reshape(-1, 1)
    ranks = rank == jnp.arange(8, dtype=F32)
    once = jnp.concatenate([row_spot, col_spot], axis=1)
    return jnp.concatenate(
        [once, once, once, ranks, (validity > 0)[:, None], jnp.zeros((picture.shape[0], 23), bool)], axis=1
    ).astype(BF)


def on_device_fast(
    tokens,
    teacher,
    picture,
    places,
    validity,
    first_gain,
    first_shift,
    mixer_weight,
    mixer_bias,
    output_weight,
    output_bias,
    second_gain,
    second_shift,
    upward_weight,
    upward_bias,
    downward_weight,
    downward_bias,
):
    member = lax.axis_index("fsdp")
    data_index = lax.axis_index("dp")
    data_ways = lax.axis_size("dp")
    marks = row_marks(picture, places, validity)
    counts = jnp.sum((validity > 0).astype(F32).reshape(3, ROW_PATCHES), axis=1)
    vectors = (first_gain, first_shift, output_bias, second_gain, second_shift, downward_bias, upward_bias, mixer_bias)
    packed = jnp.concatenate(list(vectors) + [jnp.pad(counts.astype(BF), (0, 93))])[None]
    everyone = lax.all_gather(packed, ("dp", "fsdp"), axis=0, tiled=True)
    everyone = everyone.reshape(data_ways, lax.axis_size("fsdp"), -1)
    tally = jnp.sum(everyone[:, :, 2080:2083].astype(F32))
    factor = 2.0 * ((tokens.shape[0] * data_ways * lax.axis_size("fsdp")) / tally)
    whole = everyone[:, 0].astype(F32)
    rows = [whole[:, BLK * i : BLK * (i + 1)].reshape(1, D) for i in range(6)]
    up_all = whole[:, 960:1600].reshape(4, F)
    mix_all = whole[:, 1600:2080].reshape(3, 4, W)
    up_piece = lax.dynamic_slice_in_dim(up_all, member, 1, 0)
    mix_piece = lax.dynamic_slice_in_dim(mix_all, member, 1, 1).reshape(1, 3 * W)
    vecs = jnp.concatenate(rows + [up_piece, jnp.full((1, D), factor, F32)], axis=0)
    wa = jnp.concatenate([mixer_weight.reshape(BLK, 3 * W), output_weight.T], axis=1)
    tabs = turn_tables()
    (res, gz, gy, mid, n1, n2, act, da, qk, v, o, aux, w, err) = forward_call(
        tokens, teacher, marks, wa, upward_weight, downward_weight.T, vecs, mix_piece, tabs
    )
    gtok, gw, small = backward_call(
        tokens, gz, gy, mid, n1, n2, act, da, qk, v, o, aux, w, vecs, tabs, err
    )
    pieces = [own_slice(small[i], data_index, data_ways) for i in range(6)]
    loss = jnp.sum(small[6]) / (tally * D)
    up_bias = own_slice(small[8:12].reshape(FF), data_index, data_ways)
    mixed = small[12:16, : 3 * W].reshape(4, 3, W).transpose(1, 0, 2).reshape(3 * D)
    return (
        res,
        loss,
        gtok,
        pieces[0],
        pieces[1],
        gw[0, :, : 3 * W].reshape(BLK, 3, W),
        own_slice(mixed[: 2 * D], data_index, data_ways),
        own_slice(mixed[2 * D :], data_index, data_ways),
        gw[0, :, 3 * W :].T,
        pieces[2],
        pieces[3],
        pieces[4],
        gw[1],
        up_bias,
        gw[2].T,
        pieces[5],
    )


def solution(mesh):
    fast = mesh.shape["dp"] == 8 and mesh.shape["fsdp"] == 4
    return jax.shard_map(
        on_device_fast if fast else on_device,
        mesh=mesh,
        in_specs=(
            P(("dp", "fsdp"), None),
            P(("dp", "fsdp"), None),
            P(("dp", "fsdp")),
            P(("dp", "fsdp"), None),
            P(("dp", "fsdp")),
            P("dp"),
            P("dp"),
            P("dp", None, "fsdp"),
            P("dp"),
            P("fsdp", "dp"),
            P("dp"),
            P("dp"),
            P("dp"),
            P("dp", "fsdp"),
            P("dp"),
            P("fsdp", "dp"),
            P("dp"),
        ),
        out_specs=(
            P(("dp", "fsdp"), None),
            P(),
            P(("dp", "fsdp"), None),
            P("dp"),
            P("dp"),
            P("dp", None, "fsdp"),
            P("dp"),
            P("dp"),
            P("fsdp", "dp"),
            P("dp"),
            P("dp"),
            P("dp"),
            P("dp", "fsdp"),
            P("dp"),
            P("fsdp", "dp"),
            P("dp"),
        ),
        check_vma=False,
    )
```

```python
import numpy as np
import jax
import jax.numpy as jnp
from jax import lax
from jax.experimental import pallas as pl
from jax.experimental.pallas import tpu as pltpu
from jax.sharding import PartitionSpec as P

D = 1280
HD = 80
FF = 5120
ROW_PATCHES = 128
MB = 3


EPSILON = 1e-06


def norm_forward(values, scaler, offset):
    average = jnp.mean(values, axis=-1, keepdims=True)
    centered = values - average
    reciprocal = lax.rsqrt(jnp.mean(centered * centered, axis=-1, keepdims=True) + EPSILON)
    normed = centered * reciprocal
    return (normed * scaler.astype(jnp.float32) + offset.astype(jnp.float32), normed, reciprocal)


def norm_backward(gradient, normed, reciprocal, scaler):
    scaled = gradient * scaler.astype(jnp.float32)
    adjusted = (
        scaled
        - jnp.mean(scaled, axis=-1, keepdims=True)
        - normed * jnp.mean(scaled * normed, axis=-1, keepdims=True)
    )
    return (adjusted * reciprocal, jnp.sum(gradient * normed, axis=0), jnp.sum(gradient, axis=0))


def tables(places):
    quarter = HD // 4
    frequency = 1.0 / 10000.0 ** (jnp.arange(quarter, dtype=jnp.float32) * 4.0 / HD)
    row_angle = places[:, 0:1].astype(jnp.float32) * frequency
    col_angle = places[:, 1:2].astype(jnp.float32) * frequency
    angle_all = jnp.concatenate([row_angle, col_angle, row_angle, col_angle], axis=-1)
    return (jnp.cos(angle_all)[:, None, :], jnp.sin(angle_all)[:, None, :])


def rotate(values, cosine, sine):
    halfway = HD // 2
    flipped = jnp.concatenate([-values[..., halfway:], values[..., :halfway]], axis=-1)
    return values * cosine + flipped * sine


def unrotate(gradient, cosine, sine):
    halfway = HD // 2
    shifted = gradient * sine
    return gradient * cosine + jnp.concatenate(
        [shifted[..., halfway:], -shifted[..., :halfway]], axis=-1
    )


def allowed_mask(picture, validity):
    picture_rows = picture.reshape(-1, ROW_PATCHES)
    occupancy_flags = validity.reshape(-1, ROW_PATCHES) > 0
    shared_picture_mask = picture_rows[:, :, None] == picture_rows[:, None, :]
    self_pairs = jnp.eye(ROW_PATCHES, dtype=bool)[None]
    return (shared_picture_mask & occupancy_flags[:, None, :] | self_pairs)[:, None]


def scores_of(query, key_rows, permitted_pairs):
    products = jnp.einsum(
        "bqhd,bkhd->bhqk", query, key_rows, preferred_element_type=jnp.float32
    ) * HD ** (-0.5)
    return jnp.where(permitted_pairs, products, -1e30)


def attend(query, key_rows, value_rows, permitted_pairs):
    scores = scores_of(query, key_rows, permitted_pairs)
    maximum = jnp.max(scores, axis=-1, keepdims=True)
    log_total = maximum + jnp.log(jnp.sum(jnp.exp(scores - maximum), axis=-1, keepdims=True))
    probs = jnp.exp(scores - log_total).astype(jnp.bfloat16)
    attended = jnp.einsum("bhqk,bkhd->bqhd", probs, value_rows, preferred_element_type=jnp.float32)
    return (attended, log_total)


def attend_back(grad_attended, query, key_rows, value_rows, permitted_pairs, log_total):
    scores = scores_of(query, key_rows, permitted_pairs)
    probs = jnp.exp(scores - log_total)
    grad_probs = jnp.einsum(
        "bqhd,bkhd->bhqk", grad_attended, value_rows, preferred_element_type=jnp.float32
    )
    delta = jnp.sum(grad_probs * probs, axis=-1, keepdims=True)
    grad_scores = (probs * (grad_probs - delta)).astype(jnp.bfloat16)
    scaling = HD ** (-0.5)
    grad_query = (
        jnp.einsum("bhqk,bkhd->bqhd", grad_scores, key_rows, preferred_element_type=jnp.float32)
        * scaling
    )
    grad_key = (
        jnp.einsum("bhqk,bqhd->bkhd", grad_scores, query, preferred_element_type=jnp.float32)
        * scaling
    )
    grad_value = jnp.einsum(
        "bhqk,bqhd->bkhd",
        probs.astype(jnp.bfloat16),
        grad_attended,
        preferred_element_type=jnp.float32,
    )
    return (grad_query, grad_key, grad_value)


def quick_gelu_grad(grad_active, upper):
    sigmoid_up = jax.nn.sigmoid(1.702 * upper)
    return (grad_active * (sigmoid_up + 1.702 * upper * sigmoid_up * (1.0 - sigmoid_up))).astype(
        jnp.bfloat16
    )


def own_slice(vector, data_index, data_ways):
    length = vector.shape[0] // data_ways
    return lax.dynamic_slice_in_dim(vector, data_index * length, length, 0)


def on_device(
    tokens,
    teacher,
    picture,
    places,
    validity,
    first_gain,
    first_shift,
    mixer_weight,
    mixer_bias,
    output_weight,
    output_bias,
    second_gain,
    second_shift,
    upward_weight,
    upward_bias,
    downward_weight,
    downward_bias,
):
    data_ways = lax.axis_size("dp")
    split_ways = lax.axis_size("fsdp")
    member = lax.axis_index("fsdp")
    data_index = lax.axis_index("dp")
    occupancy_flags = validity.astype(jnp.float32)
    token_tally = lax.psum(jnp.sum(occupancy_flags), ("dp", "fsdp"))
    factor = tokens.shape[0] * data_ways * split_ways / token_tally
    (
        mixer_local,
        output_local,
        upward_local,
        downward_local,
        gain_one,
        shift_one,
        mixer_shift,
        output_shift,
        gain_two,
        shift_two,
        upward_shift,
        downward_shift,
    ) = (
        lax.all_gather(mixer_weight, "dp", axis=0, tiled=True),
        lax.all_gather(output_weight, "dp", axis=1, tiled=True),
        lax.all_gather(upward_weight, "dp", axis=0, tiled=True),
        lax.all_gather(downward_weight, "dp", axis=1, tiled=True),
        lax.all_gather(first_gain, "dp", axis=0, tiled=True),
        lax.all_gather(first_shift, "dp", axis=0, tiled=True),
        lax.all_gather(mixer_bias, "dp", axis=0, tiled=True),
        lax.all_gather(output_bias, "dp", axis=0, tiled=True),
        lax.all_gather(second_gain, "dp", axis=0, tiled=True),
        lax.all_gather(second_shift, "dp", axis=0, tiled=True),
        lax.all_gather(upward_bias, "dp", axis=0, tiled=True),
        lax.all_gather(downward_bias, "dp", axis=0, tiled=True),
    )
    width_local = output_local.shape[0]
    heads_local = width_local // HD
    hidden_local = upward_local.shape[1]
    mixer_flat = mixer_local.reshape(D, 3 * width_local)
    mixer_piece = lax.dynamic_slice_in_dim(
        mixer_shift.reshape(3, D), member * width_local, width_local, 1
    )
    mixer_piece = mixer_piece.reshape(3 * width_local).astype(jnp.float32)
    upward_piece = lax.dynamic_slice_in_dim(
        upward_shift, member * hidden_local, hidden_local, 0
    ).astype(jnp.float32)
    packed_rows = tokens.shape[0] // MB
    errors = jnp.zeros((), jnp.float32)
    matrix_sums = None
    small_sums = None
    results = []
    input_grads = []
    for micro in range(MB):
        start_offset = micro * packed_rows
        inputs = tokens[start_offset : start_offset + packed_rows].astype(jnp.float32)
        target = teacher[start_offset : start_offset + packed_rows].astype(jnp.float32)
        occupied_rows = occupancy_flags[start_offset : start_offset + packed_rows]
        picture_rows = picture[start_offset : start_offset + packed_rows]
        local_picture = (picture_rows - picture_rows[0]).astype(jnp.bfloat16)
        place_rows = places[start_offset : start_offset + packed_rows].astype(jnp.bfloat16)
        live_marks = validity[start_offset : start_offset + packed_rows].astype(jnp.bfloat16)
        shifted_one, normed_one, recip_one = norm_forward(inputs, gain_one, shift_one)
        lowered_one = shifted_one.astype(jnp.bfloat16)
        group_one, group_picture, group_places, group_live = (
            lax.all_gather(lowered_one, "fsdp", axis=0, tiled=True),
            lax.all_gather(local_picture, "fsdp", axis=0, tiled=True),
            lax.all_gather(place_rows, "fsdp", axis=0, tiled=True),
            lax.all_gather(live_marks, "fsdp", axis=0, tiled=True),
        )
        group_rows = group_one.shape[0]
        mixed = jnp.dot(group_one, mixer_flat, preferred_element_type=jnp.float32) + mixer_piece
        mixed = mixed.reshape(group_rows, 3, heads_local, HD)
        cosine, sine = tables(group_places)
        query = (
            rotate(mixed[:, 0], cosine, sine)
            .astype(jnp.bfloat16)
            .reshape(-1, ROW_PATCHES, heads_local, HD)
        )
        key_rows = (
            rotate(mixed[:, 1], cosine, sine)
            .astype(jnp.bfloat16)
            .reshape(-1, ROW_PATCHES, heads_local, HD)
        )
        value_rows = mixed[:, 2].astype(jnp.bfloat16).reshape(-1, ROW_PATCHES, heads_local, HD)
        permitted_pairs = allowed_mask(group_picture, group_live)
        attended, log_total = attend(query, key_rows, value_rows, permitted_pairs)
        attended = attended.reshape(group_rows, width_local).astype(jnp.bfloat16)
        branch = lax.psum_scatter(
            jnp.dot(attended, output_local, preferred_element_type=jnp.float32).astype(
                jnp.bfloat16
            ),
            "fsdp",
            scatter_dimension=0,
            tiled=True,
        ).astype(jnp.float32)
        middle = inputs + branch + output_shift.astype(jnp.float32)
        shifted_two, normed_two, recip_two = norm_forward(middle, gain_two, shift_two)
        lowered_two = shifted_two.astype(jnp.bfloat16)
        group_two = lax.all_gather(lowered_two, "fsdp", axis=0, tiled=True)
        upper = jnp.dot(group_two, upward_local, preferred_element_type=jnp.float32) + upward_piece
        active = (upper * jax.nn.sigmoid(1.702 * upper)).astype(jnp.bfloat16)
        lowered = lax.psum_scatter(
            jnp.dot(active, downward_local, preferred_element_type=jnp.float32).astype(
                jnp.bfloat16
            ),
            "fsdp",
            scatter_dimension=0,
            tiled=True,
        ).astype(jnp.float32)
        outputs = middle + lowered + downward_shift.astype(jnp.float32)
        difference = outputs - target
        masked = occupied_rows[:, None] * difference
        errors = errors + jnp.sum(masked * difference)
        grad_out = 2.0 * factor * masked
        grad_low = grad_out.astype(jnp.bfloat16)
        down_bias_term = jnp.sum(grad_low.astype(jnp.float32), axis=0)
        group_grad = lax.all_gather(grad_low, "fsdp", axis=0, tiled=True)
        g_down = jnp.einsum("rf,rd->fd", active, group_grad, preferred_element_type=jnp.float32)
        grad_active = jnp.einsum(
            "rd,fd->rf", group_grad, downward_local, preferred_element_type=jnp.float32
        )
        grad_upper = quick_gelu_grad(grad_active, upper)
        g_up = jnp.einsum("rd,rf->df", group_two, grad_upper, preferred_element_type=jnp.float32)
        up_bias_term = lax.dynamic_update_slice_in_dim(
            jnp.zeros((FF,), jnp.float32),
            jnp.sum(grad_upper.astype(jnp.float32), axis=0),
            member * hidden_local,
            0,
        )
        grad_two = lax.psum_scatter(
            jnp.einsum(
                "rf,df->rd", grad_upper, upward_local, preferred_element_type=jnp.float32
            ).astype(jnp.bfloat16),
            "fsdp",
            scatter_dimension=0,
            tiled=True,
        ).astype(jnp.float32)
        back_two, g_gain_two, g_shift_two = norm_backward(grad_two, normed_two, recip_two, gain_two)
        grad_middle = grad_out + back_two
        grad_branch = grad_middle.astype(jnp.bfloat16)
        out_bias_term = jnp.sum(grad_branch.astype(jnp.float32), axis=0)
        group_branch = lax.all_gather(grad_branch, "fsdp", axis=0, tiled=True)
        g_output = jnp.einsum(
            "rd,re->de", attended, group_branch, preferred_element_type=jnp.float32
        )
        grad_attended = jnp.einsum(
            "re,de->rd", group_branch, output_local, preferred_element_type=jnp.float32
        )
        grad_attended = grad_attended.astype(jnp.bfloat16).reshape(-1, ROW_PATCHES, heads_local, HD)
        grad_query, grad_key, grad_value = attend_back(
            grad_attended, query, key_rows, value_rows, permitted_pairs, log_total
        )
        grad_mixed = jnp.stack(
            [
                unrotate(grad_query.reshape(group_rows, heads_local, HD), cosine, sine),
                unrotate(grad_key.reshape(group_rows, heads_local, HD), cosine, sine),
                grad_value.reshape(group_rows, heads_local, HD),
            ],
            axis=1,
        )
        grad_mixed = grad_mixed.reshape(group_rows, 3 * width_local).astype(jnp.bfloat16)
        g_mixer = jnp.einsum("rd,re->de", group_one, grad_mixed, preferred_element_type=jnp.float32)
        g_mixer = g_mixer.reshape(D, 3, width_local)
        mixer_bias_term = lax.dynamic_update_slice_in_dim(
            jnp.zeros((3, D), jnp.float32),
            jnp.sum(grad_mixed.astype(jnp.float32), axis=0).reshape(3, width_local),
            member * width_local,
            1,
        )
        mixer_bias_term = mixer_bias_term.reshape(3 * D)
        grad_one = lax.psum_scatter(
            jnp.einsum(
                "re,de->rd", grad_mixed, mixer_flat, preferred_element_type=jnp.float32
            ).astype(jnp.bfloat16),
            "fsdp",
            scatter_dimension=0,
            tiled=True,
        ).astype(jnp.float32)
        back_one, g_gain_one, g_shift_one = norm_backward(grad_one, normed_one, recip_one, gain_one)
        grad_inputs = grad_middle + back_one
        matrices = (g_mixer, g_output, g_up, g_down)
        smalls = (
            g_gain_one,
            g_shift_one,
            mixer_bias_term,
            out_bias_term,
            g_gain_two,
            g_shift_two,
            up_bias_term,
            down_bias_term,
        )
        matrix_sums = (
            matrices if matrix_sums is None else jax.tree.map(jnp.add, matrix_sums, matrices)
        )
        small_sums = smalls if small_sums is None else jax.tree.map(jnp.add, small_sums, smalls)
        results.append(outputs.astype(jnp.bfloat16))
        input_grads.append(grad_inputs)
    g_mixer_sum, g_output_sum, g_up_sum, g_down_sum = matrix_sums
    reduced = (
        lax.psum_scatter(
            g_mixer_sum.astype(jnp.bfloat16), "dp", scatter_dimension=0, tiled=True
        ).astype(jnp.float32),
        lax.psum_scatter(
            g_output_sum.astype(jnp.bfloat16), "dp", scatter_dimension=1, tiled=True
        ).astype(jnp.float32),
        lax.psum_scatter(
            g_up_sum.astype(jnp.bfloat16), "dp", scatter_dimension=0, tiled=True
        ).astype(jnp.float32),
        lax.psum_scatter(
            g_down_sum.astype(jnp.bfloat16), "dp", scatter_dimension=1, tiled=True
        ).astype(jnp.float32),
    )
    totals = lax.psum(
        (
            small_sums[0],
            small_sums[1],
            small_sums[2],
            small_sums[3],
            small_sums[4],
            small_sums[5],
            small_sums[6],
            small_sums[7],
            errors,
        ),
        ("dp", "fsdp"),
    )
    pieces = [own_slice(totals[index], data_index, data_ways) for index in range(8)]
    query_key_piece = own_slice(totals[2][: 2 * D], data_index, data_ways)
    value_piece = own_slice(totals[2][2 * D :], data_index, data_ways)
    loss = totals[8] / (token_tally * D)
    return (
        jnp.concatenate(results, axis=0),
        loss,
        jnp.concatenate(input_grads, axis=0),
        pieces[0],
        pieces[1],
        reduced[0],
        query_key_piece,
        value_piece,
        reduced[1],
        pieces[3],
        pieces[4],
        pieces[5],
        reduced[2],
        pieces[6],
        reduced[3],
        pieces[7],
    )


BF = jnp.bfloat16
F32 = jnp.float32
HEADS_LOCAL = 4
W = 320
F = 1280
R = 384
G = 1536
BLK = 160
SUB = 128
QUAD = 512
HALF = 640
MESH_ID = pl.DeviceIdType.MESH


def _nn(a, b):
    return lax.dot_general(a, b, (((1,), (0,)), ((), ())), preferred_element_type=F32)


def _nt(a, b):
    return lax.dot_general(a, b, (((1,), (1,)), ((), ())), preferred_element_type=F32)


def _tn(a, b):
    return lax.dot_general(a, b, (((0,), (0,)), ((), ())), preferred_element_type=F32)


def _ds(start, size, step):
    if isinstance(start, int):
        return pl.ds(start, size)
    return pl.ds(pl.multiple_of(start, step), size)


class Place:
    def __init__(self):
        dp = lax.axis_index("dp")
        fs = lax.axis_index("fsdp")
        z, x = lax.div(dp, 2), lax.rem(dp, 2)
        y, c = lax.div(fs, 2), lax.rem(fs, 2)
        self.z, self.x, self.fs, self.dp = z, x, fs, dp
        self.core = (dp, 2 * y + 1 - c)
        self.ynb = (dp, 2 * (1 - y) + c)
        self.xnb = (2 * z + 1 - x, fs)
        self.zs = (z, z + 1 - 2 * lax.rem(z, 2), lax.rem(z + 2, 4), 3 - z)
        self.zn = tuple((2 * zk + x, fs) for zk in self.zs)
        self.up = (2 * jnp.minimum(z + 1, 3) + x, fs)
        self.down = (2 * jnp.maximum(z - 1, 0) + x, fs)
        self.near = lax.div(z, 2)
        self.far = 1 - self.near

    def barrier(self):
        sem = pltpu.get_barrier_semaphore()
        for peer in (self.core, self.ynb, self.xnb) + self.zn[1:]:
            pl.semaphore_signal(sem, inc=1, device_id=peer, device_id_type=MESH_ID)
        pl.semaphore_wait(sem, 6)


def _send(src, dst, ss, rs, peer):
    return pltpu.make_async_remote_copy(
        src_ref=src, dst_ref=dst, send_sem=ss, recv_sem=rs, device_id=peer, device_id_type=MESH_ID
    )


class Gather:
    def __init__(self, place, buf, ss, rs, cols=slice(None)):
        self.place, self.buf, self.ss, self.rs, self.cols = place, buf, ss, rs, cols

    def part(self, s, slot):
        return self.buf.at[_ds(QUAD * s + SUB * slot, SUB, SUB), self.cols]

    def to_core(self, s):
        return _send(self.part(s, 0), self.part(s, 1), self.ss.at[s], self.rs.at[s], self.place.core)

    def to_y(self, s):
        return _send(self.part(s, 0), self.part(s, 2), self.ss.at[3 + s], self.rs.at[3 + s], self.place.ynb)

    def on(self, s):
        return _send(self.part(s, 2), self.part(s, 3), self.ss.at[6 + s], self.rs.at[6 + s], self.place.core)

    def start(self, s):
        self.to_y(s).start()
        self.to_core(s).start()

    def pass_on(self, s):
        self.to_y(s).wait_recv()
        self.on(s).start()

    def ready(self, s):
        self.to_core(s).wait_recv()
        self.on(s).wait_recv()

    def end(self):
        for s in range(3):
            self.to_core(s).wait_send()
            self.to_y(s).wait_send()
            self.on(s).wait_send()


class Scatter:
    def __init__(self, place, sb, rb, own, ss, rs, cols=slice(None)):
        self.place, self.sb, self.rb, self.own, self.ss, self.rs, self.cols = place, sb, rb, own, ss, rs, cols

    def copy(self, kind, s):
        peer = self.place.ynb if kind == 1 else self.place.core
        slot = 2 + s if kind == 1 else kind // 2
        return _send(
            self.sb.at[slot, :, self.cols],
            self.rb.at[kind, s, :, self.cols],
            self.ss.at[3 * kind + s],
            self.rs.at[3 * kind + s],
            peer,
        )

    def again(self, kind, s):
        if isinstance(s, int):
            if s > 0:
                self.copy(kind, s - 1).wait_send()
        else:
            pl.when(s > 0)(lambda: self.copy(kind, s - 1).wait_send())

    def post(self, s, lhs, rhs):
        rows = QUAD * s
        term = _nt(lhs(_ds(rows + 2 * SUB, 2 * SUB, SUB)), rhs())
        self.again(0, s)
        self.sb[0, :, self.cols] = term[SUB:].astype(BF)
        self.copy(0, s).start()
        mine = _nt(lhs(_ds(rows, 2 * SUB, SUB)), rhs())
        self.again(2, s)
        self.sb[1, :, self.cols] = mine[SUB:].astype(BF)
        self.copy(2, s).start()
        self.own[_ds(SUB * s, SUB, SUB), self.cols] = mine[:SUB]
        self.copy(0, s).wait_recv()
        self.sb[2 + s, :, self.cols] = (term[:SUB] + self.rb[0, s, :, self.cols].astype(F32)).astype(BF)
        self.copy(1, s).start()

    def wait(self, s):
        self.copy(2, s).wait_recv()
        self.copy(1, s).wait_recv()

    def total(self, s, i, step):
        sub = _ds(step * i, step, step)
        return self.own[_ds(SUB * s + step * i, step, step), self.cols] + (
            self.rb[2, s, sub, self.cols].astype(F32) + self.rb[1, s, sub, self.cols].astype(F32)
        )

    def end(self):
        self.copy(0, 2).wait_send()
        self.copy(2, 2).wait_send()
        for s in range(3):
            self.copy(1, s).wait_send()


def _norm(values):
    average = jnp.mean(values, axis=-1, keepdims=True)
    centered = values - average
    reciprocal = lax.rsqrt(jnp.mean(centered * centered, axis=-1, keepdims=True) + EPSILON)
    return centered * reciprocal, reciprocal


def _head_rows(lanes, offset):
    lane = lax.broadcasted_iota(jnp.int32, (1, lanes), 1) - offset
    return [
        jnp.where((lane >= HD * h) & (lane < HD * h + HD), 1.0, 0.0).astype(BF)
        for h in range(HEADS_LOCAL)
    ]


def _stack(values, heads):
    return jnp.concatenate([values * head for head in heads], axis=0)


def _allowed(auxb):
    lane = lax.broadcasted_iota(jnp.int32, (1, 128), 1)
    picks = (lane >= 96) & (lane < 104)
    left = jnp.where(picks, auxb.astype(F32), jnp.where(lane == 104, 1.0, 0.0)).astype(BF)
    score = _nt(left, auxb)
    here = lax.broadcasted_iota(jnp.int32, (128, 128), 0)
    there = lax.broadcasted_iota(jnp.int32, (128, 128), 1)
    return (score > 1.5) | (here == there)


def _softmax(scores, allowed):
    probs = []
    for h in range(HEADS_LOCAL):
        part = jnp.where(allowed, scores[:, 128 * h : 128 * h + 128], -1e30)
        grown = jnp.exp(part - jnp.max(part, axis=-1, keepdims=True))
        probs.append(grown * (1.0 / jnp.sum(grown, axis=-1, keepdims=True)))
    return probs


PIECES = ((0, 0, 1024), (0, 1024, 256), (1, 0, 1280), (2, 0, 1280))


def layer_kernel(
    tok_h, teach_h, aux_h, wa_h, wu_h, wd_h, sv, tabs,
    res_h, gtok_h, gw_h, small_o, loss_o, keep_h,
    tok, aux, w, wo, n1a, n2, gu, gzb, qk, v, o, acc, own, mid, gy, sb, rb,
    gb, xin, zin, fin, vecs, cst, cca, small, stage, came,
    ws, wr, ags, agr, rss, rsr, vs, vr, cs, cr, xs, xr, zs, zr, ss, sr, ls, os_, xfree, zfree, gfree,
):
    place = Place()
    z, x = place.z, place.x
    patches = TOTAL[0]
    mine = _ds(BLK * (2 * z + x), BLK, 32)
    loads = [
        pltpu.make_async_copy(src, dst, ls.at[i])
        for i, (src, dst) in enumerate(
            [(tok_h, tok)]
            + [(aux_h.at[pl.ds(SUB * s, SUB), :], aux.at[pl.ds(QUAD * s, SUB), :]) for s in range(3)]
            + [(wa_h, w.at[0, mine, :]), (wu_h, w.at[1, mine, :]), (wd_h, w.at[2, mine, :])]
        )
    ]
    for copy in loads:
        copy.start()
    place.barrier()

    shards = (wa_h, wu_h, wd_h)

    def at(piece, zk, xk):
        third, start, size = PIECES[piece]
        return w.at[third, _ds(BLK * (2 * zk + xk), BLK, 32), pl.ds(start, size)]

    def shard(piece):
        third, start, size = PIECES[piece]
        return shards[third].at[:, pl.ds(start, size)]

    def first(piece, i):
        peer = (place.xnb, place.up, place.down)[i]
        return _send(shard(piece), at(piece, z, x), ws.at[piece, i], wr.at[piece, 2 * z + x], peer)

    def begin_z(piece):
        pl.when(z < 3)(lambda: first(piece, 1).start())
        pl.when(z > 0)(lambda: first(piece, 2).start())

    def begin_x(piece):
        first(piece, 0).start()

    def hop(piece, d, i):
        zk = jnp.maximum(z - d, 0) if i < 2 else jnp.minimum(z + d, 3)
        peer = (place.up, place.xnb, place.down, place.xnb)[i]
        there = at(piece, zk, x)
        return _send(there, there, ws.at[piece, 4 * d - 1 + i], wr.at[piece, 2 * zk + x], peer)

    def relay(piece, d):
        @pl.when(z >= d)
        def _():
            hop(piece, d, 0).wait_recv()
            pl.when(z < 3)(lambda: hop(piece, d, 0).start())
            hop(piece, d, 1).start()

        @pl.when(z + d <= 3)
        def _():
            hop(piece, d, 2).wait_recv()
            pl.when(z > 0)(lambda: hop(piece, d, 2).start())
            hop(piece, d, 3).start()

    def over_x(piece, zk):
        there = at(piece, zk, 1 - x)
        _send(there, there, ws.at[piece, 0], wr.at[piece, 2 * zk + 1 - x], place.xnb).wait_recv()

    def complete(piece):
        for k in range(4):
            over_x(piece, place.zs[k])

    def sent(piece):
        first(piece, 0).wait_send()
        pl.when(z < 3)(lambda: first(piece, 1).wait_send())
        pl.when(z > 0)(lambda: first(piece, 2).wait_send())
        for d in range(1, 4):

            @pl.when(z >= d)
            def _(d=d):
                pl.when(z < 3)(lambda: hop(piece, d, 0).wait_send())
                hop(piece, d, 1).wait_send()

            @pl.when(z + d <= 3)
            def _(d=d):
                pl.when(z > 0)(lambda: hop(piece, d, 2).wait_send())
                hop(piece, d, 3).wait_send()

    outs = []

    def out(src, dst):
        copy = pltpu.make_async_copy(src, dst, os_.at[len(outs)])
        copy.start()
        outs.append(copy)
        return len(outs) - 1

    begin_z(0)
    begin_x(0)

    vector_hops = [
        _send(stage.at[i, pl.ds(0, 8), :], came.at[i, pl.ds(0, 8), :], vs.at[i], vr.at[i], peer)
        for i, peer in enumerate((place.xnb, place.zn[1], place.zn[2]))
    ]
    stage[0, :8, :] = sv[...]
    agx = Gather(place, aux, ags.at[1], agr.at[1])
    for i in range(3):
        vector_hops[i].start()
        loads[1 + i].wait()
        agx.start(i)
        vector_hops[i].wait_recv()
        total = stage[i, :8, :] + came[i, :8, :]
        if i < 2:
            stage[i + 1, :8, :] = total
        else:
            vecs[...] = total

    loads[0].wait()
    ag1 = Gather(place, n1a, ags.at[0], agr.at[0])

    def first_norm(i, s):
        rows = _ds(QUAD * s + 32 * i, 32, 32)
        normed, _r = _norm(tok[_ds(SUB * s + 32 * i, 32, 32), :].astype(F32))
        n1a[rows, :] = (normed * vecs[0:1, :] + vecs[1:2, :]).astype(BF)
        return s

    for s in range(3):
        lax.fori_loop(0, 4, first_norm, s)
        ag1.start(s)
    relay(0, 1)
    begin_z(1)
    for s in range(3):
        agx.pass_on(s)
    ag1.pass_on(0)
    ag1.pass_on(1)
    relay(0, 2)
    begin_z(2)
    for s in range(3):
        agx.ready(s)

    count_hops = [
        _send(cst.at[i], cca.at[i], cs.at[i], cr.at[i], peer)
        for i, peer in enumerate((place.xnb, place.zn[1], place.zn[2]))
    ]
    cst[0] = _nn(jnp.ones((8, G), BF), aux[...])
    count_hops[0].start()
    ag1.pass_on(2)
    count_hops[0].wait_recv()
    cst[1] = cst[0] + cca[0]
    count_hops[1].start()
    relay(0, 3)
    begin_x(1)
    relay(1, 1)
    count_hops[1].wait_recv()
    cst[2] = cst[1] + cca[1]
    count_hops[2].start()
    relay(1, 2)
    relay(1, 3)
    begin_x(2)
    count_hops[2].wait_recv()
    real_count = (cst[2] + cca[2])[0:1, 104:105]
    complete(0)
    loads[4].wait()

    left = _head_rows(2 * W, 0)
    right = _head_rows(2 * W, W)
    side = _head_rows(W, 0)
    rs1 = Scatter(place, sb, rb, own, rss.at[0], rsr.at[0])

    def attend_part(s, _):
        ag1.ready(s)
        acc[:, : 3 * W] = _nn(n1a[_ds(QUAD * s, QUAD, QUAD), :], w[0, :, : 3 * W]) + vecs[7:8, : 3 * W]

        def attend_rows(i, _):
            here = _ds(SUB * i, SUB, SUB)
            rows = _ds(QUAD * s + SUB * i, SUB, SUB)
            auxb = aux[rows, :]
            angle = _nn(auxb, tabs[...])
            raw = acc[here, : 2 * W]
            turned = (
                raw * angle[:, : 2 * W]
                + pltpu.roll(raw, 2 * W - 40, 1) * angle[:, 2 * W : 4 * W]
                + pltpu.roll(raw, 40, 1) * angle[:, 4 * W :]
            )
            qkb = turned.astype(BF)
            kqb = pltpu.roll(turned, W, 1).astype(BF)
            vb = acc[here, 2 * W : 3 * W].astype(BF)
            qk[rows, :] = qkb
            v[rows, :] = vb
            scores = _nt(qkb, _stack(kqb, left)) * HD ** (-0.5)
            probs = _softmax(scores, _allowed(auxb))
            flat = jnp.concatenate([p.astype(BF) for p in probs], axis=1)
            o[rows, :] = _nn(flat, _stack(vb, side)).astype(BF)
            return 0

        lax.fori_loop(0, 4, attend_rows, 0)

        @pl.when(s == 0)
        def _():
            complete(1)
            wo[...] = w[0, :, 3 * W :]
            relay(2, 1)

        rs1.post(s, lambda rows: o[rows, :], lambda: wo[...])

        @pl.when(s == 1)
        def _():
            relay(2, 2)
            begin_z(3)

        return 0

    lax.fori_loop(0, 3, attend_part, 0)
    n1_kept = out(n1a, keep_h)
    ag2 = Gather(place, n2, ags.at[2], agr.at[2])

    def second_norm(s, _):
        rs1.wait(s)

        def rows_of(i, _):
            rows = _ds(SUB * s + 32 * i, 32, 32)
            middle = tok[rows, :].astype(F32) + rs1.total(s, i, 32) + vecs[2:3, :]
            mid[rows, :] = middle
            normed, _r = _norm(middle)
            n2[_ds(QUAD * s + 32 * i, 32, 32), :] = (normed * vecs[3:4, :] + vecs[4:5, :]).astype(BF)
            return 0

        lax.fori_loop(0, 4, rows_of, 0)
        ag2.start(s)

        @pl.when(s == 0)
        def _():
            relay(2, 3)
            begin_x(3)

        return 0

    lax.fori_loop(0, 3, second_norm, 0)
    teach = tok
    teach_load = pltpu.make_async_copy(teach_h, teach, ls.at[7])
    teach_load.start()
    relay(3, 1)
    ag1.end()
    outs[n1_kept].wait()
    loads[5].wait()
    complete(2)

    def up_part(s, _):
        ag2.pass_on(s)
        ag2.ready(s)
        acc[...] = _nn(n2[_ds(QUAD * s, QUAD, QUAD), :], w[1]) + vecs[6:7, :]

        def rows_of(i, _):
            upper = acc[_ds(32 * i, 32, 32), :]
            rows = _ds(QUAD * s + 32 * i, 32, 32)
            gate = 1.0 / (1.0 + jnp.exp(-1.702 * upper))
            n1a[rows, :] = (upper * gate).astype(BF)
            gu[rows, :] = (gate + 1.702 * upper * gate * (1.0 - gate)).astype(BF)
            return 0

        lax.fori_loop(0, QUAD // 32, rows_of, 0)
        return 0

    lax.fori_loop(0, 3, up_part, 0)
    act = n1a
    relay(3, 2)
    rs1.end()
    loads[6].wait()
    teach_load.wait()

    cols = {0: _ds(HALF * place.near, HALF, 128), 1: _ds(HALF * place.far, HALF, 128)}
    factor = 2.0 * patches / real_count
    downs = [Scatter(place, sb, rb, own, rss.at[1 + j], rsr.at[1 + j], cols[j]) for j in range(2)]
    gathers = [Gather(place, gzb, ags.at[3 + j], agr.at[3 + j], cols[j]) for j in range(2)]
    small[...] = jnp.zeros_like(small)

    for j in range(2):
        for k in ((0, 1), (2, 3))[j]:
            over_x(3, place.zs[k])
        half = (place.near, place.far)[j]

        def down_part(s, _, j=j, half=half):
            downs[j].post(s, lambda rows: act[rows, :], lambda: w[2, _ds(HALF * half, HALF, 128), :])
            return 0

        lax.fori_loop(0, 3, down_part, 0)

        def finish_part(s, sums, j=j):
            downs[j].wait(s)

            def rows_of(i, sums):
                rows = _ds(SUB * s + 32 * i, 32, 32)
                result = mid[rows, cols[j]] + downs[j].total(s, i, 32) + vecs[5:6, cols[j]]
                real = aux[_ds(QUAD * s + 32 * i, 32, 32), 104:105].astype(F32)
                difference = result - teach[rows, cols[j]].astype(F32)
                masked = real * difference
                gout = factor * masked
                low = gout.astype(BF)
                gy[rows, cols[j]] = gout
                teach[rows, cols[j]] = result.astype(BF)
                gzb[_ds(QUAD * s + 32 * i, 32, 32), cols[j]] = low
                return (
                    sums[0] + jnp.sum(masked * difference, axis=0, keepdims=True),
                    sums[1] + jnp.sum(low.astype(F32), axis=0, keepdims=True),
                )

            sums = lax.fori_loop(0, 4, rows_of, sums)
            gathers[j].start(s)
            if j == 0:
                pl.when(s == 1)(lambda: relay(3, 3))
            else:
                gathers[0].pass_on(s)
            return sums

        zero = jnp.zeros((1, HALF), F32)
        sums = lax.fori_loop(0, 3, finish_part, (zero, zero))
        small[6:7, cols[j]] = sums[0]
        small[5:6, cols[j]] = sums[1]
    res_out = out(teach, res_h)

    def to_x(chunk, slot, k):
        rows = _ds(BLK * (2 * place.zs[k] + 1 - x), BLK, 32)
        return _send(gb.at[slot, rows, :], xin.at[slot, k], xs.at[chunk, k], xr.at[chunk, k], place.xnb)

    def to_z(chunk, slot, k):
        rows = _ds(BLK * (2 * place.zs[k] + x), BLK, 32)
        return _send(
            gb.at[slot, rows, :], zin.at[slot, k - 1], zs.at[chunk, k - 1], zr.at[chunk, k - 1], place.zn[k]
        )

    def tile(slot, lhs, rhs, half):
        rows = _ds(HALF * half, HALF, 128)
        for part in range(2):
            cols = pl.ds(HALF * part, HALF)
            gb[slot, rows, cols] = _tn(lhs[:, rows], rhs[:, cols]).astype(BF)

    def add_x(chunk, slot, k):
        to_x(chunk, slot, k).wait_recv()
        rows = _ds(BLK * (2 * place.zs[k] + x), BLK, 32)
        gb[slot, rows, :] = (gb[slot, rows, :].astype(F32) + xin[slot, k].astype(F32)).astype(BF)
        to_z(chunk, slot, k).start()

    def add_z(chunk, slot):
        to_x(chunk, slot, 0).wait_recv()
        for k in range(1, 4):
            to_z(chunk, slot, k).wait_recv()

        def rows_of(i, _):
            rows = _ds(32 * i, 32, 32)
            kept = _ds(BLK * (2 * z + x) + 32 * i, 32, 32)
            fin[rows, :] = (gb[slot, kept, :].astype(F32) + xin[slot, 0, rows, :].astype(F32)) + (
                zin[slot, 0, rows, :].astype(F32)
                + zin[slot, 1, rows, :].astype(F32)
                + zin[slot, 2, rows, :].astype(F32)
            )
            return 0

        lax.fori_loop(0, BLK // 32, rows_of, 0)
        return out(fin, gw_h.at[chunk])

    for s in range(3):
        gathers[0].ready(s)
    tile(0, gzb, act, place.near)
    to_x(2, 0, 1).start()
    to_x(2, 0, 0).start()

    for copy in downs:
        copy.end()
    rs3 = Scatter(place, sb, rb, own, rss.at[3], rsr.at[3])
    up_total = jnp.zeros((1, F), F32)
    for s in range(3):
        gathers[1].pass_on(s)
    gathers[1].ready(0)
    for s in range(3):
        acc[...] = _nn(gzb[pl.ds(QUAD * s, QUAD), :], w[2])

        def gate_rows(i, total, s=s):
            rows = _ds(QUAD * s + 32 * i, 32, 32)
            low = (acc[_ds(32 * i, 32, 32), :] * gu[rows, :].astype(F32)).astype(BF)
            gu[rows, :] = low
            return total + jnp.sum(low.astype(F32), axis=0, keepdims=True)

        up_total = lax.fori_loop(0, QUAD // 32, gate_rows, up_total)
        rs3.post(s, lambda rows: gu[rows, :], lambda: w[1])
        if s == 0:
            for t in (1, 2):
                gathers[1].ready(t)
            tile(0, gzb, act, place.far)
            to_x(2, 0, 2).start()
            to_x(2, 0, 3).start()
    for gather in gathers:
        gather.end()
    for peer in (place.core, place.ynb):
        pl.semaphore_signal(gfree, inc=1, device_id=peer, device_id_type=MESH_ID)
    n1_back = pltpu.make_async_copy(keep_h, n1a, ls.at[8])
    n1_back.start()
    outs[res_out].wait()
    tok_back = pltpu.make_async_copy(tok_h, tok, ls.at[9])
    tok_back.start()
    small[pl.ds(8 + place.fs, 1), :] = up_total
    add_x(2, 0, 1)
    tile(1, n2, gu, place.far)
    to_x(1, 1, 2).start()
    to_x(1, 1, 3).start()
    pl.semaphore_wait(gfree, 2)
    ag3 = Gather(place, gzb, ags.at[5], agr.at[5])

    def norm_rows(s, i, sums, values, gain, terms):
        rows = _ds(SUB * s + 32 * i, 32, 32)
        grad = terms.total(s, i, 32)
        normed, reciprocal = _norm(values[rows, :].astype(F32))
        scaled = grad * gain
        back = (
            scaled
            - jnp.mean(scaled, axis=-1, keepdims=True)
            - normed * jnp.mean(scaled * normed, axis=-1, keepdims=True)
        ) * reciprocal
        total = gy[rows, :] + back
        gy[rows, :] = total
        pair = (
            sums[0] + jnp.sum(grad * normed, axis=0, keepdims=True),
            sums[1] + jnp.sum(grad, axis=0, keepdims=True),
        )
        return total, pair

    zero = jnp.zeros((1, D), F32)

    def second_back(s, sums):
        rs3.wait(s)

        def rows_of(i, sums):
            total, pair = norm_rows(s, i, sums[:2], mid, vecs[3:4, :], rs3)
            low = total.astype(BF)
            gzb[_ds(QUAD * s + 32 * i, 32, 32), :] = low
            return pair + (sums[2] + jnp.sum(low.astype(F32), axis=0, keepdims=True),)

        sums = lax.fori_loop(0, 4, rows_of, sums)
        ag3.start(s)
        return sums

    gain2, shift2, outb = lax.fori_loop(0, 3, second_back, (zero, zero, zero))
    small[2:3, :] = outb
    small[3:4, :] = gain2
    small[4:5, :] = shift2
    tile(1, n2, gu, place.near)
    to_x(1, 1, 1).start()
    to_x(1, 1, 0).start()
    add_x(2, 0, 2)
    add_x(2, 0, 3)
    rs3.end()
    rs4 = Scatter(place, sb, rb, own, rss.at[4], rsr.at[4])

    def attend_back(s, total):
        ag3.pass_on(s)
        ag3.ready(s)
        acc[:, :W] = _nn(gzb[_ds(QUAD * s, QUAD, QUAD), :], wo[...])

        def attend_rows(i, total):
            rows = _ds(QUAD * s + SUB * i, SUB, SUB)
            auxb = aux[rows, :]
            qkb = qk[rows, :]
            kqb = pltpu.roll(qkb.astype(F32), W, 1).astype(BF)
            vb = v[rows, :]
            gob = acc[_ds(SUB * i, SUB, SUB), :W].astype(BF)
            keys = _stack(kqb, left)
            scores = _nt(qkb, keys) * HD ** (-0.5)
            probs = _softmax(scores, _allowed(auxb))
            gprobs = _nt(gob, _stack(vb, side))
            gscores = []
            for h in range(HEADS_LOCAL):
                gp = gprobs[:, 128 * h : 128 * h + 128]
                delta = jnp.sum(gp * probs[h], axis=-1, keepdims=True)
                gscores.append((probs[h] * (gp - delta)).astype(BF))
            flat = jnp.concatenate(gscores, axis=1)
            tall = jnp.concatenate(gscores, axis=0)
            ptall = jnp.concatenate([p.astype(BF) for p in probs], axis=0)
            gqk = (_nn(flat, keys) + _tn(tall, _stack(kqb, right))) * HD ** (-0.5)
            gv = _tn(ptall, _stack(gob, side))
            angle = _nn(auxb, tabs[...])
            turned = (
                gqk * angle[:, : 2 * W]
                + pltpu.roll(gqk * angle[:, 4 * W :], 2 * W - 40, 1)
                + pltpu.roll(gqk * angle[:, 2 * W : 4 * W], 40, 1)
            )
            low = jnp.concatenate([turned, gv], axis=1).astype(BF)
            gu[rows, : 3 * W] = low
            return total + jnp.sum(low.astype(F32), axis=0, keepdims=True)

        total = lax.fori_loop(0, 4, attend_rows, total)
        rs4.post(s, lambda rows: gu[rows, : 3 * W], lambda: w[0, :, : 3 * W])

        @pl.when(s == 0)
        def _():
            add_x(1, 1, 2)

        @pl.when(s == 1)
        def _():
            add_x(1, 1, 3)

        return total

    mix_total = lax.fori_loop(0, 3, attend_back, jnp.zeros((1, 3 * W), F32))
    small[pl.ds(12 + place.fs, 1), : 3 * W] = mix_total

    down_out = add_z(2, 0)
    pl.semaphore_signal(xfree, inc=1, device_id=place.xnb, device_id_type=MESH_ID)
    for peer in place.zn[1:]:
        pl.semaphore_signal(zfree, inc=1, device_id=peer, device_id_type=MESH_ID)

    for k in range(4):
        to_x(2, 0, k).wait_send()
    for k in range(1, 4):
        to_z(2, 0, k).wait_send()
    n1_back.wait()

    def last_tile(half):
        rows = _ds(HALF * half, HALF, 128)
        gb[0, rows, : 3 * W] = _tn(n1a[:, rows], gu[:, : 3 * W]).astype(BF)
        gb[0, rows, 3 * W :] = _tn(gzb[:, rows], o[...]).astype(BF)

    last_tile(place.far)
    pl.semaphore_wait(xfree, 1)
    to_x(0, 0, 2).start()
    to_x(0, 0, 3).start()
    last_tile(place.near)
    to_x(0, 0, 1).start()
    to_x(0, 0, 0).start()
    add_x(1, 1, 1)

    tok_back.wait()

    def first_back(s, sums):
        rs4.wait(s)
        return lax.fori_loop(0, 4, lambda i, t: norm_rows(s, i, t, tok, vecs[0:1, :], rs4)[1], sums)

    gain1, shift1 = lax.fori_loop(0, 3, first_back, (zero, zero))
    out(gy, gtok_h)
    small[0:1, :] = gain1
    small[1:2, :] = shift1

    hops = [
        _send(stage.at[i], came.at[i], ss.at[i], sr.at[i], peer)
        for i, peer in enumerate((place.core, place.ynb, place.xnb, place.zn[1], place.zn[2]))
    ]
    for hop_ in vector_hops:
        hop_.wait_send()
    stage[0] = small[...]
    hops[0].start()
    pl.semaphore_wait(zfree, 3)
    outs[down_out].wait()

    def next_hop(i):
        hops[i].wait_recv()
        total = stage[i] + came[i]
        if i < 4:
            stage[i + 1] = total
            hops[i + 1].start()
        else:
            small_o[...] = total
            loss_o[...] = jnp.sum(total[6:7, :], axis=-1, keepdims=True) / (real_count * D)

    add_x(0, 0, 2)
    next_hop(0)
    up_out = add_z(1, 1)
    next_hop(1)
    add_x(0, 0, 3)
    next_hop(2)
    add_x(0, 0, 1)
    next_hop(3)
    next_hop(4)
    outs[up_out].wait()
    add_z(0, 0)

    for piece in range(4):
        sent(piece)
    agx.end()
    ag2.end()
    ag3.end()
    rs4.end()
    for hop_ in count_hops + hops:
        hop_.wait_send()
    for chunk, slot in ((1, 1), (0, 0)):
        for k in range(4):
            to_x(chunk, slot, k).wait_send()
        for k in range(1, 4):
            to_z(chunk, slot, k).wait_send()
    for i, copy in enumerate(outs):
        if i not in (n1_kept, res_out, down_out, up_out):
            copy.wait()


TOTAL = [0]


def layer_call(*operands):
    any_, vm = pl.ANY, pltpu.VMEM
    outs = [
        ((R, D), BF, any_),
        ((R, D), F32, any_),
        ((3, BLK, D), F32, any_),
        ((16, D), F32, vm),
        ((1, 1), F32, vm),
        ((G, D), BF, any_),
    ]
    dma = pltpu.SemaphoreType.DMA
    scratch = [
        vm((R, D), BF),
        vm((G, 128), BF),
        vm((3, D, D), BF),
        vm((D, W), BF),
        vm((G, D), BF),
        vm((G, D), BF),
        vm((G, F), BF),
        vm((G, D), BF),
        vm((G, 2 * W), BF),
        vm((G, W), BF),
        vm((G, W), BF),
        vm((QUAD, D), F32),
        vm((R, D), F32),
        vm((R, D), F32),
        vm((R, D), F32),
        vm((5, SUB, D), BF),
        vm((3, 3, SUB, D), BF),
        vm((2, D, D), BF),
        vm((2, 4, BLK, D), BF),
        vm((2, 3, BLK, D), BF),
        vm((BLK, D), F32),
        vm((8, D), F32),
        vm((3, 8, 128), F32),
        vm((3, 8, 128), F32),
        vm((16, D), F32),
        vm((5, 16, D), F32),
        vm((5, 16, D), F32),
        dma((4, 15)),
        dma((4, 8)),
        dma((6, 9)),
        dma((6, 9)),
        dma((5, 9)),
        dma((5, 9)),
        dma((3,)),
        dma((3,)),
        dma((3,)),
        dma((3,)),
        dma((3, 4)),
        dma((3, 4)),
        dma((3, 3)),
        dma((3, 3)),
        dma((5,)),
        dma((5,)),
        dma((10,)),
        dma((8,)),
        pltpu.SemaphoreType.REGULAR,
        pltpu.SemaphoreType.REGULAR,
        pltpu.SemaphoreType.REGULAR,
    ]
    ins = [any_] * 6 + [vm] * 2
    return pl.pallas_call(
        layer_kernel,
        out_shape=[jax.ShapeDtypeStruct(shape, dtype) for shape, dtype, _ in outs],
        in_specs=[pl.BlockSpec(memory_space=space) for space in ins],
        out_specs=[pl.BlockSpec(memory_space=space) for _, _, space in outs],
        scratch_shapes=scratch,
        compiler_params=pltpu.CompilerParams(
            collective_id=1, has_side_effects=True, vmem_limit_bytes=64 << 20
        ),
        name="layer",
    )(*operands)


def turn_tables():
    import ml_dtypes

    quarter = HD // 4
    frequency = (1.0 / np.float32(10000.0) ** (np.arange(quarter, dtype=np.float32) * 4.0 / HD)).astype(np.float32)
    angle = (np.arange(16, dtype=np.float32)[:, None] * frequency[None, :]).astype(np.float32)
    cosine, sine = np.cos(angle.astype(np.float64)), np.sin(angle.astype(np.float64))
    zero = np.zeros_like(cosine)

    def head(first, second):
        top = np.concatenate([first, zero, second, zero], axis=1)
        low = np.concatenate([zero, first, zero, second], axis=1)
        return np.tile(np.concatenate([top, low], axis=0), (1, 2 * HEADS_LOCAL))

    full = np.concatenate([head(cosine, cosine), head(-sine, zero), head(zero, sine)], axis=1).astype(np.float32)
    terms = []
    rest = full
    for _ in range(3):
        term = rest.astype(ml_dtypes.bfloat16)
        terms.append(term)
        rest = rest - term.astype(np.float32)
    terms.append(np.zeros((32, full.shape[1]), ml_dtypes.bfloat16))
    return jnp.asarray(np.concatenate(terms, axis=0))


def row_marks(picture, places, validity):
    spots = jnp.arange(16, dtype=jnp.int32)
    row_spot = places[:, 0:1] == spots
    col_spot = places[:, 1:2] == spots
    pictures = picture.reshape(-1, ROW_PATCHES)
    change = (pictures[:, 1:] != pictures[:, :-1]).astype(BF)
    change = jnp.pad(change, ((0, 0), (1, 0)))
    upto = jnp.triu(jnp.ones((ROW_PATCHES, ROW_PATCHES), BF))
    rank = jnp.dot(change, upto, preferred_element_type=F32).reshape(-1, 1)
    ranks = rank == jnp.arange(8, dtype=F32)
    once = jnp.concatenate([row_spot, col_spot], axis=1)
    return jnp.concatenate(
        [once, once, once, ranks, (validity > 0)[:, None], jnp.zeros((picture.shape[0], 23), bool)], axis=1
    ).astype(BF)


def on_device_fast(
    tokens,
    teacher,
    picture,
    places,
    validity,
    first_gain,
    first_shift,
    mixer_weight,
    mixer_bias,
    output_weight,
    output_bias,
    second_gain,
    second_shift,
    upward_weight,
    upward_bias,
    downward_weight,
    downward_bias,
):
    member = lax.axis_index("fsdp")
    data_index = lax.axis_index("dp")
    data_ways = lax.axis_size("dp")
    TOTAL[0] = float(tokens.shape[0] * data_ways * lax.axis_size("fsdp"))
    marks = row_marks(picture, places, validity)
    vectors = (first_gain, first_shift, output_bias, second_gain, second_shift, downward_bias)
    spots = jnp.zeros((6, D), F32)
    spots = lax.dynamic_update_slice(spots, jnp.stack(vectors).astype(F32), (0, BLK * data_index))
    up_all = lax.dynamic_update_slice(jnp.zeros((FF,), F32), upward_bias.astype(F32), (640 * data_index,))
    up_piece = lax.dynamic_slice_in_dim(up_all.reshape(4, F), member, 1, 0)
    mix_all = lax.dynamic_update_slice(jnp.zeros((3 * D,), F32), mixer_bias.astype(F32), (480 * data_index,))
    mix_piece = lax.dynamic_slice_in_dim(mix_all.reshape(3, 4, W), member, 1, 1).reshape(1, 3 * W)
    sv = jnp.concatenate([spots, up_piece, jnp.pad(mix_piece, ((0, 0), (0, D - 3 * W)))], axis=0)
    wa = jnp.concatenate([mixer_weight.reshape(BLK, 3 * W), output_weight.T], axis=1)
    tabs = turn_tables()
    res, gtok, gw, small, loss, _ = layer_call(
        tokens, teacher, marks, wa, upward_weight, downward_weight.T, sv, tabs
    )
    pieces = [own_slice(small[i], data_index, data_ways) for i in range(6)]
    up_bias = own_slice(small[8:12].reshape(FF), data_index, data_ways)
    mixed = small[12:16, : 3 * W].reshape(4, 3, W).transpose(1, 0, 2).reshape(3 * D)
    return (
        res,
        loss.reshape(()),
        gtok,
        pieces[0],
        pieces[1],
        gw[0, :, : 3 * W].reshape(BLK, 3, W),
        own_slice(mixed[: 2 * D], data_index, data_ways),
        own_slice(mixed[2 * D :], data_index, data_ways),
        gw[0, :, 3 * W :].T,
        pieces[2],
        pieces[3],
        pieces[4],
        gw[1],
        up_bias,
        gw[2].T,
        pieces[5],
    )


def solution(mesh):
    fast = mesh.shape["dp"] == 8 and mesh.shape["fsdp"] == 4
    return jax.shard_map(
        on_device_fast if fast else on_device,
        mesh=mesh,
        in_specs=(
            P(("dp", "fsdp"), None),
            P(("dp", "fsdp"), None),
            P(("dp", "fsdp")),
            P(("dp", "fsdp"), None),
            P(("dp", "fsdp")),
            P("dp"),
            P("dp"),
            P("dp", None, "fsdp"),
            P("dp"),
            P("fsdp", "dp"),
            P("dp"),
            P("dp"),
            P("dp"),
            P("dp", "fsdp"),
            P("dp"),
            P("fsdp", "dp"),
            P("dp"),
        ),
        out_specs=(
            P(("dp", "fsdp"), None),
            P(),
            P(("dp", "fsdp"), None),
            P("dp"),
            P("dp"),
            P("dp", None, "fsdp"),
            P("dp"),
            P("dp"),
            P("fsdp", "dp"),
            P("dp"),
            P("dp"),
            P("dp"),
            P("dp", "fsdp"),
            P("dp"),
            P("fsdp", "dp"),
            P("dp"),
        ),
        check_vma=False,
    )
```

```python
import numpy as np
import jax
import jax.numpy as jnp
from jax import lax
from jax.experimental import pallas as pl
from jax.experimental.pallas import tpu as pltpu
from jax.sharding import PartitionSpec as P

D = 1280
HD = 80
FF = 5120
ROW_PATCHES = 128
MB = 3


EPSILON = 1e-06


def norm_forward(values, scaler, offset):
    average = jnp.mean(values, axis=-1, keepdims=True)
    centered = values - average
    reciprocal = lax.rsqrt(jnp.mean(centered * centered, axis=-1, keepdims=True) + EPSILON)
    normed = centered * reciprocal
    return (normed * scaler.astype(jnp.float32) + offset.astype(jnp.float32), normed, reciprocal)


def norm_backward(gradient, normed, reciprocal, scaler):
    scaled = gradient * scaler.astype(jnp.float32)
    adjusted = (
        scaled
        - jnp.mean(scaled, axis=-1, keepdims=True)
        - normed * jnp.mean(scaled * normed, axis=-1, keepdims=True)
    )
    return (adjusted * reciprocal, jnp.sum(gradient * normed, axis=0), jnp.sum(gradient, axis=0))


def tables(places):
    quarter = HD // 4
    frequency = 1.0 / 10000.0 ** (jnp.arange(quarter, dtype=jnp.float32) * 4.0 / HD)
    row_angle = places[:, 0:1].astype(jnp.float32) * frequency
    col_angle = places[:, 1:2].astype(jnp.float32) * frequency
    angle_all = jnp.concatenate([row_angle, col_angle, row_angle, col_angle], axis=-1)
    return (jnp.cos(angle_all)[:, None, :], jnp.sin(angle_all)[:, None, :])


def rotate(values, cosine, sine):
    halfway = HD // 2
    flipped = jnp.concatenate([-values[..., halfway:], values[..., :halfway]], axis=-1)
    return values * cosine + flipped * sine


def unrotate(gradient, cosine, sine):
    halfway = HD // 2
    shifted = gradient * sine
    return gradient * cosine + jnp.concatenate(
        [shifted[..., halfway:], -shifted[..., :halfway]], axis=-1
    )


def allowed_mask(picture, validity):
    picture_rows = picture.reshape(-1, ROW_PATCHES)
    occupancy_flags = validity.reshape(-1, ROW_PATCHES) > 0
    shared_picture_mask = picture_rows[:, :, None] == picture_rows[:, None, :]
    self_pairs = jnp.eye(ROW_PATCHES, dtype=bool)[None]
    return (shared_picture_mask & occupancy_flags[:, None, :] | self_pairs)[:, None]


def scores_of(query, key_rows, permitted_pairs):
    products = jnp.einsum(
        "bqhd,bkhd->bhqk", query, key_rows, preferred_element_type=jnp.float32
    ) * HD ** (-0.5)
    return jnp.where(permitted_pairs, products, -1e30)


def attend(query, key_rows, value_rows, permitted_pairs):
    scores = scores_of(query, key_rows, permitted_pairs)
    maximum = jnp.max(scores, axis=-1, keepdims=True)
    log_total = maximum + jnp.log(jnp.sum(jnp.exp(scores - maximum), axis=-1, keepdims=True))
    probs = jnp.exp(scores - log_total).astype(jnp.bfloat16)
    attended = jnp.einsum("bhqk,bkhd->bqhd", probs, value_rows, preferred_element_type=jnp.float32)
    return (attended, log_total)


def attend_back(grad_attended, query, key_rows, value_rows, permitted_pairs, log_total):
    scores = scores_of(query, key_rows, permitted_pairs)
    probs = jnp.exp(scores - log_total)
    grad_probs = jnp.einsum(
        "bqhd,bkhd->bhqk", grad_attended, value_rows, preferred_element_type=jnp.float32
    )
    delta = jnp.sum(grad_probs * probs, axis=-1, keepdims=True)
    grad_scores = (probs * (grad_probs - delta)).astype(jnp.bfloat16)
    scaling = HD ** (-0.5)
    grad_query = (
        jnp.einsum("bhqk,bkhd->bqhd", grad_scores, key_rows, preferred_element_type=jnp.float32)
        * scaling
    )
    grad_key = (
        jnp.einsum("bhqk,bqhd->bkhd", grad_scores, query, preferred_element_type=jnp.float32)
        * scaling
    )
    grad_value = jnp.einsum(
        "bhqk,bqhd->bkhd",
        probs.astype(jnp.bfloat16),
        grad_attended,
        preferred_element_type=jnp.float32,
    )
    return (grad_query, grad_key, grad_value)


def quick_gelu_grad(grad_active, upper):
    sigmoid_up = jax.nn.sigmoid(1.702 * upper)
    return (grad_active * (sigmoid_up + 1.702 * upper * sigmoid_up * (1.0 - sigmoid_up))).astype(
        jnp.bfloat16
    )


def own_slice(vector, data_index, data_ways):
    length = vector.shape[0] // data_ways
    return lax.dynamic_slice_in_dim(vector, data_index * length, length, 0)


def on_device(
    tokens,
    teacher,
    picture,
    places,
    validity,
    first_gain,
    first_shift,
    mixer_weight,
    mixer_bias,
    output_weight,
    output_bias,
    second_gain,
    second_shift,
    upward_weight,
    upward_bias,
    downward_weight,
    downward_bias,
):
    data_ways = lax.axis_size("dp")
    split_ways = lax.axis_size("fsdp")
    member = lax.axis_index("fsdp")
    data_index = lax.axis_index("dp")
    occupancy_flags = validity.astype(jnp.float32)
    token_tally = lax.psum(jnp.sum(occupancy_flags), ("dp", "fsdp"))
    factor = tokens.shape[0] * data_ways * split_ways / token_tally
    (
        mixer_local,
        output_local,
        upward_local,
        downward_local,
        gain_one,
        shift_one,
        mixer_shift,
        output_shift,
        gain_two,
        shift_two,
        upward_shift,
        downward_shift,
    ) = (
        lax.all_gather(mixer_weight, "dp", axis=0, tiled=True),
        lax.all_gather(output_weight, "dp", axis=1, tiled=True),
        lax.all_gather(upward_weight, "dp", axis=0, tiled=True),
        lax.all_gather(downward_weight, "dp", axis=1, tiled=True),
        lax.all_gather(first_gain, "dp", axis=0, tiled=True),
        lax.all_gather(first_shift, "dp", axis=0, tiled=True),
        lax.all_gather(mixer_bias, "dp", axis=0, tiled=True),
        lax.all_gather(output_bias, "dp", axis=0, tiled=True),
        lax.all_gather(second_gain, "dp", axis=0, tiled=True),
        lax.all_gather(second_shift, "dp", axis=0, tiled=True),
        lax.all_gather(upward_bias, "dp", axis=0, tiled=True),
        lax.all_gather(downward_bias, "dp", axis=0, tiled=True),
    )
    width_local = output_local.shape[0]
    heads_local = width_local // HD
    hidden_local = upward_local.shape[1]
    mixer_flat = mixer_local.reshape(D, 3 * width_local)
    mixer_piece = lax.dynamic_slice_in_dim(
        mixer_shift.reshape(3, D), member * width_local, width_local, 1
    )
    mixer_piece = mixer_piece.reshape(3 * width_local).astype(jnp.float32)
    upward_piece = lax.dynamic_slice_in_dim(
        upward_shift, member * hidden_local, hidden_local, 0
    ).astype(jnp.float32)
    packed_rows = tokens.shape[0] // MB
    errors = jnp.zeros((), jnp.float32)
    matrix_sums = None
    small_sums = None
    results = []
    input_grads = []
    for micro in range(MB):
        start_offset = micro * packed_rows
        inputs = tokens[start_offset : start_offset + packed_rows].astype(jnp.float32)
        target = teacher[start_offset : start_offset + packed_rows].astype(jnp.float32)
        occupied_rows = occupancy_flags[start_offset : start_offset + packed_rows]
        picture_rows = picture[start_offset : start_offset + packed_rows]
        local_picture = (picture_rows - picture_rows[0]).astype(jnp.bfloat16)
        place_rows = places[start_offset : start_offset + packed_rows].astype(jnp.bfloat16)
        live_marks = validity[start_offset : start_offset + packed_rows].astype(jnp.bfloat16)
        shifted_one, normed_one, recip_one = norm_forward(inputs, gain_one, shift_one)
        lowered_one = shifted_one.astype(jnp.bfloat16)
        group_one, group_picture, group_places, group_live = (
            lax.all_gather(lowered_one, "fsdp", axis=0, tiled=True),
            lax.all_gather(local_picture, "fsdp", axis=0, tiled=True),
            lax.all_gather(place_rows, "fsdp", axis=0, tiled=True),
            lax.all_gather(live_marks, "fsdp", axis=0, tiled=True),
        )
        group_rows = group_one.shape[0]
        mixed = jnp.dot(group_one, mixer_flat, preferred_element_type=jnp.float32) + mixer_piece
        mixed = mixed.reshape(group_rows, 3, heads_local, HD)
        cosine, sine = tables(group_places)
        query = (
            rotate(mixed[:, 0], cosine, sine)
            .astype(jnp.bfloat16)
            .reshape(-1, ROW_PATCHES, heads_local, HD)
        )
        key_rows = (
            rotate(mixed[:, 1], cosine, sine)
            .astype(jnp.bfloat16)
            .reshape(-1, ROW_PATCHES, heads_local, HD)
        )
        value_rows = mixed[:, 2].astype(jnp.bfloat16).reshape(-1, ROW_PATCHES, heads_local, HD)
        permitted_pairs = allowed_mask(group_picture, group_live)
        attended, log_total = attend(query, key_rows, value_rows, permitted_pairs)
        attended = attended.reshape(group_rows, width_local).astype(jnp.bfloat16)
        branch = lax.psum_scatter(
            jnp.dot(attended, output_local, preferred_element_type=jnp.float32).astype(
                jnp.bfloat16
            ),
            "fsdp",
            scatter_dimension=0,
            tiled=True,
        ).astype(jnp.float32)
        middle = inputs + branch + output_shift.astype(jnp.float32)
        shifted_two, normed_two, recip_two = norm_forward(middle, gain_two, shift_two)
        lowered_two = shifted_two.astype(jnp.bfloat16)
        group_two = lax.all_gather(lowered_two, "fsdp", axis=0, tiled=True)
        upper = jnp.dot(group_two, upward_local, preferred_element_type=jnp.float32) + upward_piece
        active = (upper * jax.nn.sigmoid(1.702 * upper)).astype(jnp.bfloat16)
        lowered = lax.psum_scatter(
            jnp.dot(active, downward_local, preferred_element_type=jnp.float32).astype(
                jnp.bfloat16
            ),
            "fsdp",
            scatter_dimension=0,
            tiled=True,
        ).astype(jnp.float32)
        outputs = middle + lowered + downward_shift.astype(jnp.float32)
        difference = outputs - target
        masked = occupied_rows[:, None] * difference
        errors = errors + jnp.sum(masked * difference)
        grad_out = 2.0 * factor * masked
        grad_low = grad_out.astype(jnp.bfloat16)
        down_bias_term = jnp.sum(grad_low.astype(jnp.float32), axis=0)
        group_grad = lax.all_gather(grad_low, "fsdp", axis=0, tiled=True)
        g_down = jnp.einsum("rf,rd->fd", active, group_grad, preferred_element_type=jnp.float32)
        grad_active = jnp.einsum(
            "rd,fd->rf", group_grad, downward_local, preferred_element_type=jnp.float32
        )
        grad_upper = quick_gelu_grad(grad_active, upper)
        g_up = jnp.einsum("rd,rf->df", group_two, grad_upper, preferred_element_type=jnp.float32)
        up_bias_term = lax.dynamic_update_slice_in_dim(
            jnp.zeros((FF,), jnp.float32),
            jnp.sum(grad_upper.astype(jnp.float32), axis=0),
            member * hidden_local,
            0,
        )
        grad_two = lax.psum_scatter(
            jnp.einsum(
                "rf,df->rd", grad_upper, upward_local, preferred_element_type=jnp.float32
            ).astype(jnp.bfloat16),
            "fsdp",
            scatter_dimension=0,
            tiled=True,
        ).astype(jnp.float32)
        back_two, g_gain_two, g_shift_two = norm_backward(grad_two, normed_two, recip_two, gain_two)
        grad_middle = grad_out + back_two
        grad_branch = grad_middle.astype(jnp.bfloat16)
        out_bias_term = jnp.sum(grad_branch.astype(jnp.float32), axis=0)
        group_branch = lax.all_gather(grad_branch, "fsdp", axis=0, tiled=True)
        g_output = jnp.einsum(
            "rd,re->de", attended, group_branch, preferred_element_type=jnp.float32
        )
        grad_attended = jnp.einsum(
            "re,de->rd", group_branch, output_local, preferred_element_type=jnp.float32
        )
        grad_attended = grad_attended.astype(jnp.bfloat16).reshape(-1, ROW_PATCHES, heads_local, HD)
        grad_query, grad_key, grad_value = attend_back(
            grad_attended, query, key_rows, value_rows, permitted_pairs, log_total
        )
        grad_mixed = jnp.stack(
            [
                unrotate(grad_query.reshape(group_rows, heads_local, HD), cosine, sine),
                unrotate(grad_key.reshape(group_rows, heads_local, HD), cosine, sine),
                grad_value.reshape(group_rows, heads_local, HD),
            ],
            axis=1,
        )
        grad_mixed = grad_mixed.reshape(group_rows, 3 * width_local).astype(jnp.bfloat16)
        g_mixer = jnp.einsum("rd,re->de", group_one, grad_mixed, preferred_element_type=jnp.float32)
        g_mixer = g_mixer.reshape(D, 3, width_local)
        mixer_bias_term = lax.dynamic_update_slice_in_dim(
            jnp.zeros((3, D), jnp.float32),
            jnp.sum(grad_mixed.astype(jnp.float32), axis=0).reshape(3, width_local),
            member * width_local,
            1,
        )
        mixer_bias_term = mixer_bias_term.reshape(3 * D)
        grad_one = lax.psum_scatter(
            jnp.einsum(
                "re,de->rd", grad_mixed, mixer_flat, preferred_element_type=jnp.float32
            ).astype(jnp.bfloat16),
            "fsdp",
            scatter_dimension=0,
            tiled=True,
        ).astype(jnp.float32)
        back_one, g_gain_one, g_shift_one = norm_backward(grad_one, normed_one, recip_one, gain_one)
        grad_inputs = grad_middle + back_one
        matrices = (g_mixer, g_output, g_up, g_down)
        smalls = (
            g_gain_one,
            g_shift_one,
            mixer_bias_term,
            out_bias_term,
            g_gain_two,
            g_shift_two,
            up_bias_term,
            down_bias_term,
        )
        matrix_sums = (
            matrices if matrix_sums is None else jax.tree.map(jnp.add, matrix_sums, matrices)
        )
        small_sums = smalls if small_sums is None else jax.tree.map(jnp.add, small_sums, smalls)
        results.append(outputs.astype(jnp.bfloat16))
        input_grads.append(grad_inputs)
    g_mixer_sum, g_output_sum, g_up_sum, g_down_sum = matrix_sums
    reduced = (
        lax.psum_scatter(
            g_mixer_sum.astype(jnp.bfloat16), "dp", scatter_dimension=0, tiled=True
        ).astype(jnp.float32),
        lax.psum_scatter(
            g_output_sum.astype(jnp.bfloat16), "dp", scatter_dimension=1, tiled=True
        ).astype(jnp.float32),
        lax.psum_scatter(
            g_up_sum.astype(jnp.bfloat16), "dp", scatter_dimension=0, tiled=True
        ).astype(jnp.float32),
        lax.psum_scatter(
            g_down_sum.astype(jnp.bfloat16), "dp", scatter_dimension=1, tiled=True
        ).astype(jnp.float32),
    )
    totals = lax.psum(
        (
            small_sums[0],
            small_sums[1],
            small_sums[2],
            small_sums[3],
            small_sums[4],
            small_sums[5],
            small_sums[6],
            small_sums[7],
            errors,
        ),
        ("dp", "fsdp"),
    )
    pieces = [own_slice(totals[index], data_index, data_ways) for index in range(8)]
    query_key_piece = own_slice(totals[2][: 2 * D], data_index, data_ways)
    value_piece = own_slice(totals[2][2 * D :], data_index, data_ways)
    loss = totals[8] / (token_tally * D)
    return (
        jnp.concatenate(results, axis=0),
        loss,
        jnp.concatenate(input_grads, axis=0),
        pieces[0],
        pieces[1],
        reduced[0],
        query_key_piece,
        value_piece,
        reduced[1],
        pieces[3],
        pieces[4],
        pieces[5],
        reduced[2],
        pieces[6],
        reduced[3],
        pieces[7],
    )


BF = jnp.bfloat16
F32 = jnp.float32
HEADS_LOCAL = 4
W = 320
F = 1280
R = 384
G = 1536
BLK = 160
SUB = 128
QUAD = 512
HALF = 640
MESH_ID = pl.DeviceIdType.MESH


def _nn(a, b):
    return lax.dot_general(a, b, (((1,), (0,)), ((), ())), preferred_element_type=F32)


def _nt(a, b):
    return lax.dot_general(a, b, (((1,), (1,)), ((), ())), preferred_element_type=F32)


def _tn(a, b):
    return lax.dot_general(a, b, (((0,), (0,)), ((), ())), preferred_element_type=F32)


def _ds(start, size, step):
    if isinstance(start, int):
        return pl.ds(start, size)
    return pl.ds(pl.multiple_of(start, step), size)


class Place:
    def __init__(self):
        dp = lax.axis_index("dp")
        fs = lax.axis_index("fsdp")
        z, x = lax.div(dp, 2), lax.rem(dp, 2)
        y, c = lax.div(fs, 2), lax.rem(fs, 2)
        self.z, self.x, self.fs, self.dp = z, x, fs, dp
        self.core = (dp, 2 * y + 1 - c)
        self.ynb = (dp, 2 * (1 - y) + c)
        self.diagonal = (dp, 2 * (1 - y) + 1 - c)
        self.mates = (2 * y + 1 - c, 2 * (1 - y) + c, 2 * (1 - y) + 1 - c)
        self.xnb = (2 * z + 1 - x, fs)
        self.zs = (z, z + 1 - 2 * lax.rem(z, 2), lax.rem(z + 2, 4), 3 - z)
        self.zn = tuple((2 * zk + x, fs) for zk in self.zs)
        self.up = (2 * jnp.minimum(z + 1, 3) + x, fs)
        self.down = (2 * jnp.maximum(z - 1, 0) + x, fs)
        self.near = lax.div(z, 2)
        self.far = 1 - self.near

    def barrier(self):
        sem = pltpu.get_barrier_semaphore()
        for peer in (self.core, self.ynb, self.diagonal, self.xnb) + self.zn[1:]:
            pl.semaphore_signal(sem, inc=1, device_id=peer, device_id_type=MESH_ID)
        pl.semaphore_wait(sem, 7)


def _send(src, dst, ss, rs, peer):
    return pltpu.make_async_remote_copy(
        src_ref=src, dst_ref=dst, send_sem=ss, recv_sem=rs, device_id=peer, device_id_type=MESH_ID
    )


class Gather:
    def __init__(self, place, buf, ss, rs, cols=slice(None)):
        self.place, self.buf, self.ss, self.rs, self.cols = place, buf, ss, rs, cols

    def part(self, s, slot):
        return self.buf.at[_ds(QUAD * s + SUB * slot, SUB, SUB), self.cols]

    def to_core(self, s):
        return _send(self.part(s, 0), self.part(s, 1), self.ss.at[s], self.rs.at[s], self.place.core)

    def to_y(self, s):
        return _send(self.part(s, 0), self.part(s, 2), self.ss.at[3 + s], self.rs.at[3 + s], self.place.ynb)

    def on(self, s):
        return _send(self.part(s, 2), self.part(s, 3), self.ss.at[6 + s], self.rs.at[6 + s], self.place.core)

    def start(self, s):
        self.to_y(s).start()
        self.to_core(s).start()

    def pass_on(self, s):
        self.to_y(s).wait_recv()
        self.on(s).start()

    def ready(self, s):
        self.to_core(s).wait_recv()
        self.on(s).wait_recv()

    def end(self):
        for s in range(3):
            self.to_core(s).wait_send()
            self.to_y(s).wait_send()
            self.on(s).wait_send()


class Scatter:
    def __init__(self, place, sb, rb, own, ss, rs, cols=slice(None)):
        self.place, self.sb, self.rb, self.own, self.ss, self.rs, self.cols = place, sb, rb, own, ss, rs, cols

    def copy(self, kind, s):
        peer = self.place.ynb if kind == 1 else self.place.core
        slot = 2 + s if kind == 1 else kind // 2
        return _send(
            self.sb.at[slot, :, self.cols],
            self.rb.at[kind, s, :, self.cols],
            self.ss.at[3 * kind + s],
            self.rs.at[3 * kind + s],
            peer,
        )

    def again(self, kind, s):
        if isinstance(s, int):
            if s > 0:
                self.copy(kind, s - 1).wait_send()
        else:
            pl.when(s > 0)(lambda: self.copy(kind, s - 1).wait_send())

    def post(self, s, lhs, rhs):
        rows = QUAD * s
        term = _nt(lhs(_ds(rows + 2 * SUB, 2 * SUB, SUB)), rhs())
        self.again(0, s)
        self.sb[0, :, self.cols] = term[SUB:].astype(BF)
        self.copy(0, s).start()
        mine = _nt(lhs(_ds(rows, 2 * SUB, SUB)), rhs())
        self.again(2, s)
        self.sb[1, :, self.cols] = mine[SUB:].astype(BF)
        self.copy(2, s).start()
        self.own[_ds(SUB * s, SUB, SUB), self.cols] = mine[:SUB]
        self.copy(0, s).wait_recv()
        self.sb[2 + s, :, self.cols] = (term[:SUB] + self.rb[0, s, :, self.cols].astype(F32)).astype(BF)
        self.copy(1, s).start()

    def wait(self, s):
        self.copy(2, s).wait_recv()
        self.copy(1, s).wait_recv()

    def total(self, s, i, step):
        sub = _ds(step * i, step, step)
        return self.own[_ds(SUB * s + step * i, step, step), self.cols] + (
            self.rb[2, s, sub, self.cols].astype(F32) + self.rb[1, s, sub, self.cols].astype(F32)
        )

    def end(self):
        self.copy(0, 2).wait_send()
        self.copy(2, 2).wait_send()
        for s in range(3):
            self.copy(1, s).wait_send()


def _norm(values):
    average = jnp.mean(values, axis=-1, keepdims=True)
    centered = values - average
    reciprocal = lax.rsqrt(jnp.mean(centered * centered, axis=-1, keepdims=True) + EPSILON)
    return centered * reciprocal, reciprocal


def _head_rows(lanes, offset):
    lane = lax.broadcasted_iota(jnp.int32, (1, lanes), 1) - offset
    return [
        jnp.where((lane >= HD * h) & (lane < HD * h + HD), 1.0, 0.0).astype(BF)
        for h in range(HEADS_LOCAL)
    ]


def _stack(values, heads):
    return jnp.concatenate([values * head for head in heads], axis=0)


def _allowed(auxb):
    lane = lax.broadcasted_iota(jnp.int32, (1, 128), 1)
    picks = (lane >= 96) & (lane < 104)
    left = jnp.where(picks, auxb.astype(F32), jnp.where(lane == 104, 1.0, 0.0)).astype(BF)
    score = _nt(left, auxb)
    here = lax.broadcasted_iota(jnp.int32, (128, 128), 0)
    there = lax.broadcasted_iota(jnp.int32, (128, 128), 1)
    return (score > 1.5) | (here == there)


def _softmax(scores, allowed):
    probs = []
    for h in range(HEADS_LOCAL):
        part = jnp.where(allowed, scores[:, 128 * h : 128 * h + 128], -1e30)
        grown = jnp.exp(part - jnp.max(part, axis=-1, keepdims=True))
        probs.append(grown * (1.0 / jnp.sum(grown, axis=-1, keepdims=True)))
    return probs


PIECES = ((0, 0, 1024), (0, 1024, 256), (1, 0, 1280), (2, 0, 1280))


def _spread(packed, place):
    dp, fs = place.dp, place.fs

    def wide(ref):
        size = ref.shape[0]
        return jnp.concatenate([ref[...].astype(F32).reshape(1, size), jnp.zeros((1, D - size), F32)], axis=1)

    rows = jnp.concatenate([wide(ref) for ref in packed[:6]], axis=0)
    rows = pltpu.roll(rows, BLK * dp, 1)
    up = pltpu.roll(wide(packed[6]), 640 * lax.rem(dp, 2), 1)
    up = up * jnp.where(lax.div(dp, 2) == fs, 1.0, 0.0)
    mixed = wide(packed[7])
    lane = lax.broadcasted_iota(jnp.int32, (1, D), 1)
    row = jnp.zeros((1, D), F32)
    for t in range(3):
        shift = 480 * dp - 960 * t - W * fs
        turned = pltpu.roll(mixed, lax.rem(shift + 4 * D, D), 1)
        mine = (lane >= W * t) & (lane < W * t + W) & (lane >= shift) & (lane < shift + 480)
        row = row + jnp.where(mine, turned, 0.0)
    return jnp.concatenate([rows, up, row], axis=0)


def _marks(pictures, spots, real, s):
    lane = lax.broadcasted_iota(jnp.int32, (3, SUB), 1)
    change = jnp.where((pictures != pltpu.roll(pictures, 1, 1)) & (lane > 0), 1.0, 0.0).astype(BF)
    here = lax.broadcasted_iota(jnp.int32, (SUB, SUB), 0)
    there = lax.broadcasted_iota(jnp.int32, (SUB, SUB), 1)
    upto = jnp.where(here <= there, 1.0, 0.0).astype(BF)
    rank = _nn(change, upto)[s : s + 1, :].astype(jnp.int32)
    spot = lax.rem(here, 32)
    row = (spot < 16) & (spot == spots[0:1, SUB * s : SUB * s + SUB])
    col = (spot >= 16) & (spot - 16 == spots[1:2, SUB * s : SUB * s + SUB])
    once = (here < 96) & (row | col)
    picture = (here >= 96) & (here < 104) & (here - 96 == rank)
    live = (here == 104) & (real[s : s + 1, :] > 0)
    return jnp.where(once | picture | live, 1.0, 0.0).T.astype(BF)


def layer_kernel(
    tok_h, teach_h, mix_h, out_h, wu_h, wd_h, v0, v1, v2, v3, v4, v5, v6, v7, pictures, spots, real, tabs,
    res_h, gtok_h, gd_h, gu_h, ga_h, small_o, loss_o, keep_h,
    tok, aux, w, wo, n1a, n2, gu, gzb, qk, v, o, acc, own, mid, gy, sb, rb,
    gb, xin, zin, fin, vecs, small, ccz, ccx, sta, stx, stz,
    ws, wr, ags, agr, rss, rsr, xs, xr, zs, zr, as_, ar, bs, br, ls, os_, xfree, zfree, gfree,
):
    place = Place()
    z, x = place.z, place.x
    patches = TOTAL[0]
    mine = _ds(BLK * (2 * z + x), BLK, 32)
    loads = [
        pltpu.make_async_copy(src, dst, ls.at[i])
        for i, (src, dst) in enumerate(
            [(mix_h.at[t], o.at[pl.ds(BLK * t, BLK), :]) for t in range(3)]
            + [(out_h, o.at[pl.ds(3 * BLK, BLK), :]), (tok_h, tok)]
            + [(wu_h, w.at[1, mine, :]), (wd_h, w.at[2, mine, :])]
        )
    ]
    for copy in loads:
        copy.start()
    stz[z, :8, :] = _spread((v0, v1, v2, v3, v4, v5, v6, v7), place)
    place.barrier()

    def over_z(buf, rows, kind):
        there = buf.at[z, rows, :]
        return [_send(there, there, as_.at[kind, k], ar.at[kind, z], place.zn[k]) for k in (1, 2, 3)]

    def from_z(buf, rows, kind):
        for k in (1, 2, 3):
            there = buf.at[place.zs[k], rows, :]
            _send(there, there, as_.at[kind, k], ar.at[kind, place.zs[k]], place.zn[k]).wait_recv()

    def swap_x(buf, rows, kind):
        return _send(buf.at[0, rows, :], buf.at[1, rows, :], bs.at[kind], br.at[kind], place.xnb)

    first8 = pl.ds(0, 8)
    vector_z = over_z(stz, first8, 0)
    for copy in vector_z:
        copy.start()

    shards = (None, wu_h, wd_h)

    def at(piece, zk, xk):
        third, start, size = PIECES[piece]
        return w.at[third, _ds(BLK * (2 * zk + xk), BLK, 32), pl.ds(start, size)]

    def shard(piece):
        third, start, size = PIECES[piece]
        if third == 0:
            return at(piece, z, x)
        return shards[third].at[:, pl.ds(start, size)]

    def first(piece, i):
        peer = (place.xnb, place.up, place.down)[i]
        return _send(shard(piece), at(piece, z, x), ws.at[piece, i], wr.at[piece, 2 * z + x], peer)

    def begin_z(piece):
        pl.when(z < 3)(lambda: first(piece, 1).start())
        pl.when(z > 0)(lambda: first(piece, 2).start())

    def begin_x(piece):
        first(piece, 0).start()

    def hop(piece, d, i):
        zk = jnp.maximum(z - d, 0) if i < 2 else jnp.minimum(z + d, 3)
        peer = (place.up, place.xnb, place.down, place.xnb)[i]
        there = at(piece, zk, x)
        return _send(there, there, ws.at[piece, 4 * d - 1 + i], wr.at[piece, 2 * zk + x], peer)

    def relay(piece, d):
        @pl.when(z >= d)
        def _():
            hop(piece, d, 0).wait_recv()
            pl.when(z < 3)(lambda: hop(piece, d, 0).start())
            hop(piece, d, 1).start()

        @pl.when(z + d <= 3)
        def _():
            hop(piece, d, 2).wait_recv()
            pl.when(z > 0)(lambda: hop(piece, d, 2).start())
            hop(piece, d, 3).start()

    def over_x(piece, zk):
        there = at(piece, zk, 1 - x)
        _send(there, there, ws.at[piece, 0], wr.at[piece, 2 * zk + 1 - x], place.xnb).wait_recv()

    def complete(piece):
        for k in range(4):
            over_x(piece, place.zs[k])

    def sent(piece):
        first(piece, 0).wait_send()
        pl.when(z < 3)(lambda: first(piece, 1).wait_send())
        pl.when(z > 0)(lambda: first(piece, 2).wait_send())
        for d in range(1, 4):

            @pl.when(z >= d)
            def _(d=d):
                pl.when(z < 3)(lambda: hop(piece, d, 0).wait_send())
                hop(piece, d, 1).wait_send()

            @pl.when(z + d <= 3)
            def _(d=d):
                pl.when(z > 0)(lambda: hop(piece, d, 2).wait_send())
                hop(piece, d, 3).wait_send()

    outs = []

    def out(src, dst):
        copy = pltpu.make_async_copy(src, dst, os_.at[len(outs)])
        copy.start()
        outs.append(copy)
        return len(outs) - 1

    for copy in loads[:4]:
        copy.wait()
    w[0, mine, :] = jnp.concatenate([o[pl.ds(BLK * t, BLK), :] for t in range(4)], axis=1)
    begin_z(0)
    agx = Gather(place, aux, ags.at[1], agr.at[1])
    for s in range(3):
        aux[pl.ds(QUAD * s, SUB), :] = _marks(pictures[...], spots[...], real[...], s)
        agx.start(s)
    loads[4].wait()

    def first_norm(i, _):
        rows = _ds(32 * i, 32, 32)
        own[rows, :] = _norm(tok[rows, :].astype(F32))[0]
        return 0

    lax.fori_loop(0, R // 32, first_norm, 0)
    from_z(stz, first8, 0)
    stx[0, :8, :] = (stz[0, :8, :] + stz[1, :8, :]) + (stz[2, :8, :] + stz[3, :8, :])
    vector_x = swap_x(stx, first8, 0)
    vector_x.start()
    begin_x(0)
    vector_x.wait_recv()
    vecs[...] = stx[0, :8, :] + stx[1, :8, :]
    ag1 = Gather(place, n1a, ags.at[0], agr.at[0])
    for s in range(3):

        def scale_rows(i, _, s=s):
            rows = _ds(QUAD * s + 32 * i, 32, 32)
            n1a[rows, :] = (own[_ds(SUB * s + 32 * i, 32, 32), :] * vecs[0:1, :] + vecs[1:2, :]).astype(BF)
            return 0

        lax.fori_loop(0, 4, scale_rows, 0)
        ag1.start(s)
    relay(0, 1)
    for s in range(3):
        agx.pass_on(s)
    relay(0, 2)
    begin_z(1)
    ag1.pass_on(0)
    relay(0, 3)
    begin_x(1)
    for s in range(3):
        agx.ready(s)
    whole = slice(None)
    count_z = over_z(ccz, whole, 1)
    count_x = swap_x(ccx, whole, 1)
    complete(0)
    for copy in vector_z + [vector_x]:
        copy.wait_send()

    side = _head_rows(W, 0)
    rs1 = Scatter(place, sb, rb, own, rss.at[0], rsr.at[0])

    def attend_part(s, _):
        ag1.ready(s)
        acc[:, : 3 * W] = _nn(n1a[_ds(QUAD * s, QUAD, QUAD), :], w[0, :, : 3 * W]) + vecs[7:8, : 3 * W]

        def attend_rows(i, _):
            here = _ds(SUB * i, SUB, SUB)
            rows = _ds(QUAD * s + SUB * i, SUB, SUB)
            auxb = aux[rows, :]
            angle = _nn(auxb, tabs[...])
            raw = acc[here, : 2 * W]
            turned = (
                raw * angle[:, : 2 * W]
                + pltpu.roll(raw, 2 * W - 40, 1) * angle[:, 2 * W : 4 * W]
                + pltpu.roll(raw, 40, 1) * angle[:, 4 * W :]
            )
            qkb = turned.astype(BF)
            kqb = pltpu.roll(turned, W, 1)[:, :W].astype(BF)
            vb = acc[here, 2 * W : 3 * W].astype(BF)
            qk[rows, :] = qkb
            v[rows, :] = vb
            scores = _nt(qkb[:, :W], _stack(kqb, side)) * HD ** (-0.5)
            probs = _softmax(scores, _allowed(auxb))
            flat = jnp.concatenate([p.astype(BF) for p in probs], axis=1)
            o[rows, :] = _nn(flat, _stack(vb, side)).astype(BF)

            @pl.when((s == 0) & (i == 0))
            def _():
                relay(1, 1)
                ag1.pass_on(1)

            @pl.when((s == 0) & (i == 1))
            def _():
                relay(1, 2)
                begin_z(2)

            @pl.when((s == 0) & (i == 2))
            def _():
                relay(1, 3)
                begin_x(2)

            return 0

        lax.fori_loop(0, 4, attend_rows, 0)

        @pl.when(s == 0)
        def _():
            complete(1)
            wo[...] = w[0, :, 3 * W :]
            ag1.pass_on(2)

        @pl.when(s == 1)
        def _():
            relay(2, 1)

        rs1.post(s, lambda rows: o[rows, :], lambda: wo[...])

        @pl.when(s == 0)
        def _():
            ccz[z] = _nn(jnp.ones((8, G), BF), aux[...])
            for copy in count_z:
                copy.start()

        @pl.when(s == 2)
        def _():
            relay(2, 2)
            begin_z(3)

        return 0

    lax.fori_loop(0, 3, attend_part, 0)
    n1_kept = out(n1a, keep_h)
    ag2 = Gather(place, n2, ags.at[2], agr.at[2])

    def second_norm(s, _):
        rs1.wait(s)

        def rows_of(i, _):
            rows = _ds(SUB * s + 32 * i, 32, 32)
            middle = tok[rows, :].astype(F32) + rs1.total(s, i, 32) + vecs[2:3, :]
            mid[rows, :] = middle
            normed, _r = _norm(middle)
            n2[_ds(QUAD * s + 32 * i, 32, 32), :] = (normed * vecs[3:4, :] + vecs[4:5, :]).astype(BF)
            return 0

        lax.fori_loop(0, 4, rows_of, 0)
        ag2.start(s)

        @pl.when(s == 0)
        def _():
            relay(2, 3)

        @pl.when(s == 1)
        def _():
            from_z(ccz, whole, 1)
            ccx[0] = (ccz[0] + ccz[1]) + (ccz[2] + ccz[3])
            count_x.start()
            begin_x(3)

        return 0

    lax.fori_loop(0, 3, second_norm, 0)
    teach = tok
    teach_load = pltpu.make_async_copy(teach_h, teach, ls.at[7])
    teach_load.start()
    relay(3, 1)
    ag1.end()
    outs[n1_kept].wait()
    loads[5].wait()
    complete(2)

    relay(3, 2)

    def up_part(s, _):
        pl.when(s == 1)(lambda: relay(3, 3))
        ag2.pass_on(s)
        ag2.ready(s)
        acc[...] = _nn(n2[_ds(QUAD * s, QUAD, QUAD), :], w[1]) + vecs[6:7, :]

        def rows_of(i, _):
            upper = acc[_ds(32 * i, 32, 32), :]
            rows = _ds(QUAD * s + 32 * i, 32, 32)
            gate = 1.0 / (1.0 + jnp.exp(-1.702 * upper))
            n1a[rows, :] = (upper * gate).astype(BF)
            gu[rows, :] = (gate + 1.702 * upper * gate * (1.0 - gate)).astype(BF)
            return 0

        lax.fori_loop(0, QUAD // 32, rows_of, 0)
        return 0

    lax.fori_loop(0, 3, up_part, 0)
    act = n1a
    rs1.end()
    loads[6].wait()
    teach_load.wait()

    cols = {0: _ds(HALF * place.near, HALF, 128), 1: _ds(HALF * place.far, HALF, 128)}
    count_x.wait_recv()
    real_count = (ccx[0] + ccx[1])[0:1, 104:105]
    factor = 2.0 * patches / real_count
    downs = [Scatter(place, sb, rb, own, rss.at[1 + j], rsr.at[1 + j], cols[j]) for j in range(2)]
    gathers = [Gather(place, gzb, ags.at[3 + j], agr.at[3 + j], cols[j]) for j in range(2)]
    small[...] = jnp.zeros_like(small)

    for j in range(2):
        for k in ((0, 1), (2, 3))[j]:
            over_x(3, place.zs[k])
        half = (place.near, place.far)[j]

        def down_part(s, _, j=j, half=half):
            downs[j].post(s, lambda rows: act[rows, :], lambda: w[2, _ds(HALF * half, HALF, 128), :])
            return 0

        lax.fori_loop(0, 3, down_part, 0)

        def finish_part(s, sums, j=j):
            downs[j].wait(s)

            def rows_of(i, sums):
                rows = _ds(SUB * s + 32 * i, 32, 32)
                result = mid[rows, cols[j]] + downs[j].total(s, i, 32) + vecs[5:6, cols[j]]
                real = aux[_ds(QUAD * s + 32 * i, 32, 32), 104:105].astype(F32)
                difference = result - teach[rows, cols[j]].astype(F32)
                masked = real * difference
                gout = factor * masked
                low = gout.astype(BF)
                gy[rows, cols[j]] = gout
                teach[rows, cols[j]] = result.astype(BF)
                gzb[_ds(QUAD * s + 32 * i, 32, 32), cols[j]] = low
                return (
                    sums[0] + jnp.sum(masked * difference, axis=0, keepdims=True),
                    sums[1] + jnp.sum(low.astype(F32), axis=0, keepdims=True),
                )

            sums = lax.fori_loop(0, 4, rows_of, sums)
            gathers[j].start(s)
            if j == 1:
                gathers[0].pass_on(s)
            return sums

        zero = jnp.zeros((1, HALF), F32)
        sums = lax.fori_loop(0, 3, finish_part, (zero, zero))
        small[6:7, cols[j]] = sums[0]
        small[5:6, cols[j]] = sums[1]
    res_out = out(teach, res_h)

    def to_x(chunk, slot, k):
        rows = _ds(BLK * (2 * place.zs[k] + 1 - x), BLK, 32)
        return _send(gb.at[slot, rows, :], xin.at[slot, k], xs.at[chunk, k], xr.at[chunk, k], place.xnb)

    def block(k):
        return _ds(BLK * (2 * place.zs[k] + x), BLK, 32)

    def to_z(chunk, slot, i):
        k, peer = ((3, place.zn[1]), (1, place.zn[1]), (2, place.zn[2]))[i]
        return _send(gb.at[slot, block(k), :], zin.at[slot, i], zs.at[chunk, i], zr.at[chunk, i], peer)

    def tile(slot, lhs, rhs, half):
        rows = _ds(HALF * half, HALF, 128)
        for part in range(2):
            cols = pl.ds(HALF * part, HALF)
            gb[slot, rows, cols] = _tn(lhs[:, rows], rhs[:, cols]).astype(BF)

    def add_x(chunk, slot, i):
        k = (3, 1)[i]
        to_x(chunk, slot, k).wait_recv()
        gb[slot, block(k), :] = (gb[slot, block(k), :].astype(F32) + xin[slot, k].astype(F32)).astype(BF)
        to_z(chunk, slot, i).start()

    def combine(chunk, slot):
        to_x(chunk, slot, 2).wait_recv()
        to_z(chunk, slot, 0).wait_recv()
        gb[slot, block(2), :] = (
            (gb[slot, block(2), :].astype(F32) + xin[slot, 2].astype(F32)) + zin[slot, 0].astype(F32)
        ).astype(BF)
        to_z(chunk, slot, 2).start()

    def add_own(chunk, slot):
        to_x(chunk, slot, 0).wait_recv()
        fin[...] = gb[slot, block(0), :].astype(F32) + xin[slot, 0].astype(F32)

    def add_z(chunk, slot, dst):
        to_z(chunk, slot, 1).wait_recv()
        to_z(chunk, slot, 2).wait_recv()
        fin[...] = fin[...] + (zin[slot, 1].astype(F32) + zin[slot, 2].astype(F32))
        return out(fin, dst)

    for s in range(3):
        gathers[0].ready(s)
    tile(0, gzb, act, place.near)
    to_x(2, 0, 1).start()
    to_x(2, 0, 0).start()

    for copy in downs:
        copy.end()
    rs3 = Scatter(place, sb, rb, own, rss.at[3], rsr.at[3])
    up_total = jnp.zeros((1, F), F32)
    for s in range(3):
        gathers[1].pass_on(s)
    gathers[1].ready(0)
    for s in range(3):
        acc[...] = _nn(gzb[pl.ds(QUAD * s, QUAD), :], w[2])

        def gate_rows(i, total, s=s):
            rows = _ds(QUAD * s + 32 * i, 32, 32)
            low = (acc[_ds(32 * i, 32, 32), :] * gu[rows, :].astype(F32)).astype(BF)
            gu[rows, :] = low
            return total + jnp.sum(low.astype(F32), axis=0, keepdims=True)

        up_total = lax.fori_loop(0, QUAD // 32, gate_rows, up_total)
        rs3.post(s, lambda rows: gu[rows, :], lambda: w[1])
        if s == 0:
            for t in (1, 2):
                gathers[1].ready(t)
            tile(0, gzb, act, place.far)
            to_x(2, 0, 3).start()
            to_x(2, 0, 2).start()
        if s == 1:
            add_x(2, 0, 1)
    for gather in gathers:
        gather.end()
    for peer in (place.core, place.ynb):
        pl.semaphore_signal(gfree, inc=1, device_id=peer, device_id_type=MESH_ID)
    n1_back = pltpu.make_async_copy(keep_h, n1a, ls.at[8])
    n1_back.start()
    outs[res_out].wait()
    tok_back = pltpu.make_async_copy(tok_h, tok, ls.at[9])
    tok_back.start()
    small[pl.ds(8 + place.fs, 1), :] = up_total
    tile(1, n2, gu, place.far)
    to_x(1, 1, 3).start()
    to_x(1, 1, 2).start()
    pl.semaphore_wait(gfree, 2)
    ag3 = Gather(place, gzb, ags.at[5], agr.at[5])

    def norm_rows(s, i, sums, values, gain, terms):
        rows = _ds(SUB * s + 32 * i, 32, 32)
        grad = terms.total(s, i, 32)
        normed, reciprocal = _norm(values[rows, :].astype(F32))
        scaled = grad * gain
        back = (
            scaled
            - jnp.mean(scaled, axis=-1, keepdims=True)
            - normed * jnp.mean(scaled * normed, axis=-1, keepdims=True)
        ) * reciprocal
        total = gy[rows, :] + back
        gy[rows, :] = total
        pair = (
            sums[0] + jnp.sum(grad * normed, axis=0, keepdims=True),
            sums[1] + jnp.sum(grad, axis=0, keepdims=True),
        )
        return total, pair

    zero = jnp.zeros((1, D), F32)

    def second_back(s, sums):
        rs3.wait(s)

        def rows_of(i, sums):
            total, pair = norm_rows(s, i, sums[:2], mid, vecs[3:4, :], rs3)
            low = total.astype(BF)
            gzb[_ds(QUAD * s + 32 * i, 32, 32), :] = low
            return pair + (sums[2] + jnp.sum(low.astype(F32), axis=0, keepdims=True),)

        sums = lax.fori_loop(0, 4, rows_of, sums)
        ag3.start(s)
        pl.when(s == 0)(lambda: add_x(2, 0, 0))
        return sums

    gain2, shift2, outb = lax.fori_loop(0, 3, second_back, (zero, zero, zero))
    small[2:3, :] = outb
    small[3:4, :] = gain2
    small[4:5, :] = shift2
    tile(1, n2, gu, place.near)
    to_x(1, 1, 1).start()
    to_x(1, 1, 0).start()
    combine(2, 0)
    add_own(2, 0)
    pl.semaphore_signal(xfree, inc=1, device_id=place.xnb, device_id_type=MESH_ID)
    rs3.end()
    rs4 = Scatter(place, sb, rb, own, rss.at[4], rsr.at[4])

    def attend_back(s, total):
        ag3.pass_on(s)
        ag3.ready(s)
        acc[:, :W] = _nn(gzb[_ds(QUAD * s, QUAD, QUAD), :], wo[...])

        def attend_rows(i, total):
            rows = _ds(QUAD * s + SUB * i, SUB, SUB)
            auxb = aux[rows, :]
            qkb = qk[rows, :]
            kqb = pltpu.roll(qkb.astype(F32), W, 1)[:, :W].astype(BF)
            vb = v[rows, :]
            gob = acc[_ds(SUB * i, SUB, SUB), :W].astype(BF)
            keys = _stack(kqb, side)
            scores = _nt(qkb[:, :W], keys) * HD ** (-0.5)
            probs = _softmax(scores, _allowed(auxb))
            gprobs = _nt(gob, _stack(vb, side))
            gscores = []
            for h in range(HEADS_LOCAL):
                gp = gprobs[:, 128 * h : 128 * h + 128]
                delta = jnp.sum(gp * probs[h], axis=-1, keepdims=True)
                gscores.append((probs[h] * (gp - delta)).astype(BF))
            flat = jnp.concatenate(gscores, axis=1)
            tall = jnp.concatenate(gscores, axis=0)
            ptall = jnp.concatenate([p.astype(BF) for p in probs], axis=0)
            gqk = jnp.concatenate([_nn(flat, keys), _tn(tall, _stack(qkb[:, :W], side))], axis=1) * HD ** (-0.5)
            gv = _tn(ptall, _stack(gob, side))
            angle = _nn(auxb, tabs[...])
            turned = (
                gqk * angle[:, : 2 * W]
                + pltpu.roll(gqk * angle[:, 4 * W :], 2 * W - 40, 1)
                + pltpu.roll(gqk * angle[:, 2 * W : 4 * W], 40, 1)
            )
            low = jnp.concatenate([turned, gv], axis=1).astype(BF)
            gu[rows, : 3 * W] = low
            return total + jnp.sum(low.astype(F32), axis=0, keepdims=True)

        total = lax.fori_loop(0, 4, attend_rows, total)
        rs4.post(s, lambda rows: gu[rows, : 3 * W], lambda: w[0, :, : 3 * W])

        pl.when(s == 0)(lambda: add_x(1, 1, 0))
        pl.when(s == 1)(lambda: combine(1, 1))
        pl.when(s == 2)(lambda: add_x(1, 1, 1))
        return total

    mix_total = lax.fori_loop(0, 3, attend_back, jnp.zeros((1, 3 * W), F32))
    small[pl.ds(12 + place.fs, 1), : 3 * W] = mix_total

    for k in range(4):
        to_x(2, 0, k).wait_send()
    for i in range(3):
        to_z(2, 0, i).wait_send()
    n1_back.wait()

    def last_tile(half):
        rows = _ds(HALF * half, HALF, 128)
        gb[0, rows, : 3 * W] = _tn(n1a[:, rows], gu[:, : 3 * W]).astype(BF)
        gb[0, rows, 3 * W :] = _tn(gzb[:, rows], o[...]).astype(BF)

    last_tile(place.far)
    pl.semaphore_wait(xfree, 1)
    to_x(0, 0, 3).start()
    to_x(0, 0, 2).start()
    last_tile(place.near)
    to_x(0, 0, 1).start()
    down_out = add_z(2, 0, gd_h)
    for peer in place.zn[1:3]:
        pl.semaphore_signal(zfree, inc=1, device_id=peer, device_id_type=MESH_ID)

    tok_back.wait()

    def first_back(s, sums):
        rs4.wait(s)

        @pl.when(s == 1)
        def _():
            pl.semaphore_wait(zfree, 2)
            add_x(0, 0, 0)

        return lax.fori_loop(0, 4, lambda i, t: norm_rows(s, i, t, tok, vecs[0:1, :], rs4)[1], sums)

    gain1, shift1 = lax.fori_loop(0, 3, first_back, (zero, zero))
    out(gy, gtok_h)
    small[0:1, :] = gain1
    small[1:2, :] = shift1

    sta[place.fs] = small[...]
    there = sta.at[place.fs]
    peers = (place.core, place.ynb, place.diagonal)
    small_f = [_send(there, there, as_.at[3, k], ar.at[3, place.fs], peer) for k, peer in enumerate(peers)]
    for copy in small_f:
        copy.start()
    outs[down_out].wait()
    for k, peer in enumerate(peers):
        there = sta.at[place.mates[k]]
        _send(there, there, as_.at[3, k], ar.at[3, place.mates[k]], peer).wait_recv()
    stx[0] = (sta[0] + sta[1]) + (sta[2] + sta[3])
    small_x = swap_x(stx, whole, 2)
    small_x.start()
    to_x(0, 0, 0).start()
    add_own(1, 1)
    combine(0, 0)
    up_out = add_z(1, 1, gu_h)
    add_x(0, 0, 1)
    small_x.wait_recv()
    stz[z] = stx[0] + stx[1]
    small_z = over_z(stz, whole, 2)
    for copy in small_z:
        copy.start()
    outs[up_out].wait()
    add_own(0, 0)
    from_z(stz, whole, 2)
    total = (stz[0] + stz[1]) + (stz[2] + stz[3])
    small_o[...] = total
    loss_o[...] = jnp.sum(total[6:7, :], axis=-1, keepdims=True) / (real_count * D)
    add_z(0, 0, ga_h)

    for piece in range(4):
        sent(piece)
    agx.end()
    ag2.end()
    ag3.end()
    rs4.end()
    for copy in count_z + [count_x] + small_f + [small_x] + small_z:
        copy.wait_send()
    for chunk, slot in ((1, 1), (0, 0)):
        for k in range(4):
            to_x(chunk, slot, k).wait_send()
        for i in range(3):
            to_z(chunk, slot, i).wait_send()
    for i, copy in enumerate(outs):
        if i not in (n1_kept, res_out, down_out, up_out):
            copy.wait()


TOTAL = [0]


def layer_call(*operands):
    any_, vm = pl.ANY, pltpu.VMEM
    outs = [
        ((R, D), BF, any_),
        ((R, D), F32, any_),
        ((BLK, D), F32, any_),
        ((BLK, D), F32, any_),
        ((BLK, D), F32, any_),
        ((16, D), F32, vm),
        ((1, 1), F32, vm),
        ((G, D), BF, any_),
    ]
    dma = pltpu.SemaphoreType.DMA
    scratch = [
        vm((R, D), BF),
        vm((G, 128), BF),
        vm((3, D, D), BF),
        vm((D, W), BF),
        vm((G, D), BF),
        vm((G, D), BF),
        vm((G, F), BF),
        vm((G, D), BF),
        vm((G, 2 * W), BF),
        vm((G, W), BF),
        vm((G, W), BF),
        vm((QUAD, D), F32),
        vm((R, D), F32),
        vm((R, D), F32),
        vm((R, D), F32),
        vm((5, SUB, D), BF),
        vm((3, 3, SUB, D), BF),
        vm((2, D, D), BF),
        vm((2, 4, BLK, D), BF),
        vm((2, 3, BLK, D), BF),
        vm((BLK, D), F32),
        vm((8, D), F32),
        vm((16, D), F32),
        vm((4, 8, 128), F32),
        vm((2, 8, 128), F32),
        vm((4, 16, D), F32),
        vm((2, 16, D), F32),
        vm((4, 16, D), F32),
        dma((4, 15)),
        dma((4, 8)),
        dma((6, 9)),
        dma((6, 9)),
        dma((5, 9)),
        dma((5, 9)),
        dma((3, 4)),
        dma((3, 4)),
        dma((3, 3)),
        dma((3, 3)),
        dma((4, 4)),
        dma((4, 4)),
        dma((3,)),
        dma((3,)),
        dma((10,)),
        dma((8,)),
        pltpu.SemaphoreType.REGULAR,
        pltpu.SemaphoreType.REGULAR,
        pltpu.SemaphoreType.REGULAR,
    ]
    ins = [any_] * 6 + [vm] * 12
    return pl.pallas_call(
        layer_kernel,
        out_shape=[jax.ShapeDtypeStruct(shape, dtype) for shape, dtype, _ in outs],
        in_specs=[pl.BlockSpec(memory_space=space) for space in ins],
        out_specs=[pl.BlockSpec(memory_space=space) for _, _, space in outs],
        scratch_shapes=scratch,
        compiler_params=pltpu.CompilerParams(
            collective_id=1, has_side_effects=True, vmem_limit_bytes=64 << 20
        ),
        name="layer",
    )(*operands)


def turn_tables():
    import ml_dtypes

    quarter = HD // 4
    frequency = (1.0 / np.float32(10000.0) ** (np.arange(quarter, dtype=np.float32) * 4.0 / HD)).astype(np.float32)
    angle = (np.arange(16, dtype=np.float32)[:, None] * frequency[None, :]).astype(np.float32)
    cosine, sine = np.cos(angle.astype(np.float64)), np.sin(angle.astype(np.float64))
    zero = np.zeros_like(cosine)

    def head(first, second):
        top = np.concatenate([first, zero, second, zero], axis=1)
        low = np.concatenate([zero, first, zero, second], axis=1)
        return np.tile(np.concatenate([top, low], axis=0), (1, 2 * HEADS_LOCAL))

    full = np.concatenate([head(cosine, cosine), head(-sine, zero), head(zero, sine)], axis=1).astype(np.float32)
    terms = []
    rest = full
    for _ in range(3):
        term = rest.astype(ml_dtypes.bfloat16)
        terms.append(term)
        rest = rest - term.astype(np.float32)
    terms.append(np.zeros((32, full.shape[1]), ml_dtypes.bfloat16))
    return jnp.asarray(np.concatenate(terms, axis=0))


def finish_kernel(
    res_i, gtok_i, gd_i, gu_i, ga_i, small, loss_i,
    res_o, loss_o, gtok_o, fg_o, fs_o, mix_o, mb_o, vb_o, out_o, ob_o, sg_o, ss_o, up_o, ub_o, down_o, db_o,
    ga, gtok, res, gd, gu, sems,
):
    dp = lax.axis_index("dp")
    copies = [
        pltpu.make_async_copy(src, dst, sems.at[i])
        for i, (src, dst) in enumerate(
            [
                (gtok_i, gtok),
                (ga_i, ga),
                (res_i, res),
                (gd_i, gd),
                (gu_i, gu),
                (gtok, gtok_o),
                (res, res_o),
                (gd, down_o),
                (gu, up_o),
            ]
        )
    ]
    for copy in copies[:5]:
        copy.start()
    loss_o[...] = loss_i[...]
    pieces = pltpu.roll(small[:8, :], lax.rem(D - BLK * dp + D, D), 1)[:, :BLK]
    for i, ref in ((0, fg_o), (1, fs_o), (2, ob_o), (3, sg_o), (4, ss_o), (5, db_o)):
        ref[...] = pieces[i : i + 1, :].reshape(BLK)
    ub_o[...] = small[pl.ds(8 + lax.div(dp, 2), 1), _ds(640 * lax.rem(dp, 2), 640, 128)].reshape(640)
    row = small[pl.ds(12 + lax.rem(dp, 4), 1), :]
    mb_o[...] = pltpu.roll(row, lax.rem(D - W * lax.div(dp, 4), D), 1)[:, :W].reshape(W)
    row = small[pl.ds(12 + lax.div(dp, 2), 1), :]
    vb_o[...] = pltpu.roll(row, 2 * W - BLK * lax.rem(dp, 2), 1)[:, :BLK].reshape(BLK)
    copies[0].wait()
    copies[5].start()
    for i in (2, 3, 4):
        copies[i].wait()
        copies[i + 4].start()
    copies[1].wait()
    for t in range(3):
        mix_o[t] = ga[:, W * t : W * t + W]
    out_o[...] = ga[:, 3 * W :]
    for copy in copies[5:]:
        copy.wait()


def finish_call(*operands):
    any_, vm = pl.ANY, pltpu.VMEM
    outs = [
        ((R, D), BF, any_),
        ((1, 1), F32, vm),
        ((R, D), F32, any_),
        ((BLK,), F32, vm),
        ((BLK,), F32, vm),
        ((3, BLK, W), F32, vm),
        ((W,), F32, vm),
        ((BLK,), F32, vm),
        ((BLK, W), F32, vm),
        ((BLK,), F32, vm),
        ((BLK,), F32, vm),
        ((BLK,), F32, vm),
        ((BLK, D), F32, any_),
        ((640,), F32, vm),
        ((BLK, D), F32, any_),
        ((BLK,), F32, vm),
    ]
    ins = [any_] * 5 + [vm] * 2
    return pl.pallas_call(
        finish_kernel,
        out_shape=[jax.ShapeDtypeStruct(shape, dtype) for shape, dtype, _ in outs],
        in_specs=[pl.BlockSpec(memory_space=space) for space in ins],
        out_specs=[pl.BlockSpec(memory_space=space) for _, _, space in outs],
        scratch_shapes=[
            vm((BLK, D), F32),
            vm((R, D), F32),
            vm((R, D), BF),
            vm((BLK, D), F32),
            vm((BLK, D), F32),
            pltpu.SemaphoreType.DMA((9,)),
        ],
        compiler_params=pltpu.CompilerParams(vmem_limit_bytes=62 << 20),
        name="finish",
    )(*operands)


def on_device_fast(
    tokens,
    teacher,
    picture,
    places,
    validity,
    first_gain,
    first_shift,
    mixer_weight,
    mixer_bias,
    output_weight,
    output_bias,
    second_gain,
    second_shift,
    upward_weight,
    upward_bias,
    downward_weight,
    downward_bias,
):
    TOTAL[0] = float(tokens.shape[0] * lax.axis_size("dp") * lax.axis_size("fsdp"))
    res, gtok, gd, gup, ga, small, loss, _ = layer_call(
        tokens,
        teacher,
        mixer_weight.transpose(1, 0, 2),
        output_weight.T,
        upward_weight,
        downward_weight.T,
        first_gain,
        first_shift,
        output_bias,
        second_gain,
        second_shift,
        downward_bias,
        upward_bias,
        mixer_bias,
        picture.reshape(3, ROW_PATCHES),
        places.T,
        validity.reshape(3, ROW_PATCHES),
        turn_tables(),
    )
    (res, loss, gtok, fg, fs, mix, mb, vb, out, ob, sg, ss, up, ub, down, db) = finish_call(
        res, gtok, gd, gup, ga, small, loss
    )
    return (res, loss.reshape(()), gtok, fg, fs, mix.transpose(1, 0, 2), mb, vb, out.T, ob, sg, ss, up, ub, down.T, db)


def solution(mesh):
    fast = mesh.shape["dp"] == 8 and mesh.shape["fsdp"] == 4
    return jax.shard_map(
        on_device_fast if fast else on_device,
        mesh=mesh,
        in_specs=(
            P(("dp", "fsdp"), None),
            P(("dp", "fsdp"), None),
            P(("dp", "fsdp")),
            P(("dp", "fsdp"), None),
            P(("dp", "fsdp")),
            P("dp"),
            P("dp"),
            P("dp", None, "fsdp"),
            P("dp"),
            P("fsdp", "dp"),
            P("dp"),
            P("dp"),
            P("dp"),
            P("dp", "fsdp"),
            P("dp"),
            P("fsdp", "dp"),
            P("dp"),
        ),
        out_specs=(
            P(("dp", "fsdp"), None),
            P(),
            P(("dp", "fsdp"), None),
            P("dp"),
            P("dp"),
            P("dp", None, "fsdp"),
            P("dp"),
            P("dp"),
            P("fsdp", "dp"),
            P("dp"),
            P("dp"),
            P("dp"),
            P("dp", "fsdp"),
            P("dp"),
            P("fsdp", "dp"),
            P("dp"),
        ),
        check_vma=False,
    )
```

```python
import numpy as np
import jax
import jax.numpy as jnp
from jax import lax
from jax.experimental import pallas as pl
from jax.experimental.pallas import tpu as pltpu
from jax.sharding import PartitionSpec as P

D = 1280
HD = 80
FF = 5120
ROW_PATCHES = 128
MB = 3


EPSILON = 1e-06


def norm_forward(values, scaler, offset):
    average = jnp.mean(values, axis=-1, keepdims=True)
    centered = values - average
    reciprocal = lax.rsqrt(jnp.mean(centered * centered, axis=-1, keepdims=True) + EPSILON)
    normed = centered * reciprocal
    return (normed * scaler.astype(jnp.float32) + offset.astype(jnp.float32), normed, reciprocal)


def norm_backward(gradient, normed, reciprocal, scaler):
    scaled = gradient * scaler.astype(jnp.float32)
    adjusted = (
        scaled
        - jnp.mean(scaled, axis=-1, keepdims=True)
        - normed * jnp.mean(scaled * normed, axis=-1, keepdims=True)
    )
    return (adjusted * reciprocal, jnp.sum(gradient * normed, axis=0), jnp.sum(gradient, axis=0))


def tables(places):
    quarter = HD // 4
    frequency = 1.0 / 10000.0 ** (jnp.arange(quarter, dtype=jnp.float32) * 4.0 / HD)
    row_angle = places[:, 0:1].astype(jnp.float32) * frequency
    col_angle = places[:, 1:2].astype(jnp.float32) * frequency
    angle_all = jnp.concatenate([row_angle, col_angle, row_angle, col_angle], axis=-1)
    return (jnp.cos(angle_all)[:, None, :], jnp.sin(angle_all)[:, None, :])


def rotate(values, cosine, sine):
    halfway = HD // 2
    flipped = jnp.concatenate([-values[..., halfway:], values[..., :halfway]], axis=-1)
    return values * cosine + flipped * sine


def unrotate(gradient, cosine, sine):
    halfway = HD // 2
    shifted = gradient * sine
    return gradient * cosine + jnp.concatenate(
        [shifted[..., halfway:], -shifted[..., :halfway]], axis=-1
    )


def allowed_mask(picture, validity):
    picture_rows = picture.reshape(-1, ROW_PATCHES)
    occupancy_flags = validity.reshape(-1, ROW_PATCHES) > 0
    shared_picture_mask = picture_rows[:, :, None] == picture_rows[:, None, :]
    self_pairs = jnp.eye(ROW_PATCHES, dtype=bool)[None]
    return (shared_picture_mask & occupancy_flags[:, None, :] | self_pairs)[:, None]


def scores_of(query, key_rows, permitted_pairs):
    products = jnp.einsum(
        "bqhd,bkhd->bhqk", query, key_rows, preferred_element_type=jnp.float32
    ) * HD ** (-0.5)
    return jnp.where(permitted_pairs, products, -1e30)


def attend(query, key_rows, value_rows, permitted_pairs):
    scores = scores_of(query, key_rows, permitted_pairs)
    maximum = jnp.max(scores, axis=-1, keepdims=True)
    log_total = maximum + jnp.log(jnp.sum(jnp.exp(scores - maximum), axis=-1, keepdims=True))
    probs = jnp.exp(scores - log_total).astype(jnp.bfloat16)
    attended = jnp.einsum("bhqk,bkhd->bqhd", probs, value_rows, preferred_element_type=jnp.float32)
    return (attended, log_total)


def attend_back(grad_attended, query, key_rows, value_rows, permitted_pairs, log_total):
    scores = scores_of(query, key_rows, permitted_pairs)
    probs = jnp.exp(scores - log_total)
    grad_probs = jnp.einsum(
        "bqhd,bkhd->bhqk", grad_attended, value_rows, preferred_element_type=jnp.float32
    )
    delta = jnp.sum(grad_probs * probs, axis=-1, keepdims=True)
    grad_scores = (probs * (grad_probs - delta)).astype(jnp.bfloat16)
    scaling = HD ** (-0.5)
    grad_query = (
        jnp.einsum("bhqk,bkhd->bqhd", grad_scores, key_rows, preferred_element_type=jnp.float32)
        * scaling
    )
    grad_key = (
        jnp.einsum("bhqk,bqhd->bkhd", grad_scores, query, preferred_element_type=jnp.float32)
        * scaling
    )
    grad_value = jnp.einsum(
        "bhqk,bqhd->bkhd",
        probs.astype(jnp.bfloat16),
        grad_attended,
        preferred_element_type=jnp.float32,
    )
    return (grad_query, grad_key, grad_value)


def quick_gelu_grad(grad_active, upper):
    sigmoid_up = jax.nn.sigmoid(1.702 * upper)
    return (grad_active * (sigmoid_up + 1.702 * upper * sigmoid_up * (1.0 - sigmoid_up))).astype(
        jnp.bfloat16
    )


def own_slice(vector, data_index, data_ways):
    length = vector.shape[0] // data_ways
    return lax.dynamic_slice_in_dim(vector, data_index * length, length, 0)


def on_device(
    tokens,
    teacher,
    picture,
    places,
    validity,
    first_gain,
    first_shift,
    mixer_weight,
    mixer_bias,
    output_weight,
    output_bias,
    second_gain,
    second_shift,
    upward_weight,
    upward_bias,
    downward_weight,
    downward_bias,
):
    data_ways = lax.axis_size("dp")
    split_ways = lax.axis_size("fsdp")
    member = lax.axis_index("fsdp")
    data_index = lax.axis_index("dp")
    occupancy_flags = validity.astype(jnp.float32)
    token_tally = lax.psum(jnp.sum(occupancy_flags), ("dp", "fsdp"))
    factor = tokens.shape[0] * data_ways * split_ways / token_tally
    (
        mixer_local,
        output_local,
        upward_local,
        downward_local,
        gain_one,
        shift_one,
        mixer_shift,
        output_shift,
        gain_two,
        shift_two,
        upward_shift,
        downward_shift,
    ) = (
        lax.all_gather(mixer_weight, "dp", axis=0, tiled=True),
        lax.all_gather(output_weight, "dp", axis=1, tiled=True),
        lax.all_gather(upward_weight, "dp", axis=0, tiled=True),
        lax.all_gather(downward_weight, "dp", axis=1, tiled=True),
        lax.all_gather(first_gain, "dp", axis=0, tiled=True),
        lax.all_gather(first_shift, "dp", axis=0, tiled=True),
        lax.all_gather(mixer_bias, "dp", axis=0, tiled=True),
        lax.all_gather(output_bias, "dp", axis=0, tiled=True),
        lax.all_gather(second_gain, "dp", axis=0, tiled=True),
        lax.all_gather(second_shift, "dp", axis=0, tiled=True),
        lax.all_gather(upward_bias, "dp", axis=0, tiled=True),
        lax.all_gather(downward_bias, "dp", axis=0, tiled=True),
    )
    width_local = output_local.shape[0]
    heads_local = width_local // HD
    hidden_local = upward_local.shape[1]
    mixer_flat = mixer_local.reshape(D, 3 * width_local)
    mixer_piece = lax.dynamic_slice_in_dim(
        mixer_shift.reshape(3, D), member * width_local, width_local, 1
    )
    mixer_piece = mixer_piece.reshape(3 * width_local).astype(jnp.float32)
    upward_piece = lax.dynamic_slice_in_dim(
        upward_shift, member * hidden_local, hidden_local, 0
    ).astype(jnp.float32)
    packed_rows = tokens.shape[0] // MB
    errors = jnp.zeros((), jnp.float32)
    matrix_sums = None
    small_sums = None
    results = []
    input_grads = []
    for micro in range(MB):
        start_offset = micro * packed_rows
        inputs = tokens[start_offset : start_offset + packed_rows].astype(jnp.float32)
        target = teacher[start_offset : start_offset + packed_rows].astype(jnp.float32)
        occupied_rows = occupancy_flags[start_offset : start_offset + packed_rows]
        picture_rows = picture[start_offset : start_offset + packed_rows]
        local_picture = (picture_rows - picture_rows[0]).astype(jnp.bfloat16)
        place_rows = places[start_offset : start_offset + packed_rows].astype(jnp.bfloat16)
        live_marks = validity[start_offset : start_offset + packed_rows].astype(jnp.bfloat16)
        shifted_one, normed_one, recip_one = norm_forward(inputs, gain_one, shift_one)
        lowered_one = shifted_one.astype(jnp.bfloat16)
        group_one, group_picture, group_places, group_live = (
            lax.all_gather(lowered_one, "fsdp", axis=0, tiled=True),
            lax.all_gather(local_picture, "fsdp", axis=0, tiled=True),
            lax.all_gather(place_rows, "fsdp", axis=0, tiled=True),
            lax.all_gather(live_marks, "fsdp", axis=0, tiled=True),
        )
        group_rows = group_one.shape[0]
        mixed = jnp.dot(group_one, mixer_flat, preferred_element_type=jnp.float32) + mixer_piece
        mixed = mixed.reshape(group_rows, 3, heads_local, HD)
        cosine, sine = tables(group_places)
        query = (
            rotate(mixed[:, 0], cosine, sine)
            .astype(jnp.bfloat16)
            .reshape(-1, ROW_PATCHES, heads_local, HD)
        )
        key_rows = (
            rotate(mixed[:, 1], cosine, sine)
            .astype(jnp.bfloat16)
            .reshape(-1, ROW_PATCHES, heads_local, HD)
        )
        value_rows = mixed[:, 2].astype(jnp.bfloat16).reshape(-1, ROW_PATCHES, heads_local, HD)
        permitted_pairs = allowed_mask(group_picture, group_live)
        attended, log_total = attend(query, key_rows, value_rows, permitted_pairs)
        attended = attended.reshape(group_rows, width_local).astype(jnp.bfloat16)
        branch = lax.psum_scatter(
            jnp.dot(attended, output_local, preferred_element_type=jnp.float32).astype(
                jnp.bfloat16
            ),
            "fsdp",
            scatter_dimension=0,
            tiled=True,
        ).astype(jnp.float32)
        middle = inputs + branch + output_shift.astype(jnp.float32)
        shifted_two, normed_two, recip_two = norm_forward(middle, gain_two, shift_two)
        lowered_two = shifted_two.astype(jnp.bfloat16)
        group_two = lax.all_gather(lowered_two, "fsdp", axis=0, tiled=True)
        upper = jnp.dot(group_two, upward_local, preferred_element_type=jnp.float32) + upward_piece
        active = (upper * jax.nn.sigmoid(1.702 * upper)).astype(jnp.bfloat16)
        lowered = lax.psum_scatter(
            jnp.dot(active, downward_local, preferred_element_type=jnp.float32).astype(
                jnp.bfloat16
            ),
            "fsdp",
            scatter_dimension=0,
            tiled=True,
        ).astype(jnp.float32)
        outputs = middle + lowered + downward_shift.astype(jnp.float32)
        difference = outputs - target
        masked = occupied_rows[:, None] * difference
        errors = errors + jnp.sum(masked * difference)
        grad_out = 2.0 * factor * masked
        grad_low = grad_out.astype(jnp.bfloat16)
        down_bias_term = jnp.sum(grad_low.astype(jnp.float32), axis=0)
        group_grad = lax.all_gather(grad_low, "fsdp", axis=0, tiled=True)
        g_down = jnp.einsum("rf,rd->fd", active, group_grad, preferred_element_type=jnp.float32)
        grad_active = jnp.einsum(
            "rd,fd->rf", group_grad, downward_local, preferred_element_type=jnp.float32
        )
        grad_upper = quick_gelu_grad(grad_active, upper)
        g_up = jnp.einsum("rd,rf->df", group_two, grad_upper, preferred_element_type=jnp.float32)
        up_bias_term = lax.dynamic_update_slice_in_dim(
            jnp.zeros((FF,), jnp.float32),
            jnp.sum(grad_upper.astype(jnp.float32), axis=0),
            member * hidden_local,
            0,
        )
        grad_two = lax.psum_scatter(
            jnp.einsum(
                "rf,df->rd", grad_upper, upward_local, preferred_element_type=jnp.float32
            ).astype(jnp.bfloat16),
            "fsdp",
            scatter_dimension=0,
            tiled=True,
        ).astype(jnp.float32)
        back_two, g_gain_two, g_shift_two = norm_backward(grad_two, normed_two, recip_two, gain_two)
        grad_middle = grad_out + back_two
        grad_branch = grad_middle.astype(jnp.bfloat16)
        out_bias_term = jnp.sum(grad_branch.astype(jnp.float32), axis=0)
        group_branch = lax.all_gather(grad_branch, "fsdp", axis=0, tiled=True)
        g_output = jnp.einsum(
            "rd,re->de", attended, group_branch, preferred_element_type=jnp.float32
        )
        grad_attended = jnp.einsum(
            "re,de->rd", group_branch, output_local, preferred_element_type=jnp.float32
        )
        grad_attended = grad_attended.astype(jnp.bfloat16).reshape(-1, ROW_PATCHES, heads_local, HD)
        grad_query, grad_key, grad_value = attend_back(
            grad_attended, query, key_rows, value_rows, permitted_pairs, log_total
        )
        grad_mixed = jnp.stack(
            [
                unrotate(grad_query.reshape(group_rows, heads_local, HD), cosine, sine),
                unrotate(grad_key.reshape(group_rows, heads_local, HD), cosine, sine),
                grad_value.reshape(group_rows, heads_local, HD),
            ],
            axis=1,
        )
        grad_mixed = grad_mixed.reshape(group_rows, 3 * width_local).astype(jnp.bfloat16)
        g_mixer = jnp.einsum("rd,re->de", group_one, grad_mixed, preferred_element_type=jnp.float32)
        g_mixer = g_mixer.reshape(D, 3, width_local)
        mixer_bias_term = lax.dynamic_update_slice_in_dim(
            jnp.zeros((3, D), jnp.float32),
            jnp.sum(grad_mixed.astype(jnp.float32), axis=0).reshape(3, width_local),
            member * width_local,
            1,
        )
        mixer_bias_term = mixer_bias_term.reshape(3 * D)
        grad_one = lax.psum_scatter(
            jnp.einsum(
                "re,de->rd", grad_mixed, mixer_flat, preferred_element_type=jnp.float32
            ).astype(jnp.bfloat16),
            "fsdp",
            scatter_dimension=0,
            tiled=True,
        ).astype(jnp.float32)
        back_one, g_gain_one, g_shift_one = norm_backward(grad_one, normed_one, recip_one, gain_one)
        grad_inputs = grad_middle + back_one
        matrices = (g_mixer, g_output, g_up, g_down)
        smalls = (
            g_gain_one,
            g_shift_one,
            mixer_bias_term,
            out_bias_term,
            g_gain_two,
            g_shift_two,
            up_bias_term,
            down_bias_term,
        )
        matrix_sums = (
            matrices if matrix_sums is None else jax.tree.map(jnp.add, matrix_sums, matrices)
        )
        small_sums = smalls if small_sums is None else jax.tree.map(jnp.add, small_sums, smalls)
        results.append(outputs.astype(jnp.bfloat16))
        input_grads.append(grad_inputs)
    g_mixer_sum, g_output_sum, g_up_sum, g_down_sum = matrix_sums
    reduced = (
        lax.psum_scatter(
            g_mixer_sum.astype(jnp.bfloat16), "dp", scatter_dimension=0, tiled=True
        ).astype(jnp.float32),
        lax.psum_scatter(
            g_output_sum.astype(jnp.bfloat16), "dp", scatter_dimension=1, tiled=True
        ).astype(jnp.float32),
        lax.psum_scatter(
            g_up_sum.astype(jnp.bfloat16), "dp", scatter_dimension=0, tiled=True
        ).astype(jnp.float32),
        lax.psum_scatter(
            g_down_sum.astype(jnp.bfloat16), "dp", scatter_dimension=1, tiled=True
        ).astype(jnp.float32),
    )
    totals = lax.psum(
        (
            small_sums[0],
            small_sums[1],
            small_sums[2],
            small_sums[3],
            small_sums[4],
            small_sums[5],
            small_sums[6],
            small_sums[7],
            errors,
        ),
        ("dp", "fsdp"),
    )
    pieces = [own_slice(totals[index], data_index, data_ways) for index in range(8)]
    query_key_piece = own_slice(totals[2][: 2 * D], data_index, data_ways)
    value_piece = own_slice(totals[2][2 * D :], data_index, data_ways)
    loss = totals[8] / (token_tally * D)
    return (
        jnp.concatenate(results, axis=0),
        loss,
        jnp.concatenate(input_grads, axis=0),
        pieces[0],
        pieces[1],
        reduced[0],
        query_key_piece,
        value_piece,
        reduced[1],
        pieces[3],
        pieces[4],
        pieces[5],
        reduced[2],
        pieces[6],
        reduced[3],
        pieces[7],
    )


BF = jnp.bfloat16
F32 = jnp.float32
HEADS_LOCAL = 4
W = 320
F = 1280
R = 384
G = 1536
BLK = 160
SUB = 128
QUAD = 512
HALF = 640
MESH_ID = pl.DeviceIdType.MESH


def _nn(a, b):
    return lax.dot_general(a, b, (((1,), (0,)), ((), ())), preferred_element_type=F32)


def _nt(a, b):
    return lax.dot_general(a, b, (((1,), (1,)), ((), ())), preferred_element_type=F32)


def _tn(a, b):
    return lax.dot_general(a, b, (((0,), (0,)), ((), ())), preferred_element_type=F32)


def _ds(start, size, step):
    if isinstance(start, int):
        return pl.ds(start, size)
    return pl.ds(pl.multiple_of(start, step), size)


class Place:
    def __init__(self):
        dp = lax.axis_index("dp")
        fs = lax.axis_index("fsdp")
        z, x = lax.div(dp, 2), lax.rem(dp, 2)
        y, c = lax.div(fs, 2), lax.rem(fs, 2)
        self.z, self.x, self.fs, self.dp = z, x, fs, dp
        self.core = (dp, 2 * y + 1 - c)
        self.ynb = (dp, 2 * (1 - y) + c)
        self.diagonal = (dp, 2 * (1 - y) + 1 - c)
        self.mates = (2 * y + 1 - c, 2 * (1 - y) + c, 2 * (1 - y) + 1 - c)
        self.xnb = (2 * z + 1 - x, fs)
        self.zs = (z, z + 1 - 2 * lax.rem(z, 2), lax.rem(z + 2, 4), 3 - z)
        self.zn = tuple((2 * zk + x, fs) for zk in self.zs)
        self.up = (2 * jnp.minimum(z + 1, 3) + x, fs)
        self.down = (2 * jnp.maximum(z - 1, 0) + x, fs)
        self.near = lax.div(z, 2)
        self.far = 1 - self.near

    def barrier(self):
        sem = pltpu.get_barrier_semaphore()
        for peer in (self.core, self.ynb, self.diagonal, self.xnb) + self.zn[1:]:
            pl.semaphore_signal(sem, inc=1, device_id=peer, device_id_type=MESH_ID)
        pl.semaphore_wait(sem, 7)


def _send(src, dst, ss, rs, peer):
    return pltpu.make_async_remote_copy(
        src_ref=src, dst_ref=dst, send_sem=ss, recv_sem=rs, device_id=peer, device_id_type=MESH_ID
    )


class Gather:
    def __init__(self, place, buf, ss, rs, cols=slice(None)):
        self.place, self.buf, self.ss, self.rs, self.cols = place, buf, ss, rs, cols

    def part(self, s, slot):
        return self.buf.at[_ds(QUAD * s + SUB * slot, SUB, SUB), self.cols]

    def to_core(self, s):
        return _send(self.part(s, 0), self.part(s, 1), self.ss.at[s], self.rs.at[s], self.place.core)

    def to_y(self, s):
        return _send(self.part(s, 0), self.part(s, 2), self.ss.at[3 + s], self.rs.at[3 + s], self.place.ynb)

    def on(self, s):
        return _send(self.part(s, 2), self.part(s, 3), self.ss.at[6 + s], self.rs.at[6 + s], self.place.core)

    def start(self, s):
        self.to_y(s).start()
        self.to_core(s).start()

    def pass_on(self, s):
        self.to_y(s).wait_recv()
        self.on(s).start()

    def ready(self, s):
        self.to_core(s).wait_recv()
        self.on(s).wait_recv()

    def end(self):
        for s in range(3):
            self.to_core(s).wait_send()
            self.to_y(s).wait_send()
            self.on(s).wait_send()


class Scatter:
    def __init__(self, place, sb, rb, own, ss, rs, cols=slice(None)):
        self.place, self.sb, self.rb, self.own, self.ss, self.rs, self.cols = place, sb, rb, own, ss, rs, cols

    def copy(self, kind, s):
        peer = self.place.ynb if kind == 1 else self.place.core
        slot = 2 + s if kind == 1 else kind // 2
        return _send(
            self.sb.at[slot, :, self.cols],
            self.rb.at[kind, s, :, self.cols],
            self.ss.at[3 * kind + s],
            self.rs.at[3 * kind + s],
            peer,
        )

    def again(self, kind, s):
        if isinstance(s, int):
            if s > 0:
                self.copy(kind, s - 1).wait_send()
        else:
            pl.when(s > 0)(lambda: self.copy(kind, s - 1).wait_send())

    def post(self, s, lhs, rhs):
        rows = QUAD * s
        term = _nt(lhs(_ds(rows + 2 * SUB, 2 * SUB, SUB)), rhs())
        self.again(0, s)
        self.sb[0, :, self.cols] = term[SUB:].astype(BF)
        self.copy(0, s).start()
        mine = _nt(lhs(_ds(rows, 2 * SUB, SUB)), rhs())
        self.again(2, s)
        self.sb[1, :, self.cols] = mine[SUB:].astype(BF)
        self.copy(2, s).start()
        self.own[_ds(SUB * s, SUB, SUB), self.cols] = mine[:SUB]
        self.copy(0, s).wait_recv()
        self.sb[2 + s, :, self.cols] = (term[:SUB] + self.rb[0, s, :, self.cols].astype(F32)).astype(BF)
        self.copy(1, s).start()

    def wait(self, s):
        self.copy(2, s).wait_recv()
        self.copy(1, s).wait_recv()

    def total(self, s, i, step):
        sub = _ds(step * i, step, step)
        return self.own[_ds(SUB * s + step * i, step, step), self.cols] + (
            self.rb[2, s, sub, self.cols].astype(F32) + self.rb[1, s, sub, self.cols].astype(F32)
        )

    def end(self):
        self.copy(0, 2).wait_send()
        self.copy(2, 2).wait_send()
        for s in range(3):
            self.copy(1, s).wait_send()


def _norm(values):
    average = jnp.mean(values, axis=-1, keepdims=True)
    centered = values - average
    reciprocal = lax.rsqrt(jnp.mean(centered * centered, axis=-1, keepdims=True) + EPSILON)
    return centered * reciprocal, reciprocal


def _head_rows(lanes, offset):
    lane = lax.broadcasted_iota(jnp.int32, (1, lanes), 1) - offset
    return [
        jnp.where((lane >= HD * h) & (lane < HD * h + HD), 1.0, 0.0).astype(BF)
        for h in range(HEADS_LOCAL)
    ]


def _stack(values, heads):
    return jnp.concatenate([values * head for head in heads], axis=0)


def _allowed(auxb):
    lane = lax.broadcasted_iota(jnp.int32, (1, 128), 1)
    picks = (lane >= 96) & (lane < 104)
    left = jnp.where(picks, auxb.astype(F32), jnp.where(lane == 104, 1.0, 0.0)).astype(BF)
    score = _nt(left, auxb)
    here = lax.broadcasted_iota(jnp.int32, (128, 128), 0)
    there = lax.broadcasted_iota(jnp.int32, (128, 128), 1)
    return (score > 1.5) | (here == there)


def _softmax(scores, allowed):
    probs = []
    for h in range(HEADS_LOCAL):
        part = jnp.where(allowed, scores[:, 128 * h : 128 * h + 128], -1e30)
        grown = jnp.exp(part - jnp.max(part, axis=-1, keepdims=True))
        probs.append(grown * (1.0 / jnp.sum(grown, axis=-1, keepdims=True)))
    return probs


PIECES = ((0, 0, 1024), (0, 1024, 256), (1, 0, 1280), (2, 0, 1280))


def _spread(packed, place):
    dp, fs = place.dp, place.fs

    def wide(ref):
        size = ref.shape[0]
        return jnp.concatenate([ref[...].astype(F32).reshape(1, size), jnp.zeros((1, D - size), F32)], axis=1)

    rows = jnp.concatenate([wide(ref) for ref in packed[:6]], axis=0)
    rows = pltpu.roll(rows, BLK * dp, 1)
    up = pltpu.roll(wide(packed[6]), 640 * lax.rem(dp, 2), 1)
    up = up * jnp.where(lax.div(dp, 2) == fs, 1.0, 0.0)
    mixed = wide(packed[7])
    lane = lax.broadcasted_iota(jnp.int32, (1, D), 1)
    row = jnp.zeros((1, D), F32)
    for t in range(3):
        shift = 480 * dp - 960 * t - W * fs
        turned = pltpu.roll(mixed, lax.rem(shift + 4 * D, D), 1)
        mine = (lane >= W * t) & (lane < W * t + W) & (lane >= shift) & (lane < shift + 480)
        row = row + jnp.where(mine, turned, 0.0)
    return jnp.concatenate([rows, up, row], axis=0)


def _marks(pictures, spots, real, s):
    lane = lax.broadcasted_iota(jnp.int32, (3, SUB), 1)
    change = jnp.where((pictures != pltpu.roll(pictures, 1, 1)) & (lane > 0), 1.0, 0.0).astype(BF)
    here = lax.broadcasted_iota(jnp.int32, (SUB, SUB), 0)
    there = lax.broadcasted_iota(jnp.int32, (SUB, SUB), 1)
    upto = jnp.where(here <= there, 1.0, 0.0).astype(BF)
    rank = _nn(change, upto)[s : s + 1, :].astype(jnp.int32)
    spot = lax.rem(here, 32)
    row = (spot < 16) & (spot == spots[0:1, SUB * s : SUB * s + SUB])
    col = (spot >= 16) & (spot - 16 == spots[1:2, SUB * s : SUB * s + SUB])
    once = (here < 96) & (row | col)
    picture = (here >= 96) & (here < 104) & (here - 96 == rank)
    live = (here == 104) & (real[s : s + 1, :] > 0)
    return jnp.where(once | picture | live, 1.0, 0.0).T.astype(BF)


def layer_kernel(
    tok_h, teach_h, mix_h, out_h, wu_h, wd_h, v0, v1, v2, v3, v4, v5, v6, v7, pictures, spots, real, tabs,
    res_h, gtok_h, gd_h, gu_h, ga_h, small_o, loss_o, keep_h,
    tok, aux, w, wo, n1a, n2, gu, gzb, qk, v, o, acc, own, mid, gy, sb, rb,
    gb, xin, zin, fin, vecs, small, ccz, ccx, sta, stx, stz,
    ws, wr, ags, agr, rss, rsr, xs, xr, zs, zr, as_, ar, bs, br, ls, os_, xfree, zfree, gfree, nfree,
):
    place = Place()
    z, x = place.z, place.x
    patches = TOTAL[0]
    mine = _ds(BLK * (2 * z + x), BLK, 32)
    loads = [
        pltpu.make_async_copy(src, dst, ls.at[i])
        for i, (src, dst) in enumerate(
            [(mix_h.at[t], o.at[pl.ds(BLK * t, BLK), :]) for t in range(3)]
            + [(out_h, o.at[pl.ds(3 * BLK, BLK), :]), (tok_h, tok)]
            + [(wu_h, w.at[1, mine, :]), (wd_h, w.at[2, mine, :])]
        )
    ]
    for copy in loads:
        copy.start()
    stz[z, :8, :] = _spread((v0, v1, v2, v3, v4, v5, v6, v7), place)
    place.barrier()

    def over_z(buf, rows, kind):
        there = buf.at[z, rows, :]
        return [_send(there, there, as_.at[kind, k], ar.at[kind, z], place.zn[k]) for k in (1, 2, 3)]

    def from_z(buf, rows, kind):
        for k in (1, 2, 3):
            there = buf.at[place.zs[k], rows, :]
            _send(there, there, as_.at[kind, k], ar.at[kind, place.zs[k]], place.zn[k]).wait_recv()

    def swap_x(buf, rows, kind):
        return _send(buf.at[0, rows, :], buf.at[1, rows, :], bs.at[kind], br.at[kind], place.xnb)

    first8 = pl.ds(0, 8)
    vector_z = over_z(stz, first8, 0)
    for copy in vector_z:
        copy.start()

    shards = (None, wu_h, wd_h)

    def at(piece, zk, xk):
        third, start, size = PIECES[piece]
        return w.at[third, _ds(BLK * (2 * zk + xk), BLK, 32), pl.ds(start, size)]

    def shard(piece):
        third, start, size = PIECES[piece]
        if third == 0:
            return at(piece, z, x)
        return shards[third].at[:, pl.ds(start, size)]

    def first(piece, i):
        peer = (place.xnb, place.up, place.down)[i]
        return _send(shard(piece), at(piece, z, x), ws.at[piece, i], wr.at[piece, 2 * z + x], peer)

    def begin_z(piece):
        pl.when(z < 3)(lambda: first(piece, 1).start())
        pl.when(z > 0)(lambda: first(piece, 2).start())

    def begin_x(piece):
        first(piece, 0).start()

    def hop(piece, d, i):
        zk = jnp.maximum(z - d, 0) if i < 2 else jnp.minimum(z + d, 3)
        peer = (place.up, place.xnb, place.down, place.xnb)[i]
        there = at(piece, zk, x)
        return _send(there, there, ws.at[piece, 4 * d - 1 + i], wr.at[piece, 2 * zk + x], peer)

    def relay(piece, d):
        @pl.when(z >= d)
        def _():
            hop(piece, d, 0).wait_recv()
            pl.when(z < 3)(lambda: hop(piece, d, 0).start())
            hop(piece, d, 1).start()

        @pl.when(z + d <= 3)
        def _():
            hop(piece, d, 2).wait_recv()
            pl.when(z > 0)(lambda: hop(piece, d, 2).start())
            hop(piece, d, 3).start()

    def over_x(piece, zk):
        there = at(piece, zk, 1 - x)
        _send(there, there, ws.at[piece, 0], wr.at[piece, 2 * zk + 1 - x], place.xnb).wait_recv()

    def complete(piece):
        for k in range(4):
            over_x(piece, place.zs[k])

    def sent(piece):
        first(piece, 0).wait_send()
        pl.when(z < 3)(lambda: first(piece, 1).wait_send())
        pl.when(z > 0)(lambda: first(piece, 2).wait_send())
        for d in range(1, 4):

            @pl.when(z >= d)
            def _(d=d):
                pl.when(z < 3)(lambda: hop(piece, d, 0).wait_send())
                hop(piece, d, 1).wait_send()

            @pl.when(z + d <= 3)
            def _(d=d):
                pl.when(z > 0)(lambda: hop(piece, d, 2).wait_send())
                hop(piece, d, 3).wait_send()

    outs = []

    def out(src, dst):
        copy = pltpu.make_async_copy(src, dst, os_.at[len(outs)])
        copy.start()
        outs.append(copy)
        return len(outs) - 1

    for copy in loads[:4]:
        copy.wait()
    w[0, mine, :] = jnp.concatenate([o[pl.ds(BLK * t, BLK), :] for t in range(4)], axis=1)
    begin_z(0)
    begin_x(0)
    agx = Gather(place, aux, ags.at[1], agr.at[1])
    for s in range(3):
        aux[pl.ds(QUAD * s, SUB), :] = _marks(pictures[...], spots[...], real[...], s)
        agx.start(s)
    loads[4].wait()

    def first_norm(i, _):
        rows = _ds(32 * i, 32, 32)
        own[rows, :] = _norm(tok[rows, :].astype(F32))[0]
        return 0

    lax.fori_loop(0, R // 32, first_norm, 0)
    from_z(stz, first8, 0)
    stx[0, :8, :] = (stz[0, :8, :] + stz[1, :8, :]) + (stz[2, :8, :] + stz[3, :8, :])
    vector_x = swap_x(stx, first8, 0)
    vector_x.start()
    vector_x.wait_recv()
    vecs[...] = stx[0, :8, :] + stx[1, :8, :]
    ag1 = Gather(place, n1a, ags.at[0], agr.at[0])
    for s in range(3):

        def scale_rows(i, _, s=s):
            rows = _ds(QUAD * s + 32 * i, 32, 32)
            n1a[rows, :] = (own[_ds(SUB * s + 32 * i, 32, 32), :] * vecs[0:1, :] + vecs[1:2, :]).astype(BF)
            return 0

        lax.fori_loop(0, 4, scale_rows, 0)
        ag1.start(s)
    relay(0, 1)
    for s in range(3):
        agx.pass_on(s)
    relay(0, 2)
    begin_z(1)
    ag1.pass_on(0)
    relay(0, 3)
    begin_x(1)
    for s in range(3):
        agx.ready(s)
    whole = slice(None)
    count_z = over_z(ccz, whole, 1)
    count_x = swap_x(ccx, whole, 1)
    complete(0)
    for copy in vector_z + [vector_x]:
        copy.wait_send()

    side = _head_rows(W, 0)
    rs1 = Scatter(place, sb, rb, own, rss.at[0], rsr.at[0])

    def attend_part(s, _):
        ag1.ready(s)
        acc[:, : 3 * W] = _nn(n1a[_ds(QUAD * s, QUAD, QUAD), :], w[0, :, : 3 * W]) + vecs[7:8, : 3 * W]

        def attend_rows(i, _):
            here = _ds(SUB * i, SUB, SUB)
            rows = _ds(QUAD * s + SUB * i, SUB, SUB)
            auxb = aux[rows, :]
            angle = _nn(auxb, tabs[...])
            raw = acc[here, : 2 * W]
            turned = (
                raw * angle[:, : 2 * W]
                + pltpu.roll(raw, 2 * W - 40, 1) * angle[:, 2 * W : 4 * W]
                + pltpu.roll(raw, 40, 1) * angle[:, 4 * W :]
            )
            qkb = turned.astype(BF)
            kqb = pltpu.roll(turned, W, 1)[:, :W].astype(BF)
            vb = acc[here, 2 * W : 3 * W].astype(BF)
            qk[rows, :] = qkb
            v[rows, :] = vb
            scores = _nt(qkb[:, :W], _stack(kqb, side)) * HD ** (-0.5)
            probs = _softmax(scores, _allowed(auxb))
            flat = jnp.concatenate([p.astype(BF) for p in probs], axis=1)
            o[rows, :] = _nn(flat, _stack(vb, side)).astype(BF)

            @pl.when((s == 0) & (i == 0))
            def _():
                relay(1, 1)
                ag1.pass_on(1)

            @pl.when((s == 0) & (i == 1))
            def _():
                relay(1, 2)
                begin_z(2)

            @pl.when((s == 0) & (i == 2))
            def _():
                relay(1, 3)
                begin_x(2)

            pl.when((s == 1) & (i == 2))(lambda: relay(2, 1))

            @pl.when((s == 2) & (i == 2))
            def _():
                relay(2, 2)
                begin_z(3)

            return 0

        lax.fori_loop(0, 4, attend_rows, 0)

        @pl.when(s == 0)
        def _():
            complete(1)
            wo[...] = w[0, :, 3 * W :]
            ag1.pass_on(2)


        rs1.post(s, lambda rows: o[rows, :], lambda: wo[...])

        @pl.when(s == 0)
        def _():
            ccz[z] = _nn(jnp.ones((8, G), BF), aux[...])
            for copy in count_z:
                copy.start()

        return 0

    lax.fori_loop(0, 3, attend_part, 0)
    n1_kept = out(n1a, keep_h)
    ag2 = Gather(place, n2, ags.at[2], agr.at[2])

    def second_norm(s, _):
        rs1.wait(s)

        def rows_of(i, _):
            rows = _ds(SUB * s + 32 * i, 32, 32)
            middle = tok[rows, :].astype(F32) + rs1.total(s, i, 32) + vecs[2:3, :]
            mid[rows, :] = middle
            normed, _r = _norm(middle)
            n2[_ds(QUAD * s + 32 * i, 32, 32), :] = (normed * vecs[3:4, :] + vecs[4:5, :]).astype(BF)
            return 0

        lax.fori_loop(0, 4, rows_of, 0)
        ag2.start(s)

        @pl.when(s == 1)
        def _():
            relay(2, 3)
            from_z(ccz, whole, 1)
            ccx[0] = (ccz[0] + ccz[1]) + (ccz[2] + ccz[3])
            count_x.start()
            begin_x(3)

        return 0

    lax.fori_loop(0, 3, second_norm, 0)
    teach = tok
    teach_load = pltpu.make_async_copy(teach_h, teach, ls.at[7])
    teach_load.start()
    relay(3, 1)
    ag1.end()
    outs[n1_kept].wait()
    loads[5].wait()
    complete(2)

    def up_part(s, _):
        pl.when(s == 1)(lambda: relay(3, 2))
        pl.when(s == 2)(lambda: relay(3, 3))
        ag2.pass_on(s)
        ag2.ready(s)
        acc[...] = _nn(n2[_ds(QUAD * s, QUAD, QUAD), :], w[1]) + vecs[6:7, :]

        def rows_of(i, _):
            upper = acc[_ds(32 * i, 32, 32), :]
            rows = _ds(QUAD * s + 32 * i, 32, 32)
            gate = 0.5 * jnp.tanh(0.851 * upper) + 0.5
            n1a[rows, :] = (upper * gate).astype(BF)
            gu[rows, :] = (gate + 1.702 * upper * gate * (1.0 - gate)).astype(BF)
            return 0

        lax.fori_loop(0, QUAD // 32, rows_of, 0)
        return 0

    lax.fori_loop(0, 3, up_part, 0)
    act = n1a
    rs1.end()
    loads[6].wait()
    teach_load.wait()

    cols = {0: _ds(HALF * place.near, HALF, 128), 1: _ds(HALF * place.far, HALF, 128)}
    count_x.wait_recv()
    real_count = (ccx[0] + ccx[1])[0:1, 104:105]
    factor = 2.0 * patches / real_count
    downs = [Scatter(place, sb, rb, own, rss.at[1 + j], rsr.at[1 + j], cols[j]) for j in range(2)]
    gathers = [Gather(place, gzb, ags.at[3 + j], agr.at[3 + j], cols[j]) for j in range(2)]
    small[...] = jnp.zeros_like(small)

    for j in range(2):
        for k in ((0, 1), (2, 3))[j]:
            over_x(3, place.zs[k])
        half = (place.near, place.far)[j]

        def down_part(s, _, j=j, half=half):
            downs[j].post(s, lambda rows: act[rows, :], lambda: w[2, _ds(HALF * half, HALF, 128), :])
            return 0

        lax.fori_loop(0, 3, down_part, 0)

        def finish_part(s, sums, j=j):
            downs[j].wait(s)

            def rows_of(i, sums):
                rows = _ds(SUB * s + 32 * i, 32, 32)
                result = mid[rows, cols[j]] + downs[j].total(s, i, 32) + vecs[5:6, cols[j]]
                real = aux[_ds(QUAD * s + 32 * i, 32, 32), 104:105].astype(F32)
                difference = result - teach[rows, cols[j]].astype(F32)
                masked = real * difference
                gout = factor * masked
                low = gout.astype(BF)
                gy[rows, cols[j]] = gout
                teach[rows, cols[j]] = result.astype(BF)
                gzb[_ds(QUAD * s + 32 * i, 32, 32), cols[j]] = low
                return (
                    sums[0] + jnp.sum(masked * difference, axis=0, keepdims=True),
                    sums[1] + jnp.sum(low.astype(F32), axis=0, keepdims=True),
                )

            sums = lax.fori_loop(0, 4, rows_of, sums)
            gathers[j].start(s)
            if j == 1:
                gathers[0].pass_on(s)
            return sums

        zero = jnp.zeros((1, HALF), F32)
        sums = lax.fori_loop(0, 3, finish_part, (zero, zero))
        small[6:7, cols[j]] = sums[0]
        small[5:6, cols[j]] = sums[1]
    res_out = out(teach, res_h)

    def xin_at(chunk, slot, k):
        if chunk == 3:
            return n2.at[pl.ds(BLK * k, BLK), pl.ds(256, 256)]
        return xin.at[slot, k, :, pl.ds(0, 1024)] if chunk == 0 else xin.at[slot, k]

    def zin_at(chunk, slot, i):
        if chunk == 3:
            return n2.at[pl.ds(BLK * i, BLK), pl.ds(512, 256)]
        return zin.at[slot, i, :, pl.ds(0, 1024)] if chunk == 0 else zin.at[slot, i]

    def g_rows(chunk, slot, rows):
        if chunk == 3:
            return n2.at[rows, pl.ds(0, 256)]
        return gb.at[slot, rows, pl.ds(0, 1024)] if chunk == 0 else gb.at[slot, rows, :]

    def to_x(chunk, slot, k):
        rows = _ds(BLK * (2 * place.zs[k] + 1 - x), BLK, 32)
        return _send(
            g_rows(chunk, slot, rows), xin_at(chunk, slot, k), xs.at[chunk, k], xr.at[chunk, k], place.xnb
        )

    def block(k):
        return _ds(BLK * (2 * place.zs[k] + x), BLK, 32)

    def to_z(chunk, slot, i):
        k, peer = ((3, place.zn[1]), (1, place.zn[1]), (2, place.zn[2]))[i]
        return _send(g_rows(chunk, slot, block(k)), zin_at(chunk, slot, i), zs.at[chunk, i], zr.at[chunk, i], peer)

    def tile(slot, lhs, rhs, half):
        rows = _ds(HALF * half, HALF, 128)
        for part in range(2):
            cols = pl.ds(HALF * part, HALF)
            gb[slot, rows, cols] = _tn(lhs[:, rows], rhs[:, cols]).astype(BF)

    def add_x(chunk, slot, i):
        k = (3, 1)[i]
        to_x(chunk, slot, k).wait_recv()
        ref = g_rows(chunk, slot, block(k))
        ref[...] = (ref[...].astype(F32) + xin_at(chunk, slot, k)[...].astype(F32)).astype(BF)
        to_z(chunk, slot, i).start()

    def combine(chunk, slot):
        to_x(chunk, slot, 2).wait_recv()
        to_z(chunk, slot, 0).wait_recv()
        ref = g_rows(chunk, slot, block(2))
        ref[...] = (
            (ref[...].astype(F32) + xin_at(chunk, slot, 2)[...].astype(F32)) + zin_at(chunk, slot, 0)[...].astype(F32)
        ).astype(BF)
        to_z(chunk, slot, 2).start()

    def fin_cols(chunk):
        return {0: pl.ds(0, 1024), 3: pl.ds(1024, 256)}.get(chunk, pl.ds(0, D))

    def add_own(chunk, slot):
        to_x(chunk, slot, 0).wait_recv()
        fin[:, fin_cols(chunk)] = g_rows(chunk, slot, block(0))[...].astype(F32) + xin_at(chunk, slot, 0)[...].astype(F32)

    def add_z(chunk, slot):
        to_z(chunk, slot, 1).wait_recv()
        to_z(chunk, slot, 2).wait_recv()
        cols = fin_cols(chunk)
        fin[:, cols] = fin[:, cols] + (
            zin_at(chunk, slot, 1)[...].astype(F32) + zin_at(chunk, slot, 2)[...].astype(F32)
        )

    for s in range(3):
        gathers[0].ready(s)
    tile(0, gzb, act, place.near)
    to_x(2, 0, 1).start()
    to_x(2, 0, 0).start()

    for copy in downs:
        copy.end()
    rs3 = Scatter(place, sb, rb, own, rss.at[3], rsr.at[3])
    up_total = jnp.zeros((1, F), F32)
    for s in range(3):
        gathers[1].pass_on(s)
    gathers[1].ready(0)
    for s in range(3):
        acc[...] = _nn(gzb[pl.ds(QUAD * s, QUAD), :], w[2])

        def gate_rows(i, total, s=s):
            rows = _ds(QUAD * s + 32 * i, 32, 32)
            low = (acc[_ds(32 * i, 32, 32), :] * gu[rows, :].astype(F32)).astype(BF)
            gu[rows, :] = low
            return total + jnp.sum(low.astype(F32), axis=0, keepdims=True)

        up_total = lax.fori_loop(0, QUAD // 32, gate_rows, up_total)
        rs3.post(s, lambda rows: gu[rows, :], lambda: w[1])
        if s == 0:
            for t in (1, 2):
                gathers[1].ready(t)
            tile(0, gzb, act, place.far)
            to_x(2, 0, 3).start()
            to_x(2, 0, 2).start()
    for gather in gathers:
        gather.end()
    for peer in (place.core, place.ynb):
        pl.semaphore_signal(gfree, inc=1, device_id=peer, device_id_type=MESH_ID)
    n1_back = pltpu.make_async_copy(keep_h, n1a, ls.at[8])
    n1_back.start()
    outs[res_out].wait()
    tok_back = pltpu.make_async_copy(tok_h, tok, ls.at[9])
    tok_back.start()
    small[pl.ds(8 + place.fs, 1), :] = up_total
    add_x(2, 0, 1)
    tile(1, n2, gu, place.far)
    to_x(1, 1, 3).start()
    to_x(1, 1, 2).start()
    pl.semaphore_wait(gfree, 2)
    ag3 = Gather(place, gzb, ags.at[5], agr.at[5])

    def norm_rows(s, i, sums, values, gain, terms):
        rows = _ds(SUB * s + 32 * i, 32, 32)
        grad = terms.total(s, i, 32)
        normed, reciprocal = _norm(values[rows, :].astype(F32))
        scaled = grad * gain
        back = (
            scaled
            - jnp.mean(scaled, axis=-1, keepdims=True)
            - normed * jnp.mean(scaled * normed, axis=-1, keepdims=True)
        ) * reciprocal
        total = gy[rows, :] + back
        gy[rows, :] = total
        pair = (
            sums[0] + jnp.sum(grad * normed, axis=0, keepdims=True),
            sums[1] + jnp.sum(grad, axis=0, keepdims=True),
        )
        return total, pair

    zero = jnp.zeros((1, D), F32)

    def second_back(s, sums):
        rs3.wait(s)

        def rows_of(i, sums):
            total, pair = norm_rows(s, i, sums[:2], mid, vecs[3:4, :], rs3)
            low = total.astype(BF)
            gzb[_ds(QUAD * s + 32 * i, 32, 32), :] = low
            return pair + (sums[2] + jnp.sum(low.astype(F32), axis=0, keepdims=True),)

        sums = lax.fori_loop(0, 4, rows_of, sums)
        ag3.start(s)
        return sums

    gain2, shift2, outb = lax.fori_loop(0, 3, second_back, (zero, zero, zero))
    small[2:3, :] = outb
    small[3:4, :] = gain2
    small[4:5, :] = shift2
    tile(1, n2, gu, place.near)
    to_x(1, 1, 1).start()
    to_x(1, 1, 0).start()
    ag2.end()
    for peer in (place.xnb,) + place.zn[1:3]:
        pl.semaphore_signal(nfree, inc=1, device_id=peer, device_id_type=MESH_ID)
    add_x(2, 0, 0)
    add_own(2, 0)
    rs3.end()
    rs4 = Scatter(place, sb, rb, own, rss.at[4], rsr.at[4])

    def attend_back(s, total):
        ag3.pass_on(s)
        ag3.ready(s)

        @pl.when(s == 2)
        def _():
            for half in (place.far, place.near):
                rows = _ds(HALF * half, HALF, 128)
                n2[rows, pl.ds(0, 256)] = _tn(gzb[:, rows], o[:, W - 256 :]).astype(BF)
            pl.semaphore_wait(nfree, 3)
            for k in (3, 2, 1, 0):
                to_x(3, 0, k).start()

        acc[:, :W] = _nn(gzb[_ds(QUAD * s, QUAD, QUAD), :], wo[...])

        def attend_rows(i, total):
            rows = _ds(QUAD * s + SUB * i, SUB, SUB)
            auxb = aux[rows, :]
            qkb = qk[rows, :]
            kqb = pltpu.roll(qkb.astype(F32), W, 1)[:, :W].astype(BF)
            vb = v[rows, :]
            gob = acc[_ds(SUB * i, SUB, SUB), :W].astype(BF)
            keys = _stack(kqb, side)
            scores = _nt(qkb[:, :W], keys) * HD ** (-0.5)
            probs = _softmax(scores, _allowed(auxb))
            gprobs = _nt(gob, _stack(vb, side))
            gscores = []
            for h in range(HEADS_LOCAL):
                gp = gprobs[:, 128 * h : 128 * h + 128]
                delta = jnp.sum(gp * probs[h], axis=-1, keepdims=True)
                gscores.append((probs[h] * (gp - delta)).astype(BF))
            flat = jnp.concatenate(gscores, axis=1)
            tall = jnp.concatenate(gscores, axis=0)
            ptall = jnp.concatenate([p.astype(BF) for p in probs], axis=0)
            gqk = jnp.concatenate([_nn(flat, keys), _tn(tall, _stack(qkb[:, :W], side))], axis=1) * HD ** (-0.5)
            gv = _tn(ptall, _stack(gob, side))
            angle = _nn(auxb, tabs[...])
            turned = (
                gqk * angle[:, : 2 * W]
                + pltpu.roll(gqk * angle[:, 4 * W :], 2 * W - 40, 1)
                + pltpu.roll(gqk * angle[:, 2 * W : 4 * W], 40, 1)
            )
            low = jnp.concatenate([turned, gv], axis=1).astype(BF)
            gu[rows, : 3 * W] = low
            return total + jnp.sum(low.astype(F32), axis=0, keepdims=True)

        total = lax.fori_loop(0, 4, attend_rows, total)
        rs4.post(s, lambda rows: gu[rows, : 3 * W], lambda: w[0, :, : 3 * W])


        @pl.when(s == 0)
        def _():
            combine(2, 0)
            pl.semaphore_signal(xfree, inc=1, device_id=place.xnb, device_id_type=MESH_ID)

        pl.when(s == 1)(lambda: add_x(1, 1, 0))

        @pl.when(s == 2)
        def _():
            combine(1, 1)
            add_x(1, 1, 1)

        return total

    mix_total = lax.fori_loop(0, 3, attend_back, jnp.zeros((1, 3 * W), F32))
    small[pl.ds(12 + place.fs, 1), : 3 * W] = mix_total

    for k in range(4):
        to_x(2, 0, k).wait_send()
    for i in range(3):
        to_z(2, 0, i).wait_send()
    n1_back.wait()

    def last_tile(half):
        rows = _ds(HALF * half, HALF, 128)
        gb[0, rows, : 3 * W] = _tn(n1a[:, rows], gu[:, : 3 * W]).astype(BF)
        gb[0, rows, 3 * W : 1024] = _tn(gzb[:, rows], o[:, : W - 256]).astype(BF)

    last_tile(place.far)
    pl.semaphore_wait(xfree, 1)
    to_x(0, 0, 3).start()
    to_x(0, 0, 2).start()
    last_tile(place.near)
    add_z(2, 0)
    down_out = out(fin, gd_h)
    for peer in place.zn[1:3]:
        pl.semaphore_signal(zfree, inc=1, device_id=peer, device_id_type=MESH_ID)

    tok_back.wait()

    def first_back(s, sums):
        rs4.wait(s)

        pl.when(s == 1)(lambda: add_x(3, 0, 0))
        return lax.fori_loop(0, 4, lambda i, t: norm_rows(s, i, t, tok, vecs[0:1, :], rs4)[1], sums)

    gain1, shift1 = lax.fori_loop(0, 3, first_back, (zero, zero))
    out(gy, gtok_h)
    small[0:1, :] = gain1
    small[1:2, :] = shift1

    sta[place.fs] = small[...]
    there = sta.at[place.fs]
    peers = (place.core, place.ynb, place.diagonal)
    small_f = [_send(there, there, as_.at[3, k], ar.at[3, place.fs], peer) for k, peer in enumerate(peers)]
    for copy in small_f:
        copy.start()
    outs[down_out].wait()
    for k, peer in enumerate(peers):
        there = sta.at[place.mates[k]]
        _send(there, there, as_.at[3, k], ar.at[3, place.mates[k]], peer).wait_recv()
    stx[0] = (sta[0] + sta[1]) + (sta[2] + sta[3])
    small_x = swap_x(stx, whole, 2)
    small_x.start()
    to_x(0, 0, 1).start()
    to_x(0, 0, 0).start()
    pl.semaphore_wait(zfree, 2)
    add_x(0, 0, 0)
    combine(3, 0)
    add_x(3, 0, 1)
    add_own(1, 1)
    add_z(1, 1)
    up_out = out(fin, gu_h)
    small_x.wait_recv()
    stz[z] = stx[0] + stx[1]
    small_z = over_z(stz, whole, 2)
    for copy in small_z:
        copy.start()
    combine(0, 0)
    add_x(0, 0, 1)
    outs[up_out].wait()
    add_own(3, 0)
    add_z(3, 0)
    add_own(0, 0)
    from_z(stz, whole, 2)
    total = (stz[0] + stz[1]) + (stz[2] + stz[3])
    small_o[...] = total
    loss_o[...] = jnp.sum(total[6:7, :], axis=-1, keepdims=True) / (real_count * D)
    add_z(0, 0)
    out(fin, ga_h)

    for piece in range(4):
        sent(piece)
    agx.end()
    ag3.end()
    rs4.end()
    for copy in count_z + [count_x] + small_f + [small_x] + small_z:
        copy.wait_send()
    for chunk, slot in ((1, 1), (0, 0), (3, 0)):
        for k in range(4):
            to_x(chunk, slot, k).wait_send()
        for i in range(3):
            to_z(chunk, slot, i).wait_send()
    for i, copy in enumerate(outs):
        if i not in (n1_kept, res_out, down_out, up_out):
            copy.wait()


TOTAL = [0]


def layer_call(*operands):
    any_, vm = pl.ANY, pltpu.VMEM
    outs = [
        ((R, D), BF, any_),
        ((R, D), F32, any_),
        ((BLK, D), F32, any_),
        ((BLK, D), F32, any_),
        ((BLK, D), F32, any_),
        ((16, D), F32, vm),
        ((1, 1), F32, vm),
        ((G, D), BF, any_),
    ]
    dma = pltpu.SemaphoreType.DMA
    scratch = [
        vm((R, D), BF),
        vm((G, 128), BF),
        vm((3, D, D), BF),
        vm((D, W), BF),
        vm((G, D), BF),
        vm((G, D), BF),
        vm((G, F), BF),
        vm((G, D), BF),
        vm((G, 2 * W), BF),
        vm((G, W), BF),
        vm((G, W), BF),
        vm((QUAD, D), F32),
        vm((R, D), F32),
        vm((R, D), F32),
        vm((R, D), F32),
        vm((5, SUB, D), BF),
        vm((3, 3, SUB, D), BF),
        vm((2, D, D), BF),
        vm((2, 4, BLK, D), BF),
        vm((2, 3, BLK, D), BF),
        vm((BLK, D), F32),
        vm((8, D), F32),
        vm((16, D), F32),
        vm((4, 8, 128), F32),
        vm((2, 8, 128), F32),
        vm((4, 16, D), F32),
        vm((2, 16, D), F32),
        vm((4, 16, D), F32),
        dma((4, 15)),
        dma((4, 8)),
        dma((6, 9)),
        dma((6, 9)),
        dma((5, 9)),
        dma((5, 9)),
        dma((4, 4)),
        dma((4, 4)),
        dma((4, 3)),
        dma((4, 3)),
        dma((4, 4)),
        dma((4, 4)),
        dma((3,)),
        dma((3,)),
        dma((10,)),
        dma((8,)),
        pltpu.SemaphoreType.REGULAR,
        pltpu.SemaphoreType.REGULAR,
        pltpu.SemaphoreType.REGULAR,
        pltpu.SemaphoreType.REGULAR,
    ]
    ins = [any_] * 6 + [vm] * 12
    return pl.pallas_call(
        layer_kernel,
        out_shape=[jax.ShapeDtypeStruct(shape, dtype) for shape, dtype, _ in outs],
        in_specs=[pl.BlockSpec(memory_space=space) for space in ins],
        out_specs=[pl.BlockSpec(memory_space=space) for _, _, space in outs],
        scratch_shapes=scratch,
        compiler_params=pltpu.CompilerParams(
            collective_id=1, has_side_effects=True, vmem_limit_bytes=64 << 20
        ),
        name="layer",
    )(*operands)


def turn_tables():
    import ml_dtypes

    quarter = HD // 4
    frequency = (1.0 / np.float32(10000.0) ** (np.arange(quarter, dtype=np.float32) * 4.0 / HD)).astype(np.float32)
    angle = (np.arange(16, dtype=np.float32)[:, None] * frequency[None, :]).astype(np.float32)
    cosine, sine = np.cos(angle.astype(np.float64)), np.sin(angle.astype(np.float64))
    zero = np.zeros_like(cosine)

    def head(first, second):
        top = np.concatenate([first, zero, second, zero], axis=1)
        low = np.concatenate([zero, first, zero, second], axis=1)
        return np.tile(np.concatenate([top, low], axis=0), (1, 2 * HEADS_LOCAL))

    full = np.concatenate([head(cosine, cosine), head(-sine, zero), head(zero, sine)], axis=1).astype(np.float32)
    terms = []
    rest = full
    for _ in range(3):
        term = rest.astype(ml_dtypes.bfloat16)
        terms.append(term)
        rest = rest - term.astype(np.float32)
    terms.append(np.zeros((32, full.shape[1]), ml_dtypes.bfloat16))
    return jnp.asarray(np.concatenate(terms, axis=0))


def finish_kernel(
    res_i, gtok_i, gd_i, gu_i, ga_i, small, loss_i,
    res_o, loss_o, gtok_o, fg_o, fs_o, mix_o, mb_o, vb_o, out_o, ob_o, sg_o, ss_o, up_o, ub_o, down_o, db_o,
    ga, gtok, res, gd, gu, sems,
):
    dp = lax.axis_index("dp")
    copies = [
        pltpu.make_async_copy(src, dst, sems.at[i])
        for i, (src, dst) in enumerate(
            [
                (gtok_i, gtok),
                (ga_i, ga),
                (res_i, res),
                (gd_i, gd),
                (gu_i, gu),
                (gtok, gtok_o),
                (res, res_o),
                (gd, down_o),
                (gu, up_o),
            ]
        )
    ]
    for copy in copies[:5]:
        copy.start()
    loss_o[...] = loss_i[...]
    pieces = pltpu.roll(small[:8, :], lax.rem(D - BLK * dp + D, D), 1)[:, :BLK]
    for i, ref in ((0, fg_o), (1, fs_o), (2, ob_o), (3, sg_o), (4, ss_o), (5, db_o)):
        ref[...] = pieces[i : i + 1, :].reshape(BLK)
    ub_o[...] = small[pl.ds(8 + lax.div(dp, 2), 1), _ds(640 * lax.rem(dp, 2), 640, 128)].reshape(640)
    row = small[pl.ds(12 + lax.rem(dp, 4), 1), :]
    mb_o[...] = pltpu.roll(row, lax.rem(D - W * lax.div(dp, 4), D), 1)[:, :W].reshape(W)
    row = small[pl.ds(12 + lax.div(dp, 2), 1), :]
    vb_o[...] = pltpu.roll(row, 2 * W - BLK * lax.rem(dp, 2), 1)[:, :BLK].reshape(BLK)
    copies[0].wait()
    copies[5].start()
    for i in (2, 3, 4):
        copies[i].wait()
        copies[i + 4].start()
    copies[1].wait()
    for t in range(3):
        mix_o[t] = ga[:, W * t : W * t + W]
    out_o[...] = ga[:, 3 * W :]
    for copy in copies[5:]:
        copy.wait()


def finish_call(*operands):
    any_, vm = pl.ANY, pltpu.VMEM
    outs = [
        ((R, D), BF, any_),
        ((1, 1), F32, vm),
        ((R, D), F32, any_),
        ((BLK,), F32, vm),
        ((BLK,), F32, vm),
        ((3, BLK, W), F32, vm),
        ((W,), F32, vm),
        ((BLK,), F32, vm),
        ((BLK, W), F32, vm),
        ((BLK,), F32, vm),
        ((BLK,), F32, vm),
        ((BLK,), F32, vm),
        ((BLK, D), F32, any_),
        ((640,), F32, vm),
        ((BLK, D), F32, any_),
        ((BLK,), F32, vm),
    ]
    ins = [any_] * 5 + [vm] * 2
    return pl.pallas_call(
        finish_kernel,
        out_shape=[jax.ShapeDtypeStruct(shape, dtype) for shape, dtype, _ in outs],
        in_specs=[pl.BlockSpec(memory_space=space) for space in ins],
        out_specs=[pl.BlockSpec(memory_space=space) for _, _, space in outs],
        scratch_shapes=[
            vm((BLK, D), F32),
            vm((R, D), F32),
            vm((R, D), BF),
            vm((BLK, D), F32),
            vm((BLK, D), F32),
            pltpu.SemaphoreType.DMA((9,)),
        ],
        compiler_params=pltpu.CompilerParams(vmem_limit_bytes=62 << 20),
        name="finish",
    )(*operands)


def on_device_fast(
    tokens,
    teacher,
    picture,
    places,
    validity,
    first_gain,
    first_shift,
    mixer_weight,
    mixer_bias,
    output_weight,
    output_bias,
    second_gain,
    second_shift,
    upward_weight,
    upward_bias,
    downward_weight,
    downward_bias,
):
    TOTAL[0] = float(tokens.shape[0] * lax.axis_size("dp") * lax.axis_size("fsdp"))
    res, gtok, gd, gup, ga, small, loss, _ = layer_call(
        tokens,
        teacher,
        mixer_weight.transpose(1, 0, 2),
        output_weight.T,
        upward_weight,
        downward_weight.T,
        first_gain,
        first_shift,
        output_bias,
        second_gain,
        second_shift,
        downward_bias,
        upward_bias,
        mixer_bias,
        picture.reshape(3, ROW_PATCHES),
        places.T,
        validity.reshape(3, ROW_PATCHES),
        turn_tables(),
    )
    (res, loss, gtok, fg, fs, mix, mb, vb, out, ob, sg, ss, up, ub, down, db) = finish_call(
        res, gtok, gd, gup, ga, small, loss
    )
    return (res, loss.reshape(()), gtok, fg, fs, mix.transpose(1, 0, 2), mb, vb, out.T, ob, sg, ss, up, ub, down.T, db)


def solution(mesh):
    fast = mesh.shape["dp"] == 8 and mesh.shape["fsdp"] == 4
    return jax.shard_map(
        on_device_fast if fast else on_device,
        mesh=mesh,
        in_specs=(
            P(("dp", "fsdp"), None),
            P(("dp", "fsdp"), None),
            P(("dp", "fsdp")),
            P(("dp", "fsdp"), None),
            P(("dp", "fsdp")),
            P("dp"),
            P("dp"),
            P("dp", None, "fsdp"),
            P("dp"),
            P("fsdp", "dp"),
            P("dp"),
            P("dp"),
            P("dp"),
            P("dp", "fsdp"),
            P("dp"),
            P("fsdp", "dp"),
            P("dp"),
        ),
        out_specs=(
            P(("dp", "fsdp"), None),
            P(),
            P(("dp", "fsdp"), None),
            P("dp"),
            P("dp"),
            P("dp", None, "fsdp"),
            P("dp"),
            P("dp"),
            P("fsdp", "dp"),
            P("dp"),
            P("dp"),
            P("dp"),
            P("dp", "fsdp"),
            P("dp"),
            P("fsdp", "dp"),
            P("dp"),
        ),
        check_vma=False,
    )
```

```python
import numpy as np
import jax
import jax.numpy as jnp
from jax import lax
from jax.experimental import pallas as pl
from jax.experimental.pallas import tpu as pltpu
from jax.sharding import PartitionSpec as P

D = 1280
HD = 80
FF = 5120
ROW_PATCHES = 128
MB = 3


EPSILON = 1e-06


def norm_forward(values, scaler, offset):
    average = jnp.mean(values, axis=-1, keepdims=True)
    centered = values - average
    reciprocal = lax.rsqrt(jnp.mean(centered * centered, axis=-1, keepdims=True) + EPSILON)
    normed = centered * reciprocal
    return (normed * scaler.astype(jnp.float32) + offset.astype(jnp.float32), normed, reciprocal)


def norm_backward(gradient, normed, reciprocal, scaler):
    scaled = gradient * scaler.astype(jnp.float32)
    adjusted = (
        scaled
        - jnp.mean(scaled, axis=-1, keepdims=True)
        - normed * jnp.mean(scaled * normed, axis=-1, keepdims=True)
    )
    return (adjusted * reciprocal, jnp.sum(gradient * normed, axis=0), jnp.sum(gradient, axis=0))


def tables(places):
    quarter = HD // 4
    frequency = 1.0 / 10000.0 ** (jnp.arange(quarter, dtype=jnp.float32) * 4.0 / HD)
    row_angle = places[:, 0:1].astype(jnp.float32) * frequency
    col_angle = places[:, 1:2].astype(jnp.float32) * frequency
    angle_all = jnp.concatenate([row_angle, col_angle, row_angle, col_angle], axis=-1)
    return (jnp.cos(angle_all)[:, None, :], jnp.sin(angle_all)[:, None, :])


def rotate(values, cosine, sine):
    halfway = HD // 2
    flipped = jnp.concatenate([-values[..., halfway:], values[..., :halfway]], axis=-1)
    return values * cosine + flipped * sine


def unrotate(gradient, cosine, sine):
    halfway = HD // 2
    shifted = gradient * sine
    return gradient * cosine + jnp.concatenate(
        [shifted[..., halfway:], -shifted[..., :halfway]], axis=-1
    )


def allowed_mask(picture, validity):
    picture_rows = picture.reshape(-1, ROW_PATCHES)
    occupancy_flags = validity.reshape(-1, ROW_PATCHES) > 0
    shared_picture_mask = picture_rows[:, :, None] == picture_rows[:, None, :]
    self_pairs = jnp.eye(ROW_PATCHES, dtype=bool)[None]
    return (shared_picture_mask & occupancy_flags[:, None, :] | self_pairs)[:, None]


def scores_of(query, key_rows, permitted_pairs):
    products = jnp.einsum(
        "bqhd,bkhd->bhqk", query, key_rows, preferred_element_type=jnp.float32
    ) * HD ** (-0.5)
    return jnp.where(permitted_pairs, products, -1e30)


def attend(query, key_rows, value_rows, permitted_pairs):
    scores = scores_of(query, key_rows, permitted_pairs)
    maximum = jnp.max(scores, axis=-1, keepdims=True)
    log_total = maximum + jnp.log(jnp.sum(jnp.exp(scores - maximum), axis=-1, keepdims=True))
    probs = jnp.exp(scores - log_total).astype(jnp.bfloat16)
    attended = jnp.einsum("bhqk,bkhd->bqhd", probs, value_rows, preferred_element_type=jnp.float32)
    return (attended, log_total)


def attend_back(grad_attended, query, key_rows, value_rows, permitted_pairs, log_total):
    scores = scores_of(query, key_rows, permitted_pairs)
    probs = jnp.exp(scores - log_total)
    grad_probs = jnp.einsum(
        "bqhd,bkhd->bhqk", grad_attended, value_rows, preferred_element_type=jnp.float32
    )
    delta = jnp.sum(grad_probs * probs, axis=-1, keepdims=True)
    grad_scores = (probs * (grad_probs - delta)).astype(jnp.bfloat16)
    scaling = HD ** (-0.5)
    grad_query = (
        jnp.einsum("bhqk,bkhd->bqhd", grad_scores, key_rows, preferred_element_type=jnp.float32)
        * scaling
    )
    grad_key = (
        jnp.einsum("bhqk,bqhd->bkhd", grad_scores, query, preferred_element_type=jnp.float32)
        * scaling
    )
    grad_value = jnp.einsum(
        "bhqk,bqhd->bkhd",
        probs.astype(jnp.bfloat16),
        grad_attended,
        preferred_element_type=jnp.float32,
    )
    return (grad_query, grad_key, grad_value)


def quick_gelu_grad(grad_active, upper):
    sigmoid_up = jax.nn.sigmoid(1.702 * upper)
    return (grad_active * (sigmoid_up + 1.702 * upper * sigmoid_up * (1.0 - sigmoid_up))).astype(
        jnp.bfloat16
    )


def own_slice(vector, data_index, data_ways):
    length = vector.shape[0] // data_ways
    return lax.dynamic_slice_in_dim(vector, data_index * length, length, 0)


def on_device(
    tokens,
    teacher,
    picture,
    places,
    validity,
    first_gain,
    first_shift,
    mixer_weight,
    mixer_bias,
    output_weight,
    output_bias,
    second_gain,
    second_shift,
    upward_weight,
    upward_bias,
    downward_weight,
    downward_bias,
):
    data_ways = lax.axis_size("dp")
    split_ways = lax.axis_size("fsdp")
    member = lax.axis_index("fsdp")
    data_index = lax.axis_index("dp")
    occupancy_flags = validity.astype(jnp.float32)
    token_tally = lax.psum(jnp.sum(occupancy_flags), ("dp", "fsdp"))
    factor = tokens.shape[0] * data_ways * split_ways / token_tally
    (
        mixer_local,
        output_local,
        upward_local,
        downward_local,
        gain_one,
        shift_one,
        mixer_shift,
        output_shift,
        gain_two,
        shift_two,
        upward_shift,
        downward_shift,
    ) = (
        lax.all_gather(mixer_weight, "dp", axis=0, tiled=True),
        lax.all_gather(output_weight, "dp", axis=1, tiled=True),
        lax.all_gather(upward_weight, "dp", axis=0, tiled=True),
        lax.all_gather(downward_weight, "dp", axis=1, tiled=True),
        lax.all_gather(first_gain, "dp", axis=0, tiled=True),
        lax.all_gather(first_shift, "dp", axis=0, tiled=True),
        lax.all_gather(mixer_bias, "dp", axis=0, tiled=True),
        lax.all_gather(output_bias, "dp", axis=0, tiled=True),
        lax.all_gather(second_gain, "dp", axis=0, tiled=True),
        lax.all_gather(second_shift, "dp", axis=0, tiled=True),
        lax.all_gather(upward_bias, "dp", axis=0, tiled=True),
        lax.all_gather(downward_bias, "dp", axis=0, tiled=True),
    )
    width_local = output_local.shape[0]
    heads_local = width_local // HD
    hidden_local = upward_local.shape[1]
    mixer_flat = mixer_local.reshape(D, 3 * width_local)
    mixer_piece = lax.dynamic_slice_in_dim(
        mixer_shift.reshape(3, D), member * width_local, width_local, 1
    )
    mixer_piece = mixer_piece.reshape(3 * width_local).astype(jnp.float32)
    upward_piece = lax.dynamic_slice_in_dim(
        upward_shift, member * hidden_local, hidden_local, 0
    ).astype(jnp.float32)
    packed_rows = tokens.shape[0] // MB
    errors = jnp.zeros((), jnp.float32)
    matrix_sums = None
    small_sums = None
    results = []
    input_grads = []
    for micro in range(MB):
        start_offset = micro * packed_rows
        inputs = tokens[start_offset : start_offset + packed_rows].astype(jnp.float32)
        target = teacher[start_offset : start_offset + packed_rows].astype(jnp.float32)
        occupied_rows = occupancy_flags[start_offset : start_offset + packed_rows]
        picture_rows = picture[start_offset : start_offset + packed_rows]
        local_picture = (picture_rows - picture_rows[0]).astype(jnp.bfloat16)
        place_rows = places[start_offset : start_offset + packed_rows].astype(jnp.bfloat16)
        live_marks = validity[start_offset : start_offset + packed_rows].astype(jnp.bfloat16)
        shifted_one, normed_one, recip_one = norm_forward(inputs, gain_one, shift_one)
        lowered_one = shifted_one.astype(jnp.bfloat16)
        group_one, group_picture, group_places, group_live = (
            lax.all_gather(lowered_one, "fsdp", axis=0, tiled=True),
            lax.all_gather(local_picture, "fsdp", axis=0, tiled=True),
            lax.all_gather(place_rows, "fsdp", axis=0, tiled=True),
            lax.all_gather(live_marks, "fsdp", axis=0, tiled=True),
        )
        group_rows = group_one.shape[0]
        mixed = jnp.dot(group_one, mixer_flat, preferred_element_type=jnp.float32) + mixer_piece
        mixed = mixed.reshape(group_rows, 3, heads_local, HD)
        cosine, sine = tables(group_places)
        query = (
            rotate(mixed[:, 0], cosine, sine)
            .astype(jnp.bfloat16)
            .reshape(-1, ROW_PATCHES, heads_local, HD)
        )
        key_rows = (
            rotate(mixed[:, 1], cosine, sine)
            .astype(jnp.bfloat16)
            .reshape(-1, ROW_PATCHES, heads_local, HD)
        )
        value_rows = mixed[:, 2].astype(jnp.bfloat16).reshape(-1, ROW_PATCHES, heads_local, HD)
        permitted_pairs = allowed_mask(group_picture, group_live)
        attended, log_total = attend(query, key_rows, value_rows, permitted_pairs)
        attended = attended.reshape(group_rows, width_local).astype(jnp.bfloat16)
        branch = lax.psum_scatter(
            jnp.dot(attended, output_local, preferred_element_type=jnp.float32).astype(
                jnp.bfloat16
            ),
            "fsdp",
            scatter_dimension=0,
            tiled=True,
        ).astype(jnp.float32)
        middle = inputs + branch + output_shift.astype(jnp.float32)
        shifted_two, normed_two, recip_two = norm_forward(middle, gain_two, shift_two)
        lowered_two = shifted_two.astype(jnp.bfloat16)
        group_two = lax.all_gather(lowered_two, "fsdp", axis=0, tiled=True)
        upper = jnp.dot(group_two, upward_local, preferred_element_type=jnp.float32) + upward_piece
        active = (upper * jax.nn.sigmoid(1.702 * upper)).astype(jnp.bfloat16)
        lowered = lax.psum_scatter(
            jnp.dot(active, downward_local, preferred_element_type=jnp.float32).astype(
                jnp.bfloat16
            ),
            "fsdp",
            scatter_dimension=0,
            tiled=True,
        ).astype(jnp.float32)
        outputs = middle + lowered + downward_shift.astype(jnp.float32)
        difference = outputs - target
        masked = occupied_rows[:, None] * difference
        errors = errors + jnp.sum(masked * difference)
        grad_out = 2.0 * factor * masked
        grad_low = grad_out.astype(jnp.bfloat16)
        down_bias_term = jnp.sum(grad_low.astype(jnp.float32), axis=0)
        group_grad = lax.all_gather(grad_low, "fsdp", axis=0, tiled=True)
        g_down = jnp.einsum("rf,rd->fd", active, group_grad, preferred_element_type=jnp.float32)
        grad_active = jnp.einsum(
            "rd,fd->rf", group_grad, downward_local, preferred_element_type=jnp.float32
        )
        grad_upper = quick_gelu_grad(grad_active, upper)
        g_up = jnp.einsum("rd,rf->df", group_two, grad_upper, preferred_element_type=jnp.float32)
        up_bias_term = lax.dynamic_update_slice_in_dim(
            jnp.zeros((FF,), jnp.float32),
            jnp.sum(grad_upper.astype(jnp.float32), axis=0),
            member * hidden_local,
            0,
        )
        grad_two = lax.psum_scatter(
            jnp.einsum(
                "rf,df->rd", grad_upper, upward_local, preferred_element_type=jnp.float32
            ).astype(jnp.bfloat16),
            "fsdp",
            scatter_dimension=0,
            tiled=True,
        ).astype(jnp.float32)
        back_two, g_gain_two, g_shift_two = norm_backward(grad_two, normed_two, recip_two, gain_two)
        grad_middle = grad_out + back_two
        grad_branch = grad_middle.astype(jnp.bfloat16)
        out_bias_term = jnp.sum(grad_branch.astype(jnp.float32), axis=0)
        group_branch = lax.all_gather(grad_branch, "fsdp", axis=0, tiled=True)
        g_output = jnp.einsum(
            "rd,re->de", attended, group_branch, preferred_element_type=jnp.float32
        )
        grad_attended = jnp.einsum(
            "re,de->rd", group_branch, output_local, preferred_element_type=jnp.float32
        )
        grad_attended = grad_attended.astype(jnp.bfloat16).reshape(-1, ROW_PATCHES, heads_local, HD)
        grad_query, grad_key, grad_value = attend_back(
            grad_attended, query, key_rows, value_rows, permitted_pairs, log_total
        )
        grad_mixed = jnp.stack(
            [
                unrotate(grad_query.reshape(group_rows, heads_local, HD), cosine, sine),
                unrotate(grad_key.reshape(group_rows, heads_local, HD), cosine, sine),
                grad_value.reshape(group_rows, heads_local, HD),
            ],
            axis=1,
        )
        grad_mixed = grad_mixed.reshape(group_rows, 3 * width_local).astype(jnp.bfloat16)
        g_mixer = jnp.einsum("rd,re->de", group_one, grad_mixed, preferred_element_type=jnp.float32)
        g_mixer = g_mixer.reshape(D, 3, width_local)
        mixer_bias_term = lax.dynamic_update_slice_in_dim(
            jnp.zeros((3, D), jnp.float32),
            jnp.sum(grad_mixed.astype(jnp.float32), axis=0).reshape(3, width_local),
            member * width_local,
            1,
        )
        mixer_bias_term = mixer_bias_term.reshape(3 * D)
        grad_one = lax.psum_scatter(
            jnp.einsum(
                "re,de->rd", grad_mixed, mixer_flat, preferred_element_type=jnp.float32
            ).astype(jnp.bfloat16),
            "fsdp",
            scatter_dimension=0,
            tiled=True,
        ).astype(jnp.float32)
        back_one, g_gain_one, g_shift_one = norm_backward(grad_one, normed_one, recip_one, gain_one)
        grad_inputs = grad_middle + back_one
        matrices = (g_mixer, g_output, g_up, g_down)
        smalls = (
            g_gain_one,
            g_shift_one,
            mixer_bias_term,
            out_bias_term,
            g_gain_two,
            g_shift_two,
            up_bias_term,
            down_bias_term,
        )
        matrix_sums = (
            matrices if matrix_sums is None else jax.tree.map(jnp.add, matrix_sums, matrices)
        )
        small_sums = smalls if small_sums is None else jax.tree.map(jnp.add, small_sums, smalls)
        results.append(outputs.astype(jnp.bfloat16))
        input_grads.append(grad_inputs)
    g_mixer_sum, g_output_sum, g_up_sum, g_down_sum = matrix_sums
    reduced = (
        lax.psum_scatter(
            g_mixer_sum.astype(jnp.bfloat16), "dp", scatter_dimension=0, tiled=True
        ).astype(jnp.float32),
        lax.psum_scatter(
            g_output_sum.astype(jnp.bfloat16), "dp", scatter_dimension=1, tiled=True
        ).astype(jnp.float32),
        lax.psum_scatter(
            g_up_sum.astype(jnp.bfloat16), "dp", scatter_dimension=0, tiled=True
        ).astype(jnp.float32),
        lax.psum_scatter(
            g_down_sum.astype(jnp.bfloat16), "dp", scatter_dimension=1, tiled=True
        ).astype(jnp.float32),
    )
    totals = lax.psum(
        (
            small_sums[0],
            small_sums[1],
            small_sums[2],
            small_sums[3],
            small_sums[4],
            small_sums[5],
            small_sums[6],
            small_sums[7],
            errors,
        ),
        ("dp", "fsdp"),
    )
    pieces = [own_slice(totals[index], data_index, data_ways) for index in range(8)]
    query_key_piece = own_slice(totals[2][: 2 * D], data_index, data_ways)
    value_piece = own_slice(totals[2][2 * D :], data_index, data_ways)
    loss = totals[8] / (token_tally * D)
    return (
        jnp.concatenate(results, axis=0),
        loss,
        jnp.concatenate(input_grads, axis=0),
        pieces[0],
        pieces[1],
        reduced[0],
        query_key_piece,
        value_piece,
        reduced[1],
        pieces[3],
        pieces[4],
        pieces[5],
        reduced[2],
        pieces[6],
        reduced[3],
        pieces[7],
    )


BF = jnp.bfloat16
F32 = jnp.float32
HEADS_LOCAL = 4
W = 320
F = 1280
R = 384
G = 1536
BLK = 160
SUB = 128
QUAD = 512
HALF = 640
MESH_ID = pl.DeviceIdType.MESH


def _nn(a, b):
    return lax.dot_general(a, b, (((1,), (0,)), ((), ())), preferred_element_type=F32)


def _nt(a, b):
    return lax.dot_general(a, b, (((1,), (1,)), ((), ())), preferred_element_type=F32)


def _tn(a, b):
    return lax.dot_general(a, b, (((0,), (0,)), ((), ())), preferred_element_type=F32)


def _ds(start, size, step):
    if isinstance(start, int):
        return pl.ds(start, size)
    return pl.ds(pl.multiple_of(start, step), size)


class Place:
    def __init__(self):
        dp = lax.axis_index("dp")
        fs = lax.axis_index("fsdp")
        z, x = lax.div(dp, 2), lax.rem(dp, 2)
        y, c = lax.div(fs, 2), lax.rem(fs, 2)
        self.z, self.x, self.fs, self.dp = z, x, fs, dp
        self.core = (dp, 2 * y + 1 - c)
        self.ynb = (dp, 2 * (1 - y) + c)
        self.diagonal = (dp, 2 * (1 - y) + 1 - c)
        self.mates = (2 * y + 1 - c, 2 * (1 - y) + c, 2 * (1 - y) + 1 - c)
        self.xnb = (2 * z + 1 - x, fs)
        self.zs = (z, z + 1 - 2 * lax.rem(z, 2), lax.rem(z + 2, 4), 3 - z)
        self.zn = tuple((2 * zk + x, fs) for zk in self.zs)
        self.up = (2 * jnp.minimum(z + 1, 3) + x, fs)
        self.down = (2 * jnp.maximum(z - 1, 0) + x, fs)
        self.near = lax.div(z, 2)
        self.far = 1 - self.near

    def barrier(self):
        sem = pltpu.get_barrier_semaphore()
        for peer in (self.core, self.ynb, self.diagonal, self.xnb) + self.zn[1:]:
            pl.semaphore_signal(sem, inc=1, device_id=peer, device_id_type=MESH_ID)
        pl.semaphore_wait(sem, 7)


def _send(src, dst, ss, rs, peer):
    return pltpu.make_async_remote_copy(
        src_ref=src, dst_ref=dst, send_sem=ss, recv_sem=rs, device_id=peer, device_id_type=MESH_ID
    )


class Gather:
    def __init__(self, place, buf, ss, rs, cols=slice(None)):
        self.place, self.buf, self.ss, self.rs, self.cols = place, buf, ss, rs, cols

    def part(self, s, slot):
        return self.buf.at[_ds(QUAD * s + SUB * slot, SUB, SUB), self.cols]

    def to_core(self, s):
        return _send(self.part(s, 0), self.part(s, 1), self.ss.at[s], self.rs.at[s], self.place.core)

    def to_y(self, s):
        return _send(self.part(s, 0), self.part(s, 2), self.ss.at[3 + s], self.rs.at[3 + s], self.place.ynb)

    def on(self, s):
        return _send(self.part(s, 2), self.part(s, 3), self.ss.at[6 + s], self.rs.at[6 + s], self.place.core)

    def start(self, s):
        self.to_y(s).start()
        self.to_core(s).start()

    def pass_on(self, s):
        self.to_y(s).wait_recv()
        self.on(s).start()

    def ready(self, s):
        self.to_core(s).wait_recv()
        self.on(s).wait_recv()

    def end(self):
        for s in range(3):
            self.to_core(s).wait_send()
            self.to_y(s).wait_send()
            self.on(s).wait_send()


class Scatter:
    def __init__(self, place, sb, rb, own, ss, rs, cols=slice(None)):
        self.place, self.sb, self.rb, self.own, self.ss, self.rs, self.cols = place, sb, rb, own, ss, rs, cols

    def copy(self, kind, s):
        peer = self.place.ynb if kind == 1 else self.place.core
        slot = 2 + s if kind == 1 else kind // 2
        return _send(
            self.sb.at[slot, :, self.cols],
            self.rb.at[kind, s, :, self.cols],
            self.ss.at[3 * kind + s],
            self.rs.at[3 * kind + s],
            peer,
        )

    def again(self, kind, s):
        if isinstance(s, int):
            if s > 0:
                self.copy(kind, s - 1).wait_send()
        else:
            pl.when(s > 0)(lambda: self.copy(kind, s - 1).wait_send())

    def post(self, s, lhs, rhs):
        rows = QUAD * s
        term = _nt(lhs(_ds(rows + 2 * SUB, 2 * SUB, SUB)), rhs())
        self.again(0, s)
        self.sb[0, :, self.cols] = term[SUB:].astype(BF)
        self.copy(0, s).start()
        mine = _nt(lhs(_ds(rows, 2 * SUB, SUB)), rhs())
        self.again(2, s)
        self.sb[1, :, self.cols] = mine[SUB:].astype(BF)
        self.copy(2, s).start()
        self.own[_ds(SUB * s, SUB, SUB), self.cols] = mine[:SUB]
        self.copy(0, s).wait_recv()
        self.sb[2 + s, :, self.cols] = (term[:SUB] + self.rb[0, s, :, self.cols].astype(F32)).astype(BF)
        self.copy(1, s).start()

    def wait(self, s):
        self.copy(2, s).wait_recv()
        self.copy(1, s).wait_recv()

    def total(self, s, i, step):
        sub = _ds(step * i, step, step)
        return self.own[_ds(SUB * s + step * i, step, step), self.cols] + (
            self.rb[2, s, sub, self.cols].astype(F32) + self.rb[1, s, sub, self.cols].astype(F32)
        )

    def end(self):
        self.copy(0, 2).wait_send()
        self.copy(2, 2).wait_send()
        for s in range(3):
            self.copy(1, s).wait_send()


def _norm(values):
    average = jnp.mean(values, axis=-1, keepdims=True)
    centered = values - average
    reciprocal = lax.rsqrt(jnp.mean(centered * centered, axis=-1, keepdims=True) + EPSILON)
    return centered * reciprocal, reciprocal


def _head_rows(lanes, offset):
    lane = lax.broadcasted_iota(jnp.int32, (1, lanes), 1) - offset
    return [
        jnp.where((lane >= HD * h) & (lane < HD * h + HD), 1.0, 0.0).astype(BF)
        for h in range(HEADS_LOCAL)
    ]


def _stack(values, heads):
    return jnp.concatenate([values * head for head in heads], axis=0)


def _allowed(auxb):
    lane = lax.broadcasted_iota(jnp.int32, (1, 128), 1)
    picks = (lane >= 96) & (lane < 104)
    left = jnp.where(picks, auxb.astype(F32), jnp.where(lane == 104, 1.0, 0.0)).astype(BF)
    score = _nt(left, auxb)
    here = lax.broadcasted_iota(jnp.int32, (128, 128), 0)
    there = lax.broadcasted_iota(jnp.int32, (128, 128), 1)
    return (score > 1.5) | (here == there)


def _softmax(scores, allowed):
    probs = []
    for h in range(HEADS_LOCAL):
        part = jnp.where(allowed, scores[:, 128 * h : 128 * h + 128], -1e30)
        grown = jnp.exp(part - jnp.max(part, axis=-1, keepdims=True))
        probs.append(grown * (1.0 / jnp.sum(grown, axis=-1, keepdims=True)))
    return probs


PIECES = ((0, 0, 1024), (0, 1024, 256), (1, 0, 1280), (2, 0, 1280))


def _spread(packed, place):
    dp, fs = place.dp, place.fs

    def wide(ref):
        size = ref.shape[0]
        return jnp.concatenate([ref[...].astype(F32).reshape(1, size), jnp.zeros((1, D - size), F32)], axis=1)

    rows = jnp.concatenate([wide(ref) for ref in packed[:6]], axis=0)
    rows = pltpu.roll(rows, BLK * dp, 1)
    up = pltpu.roll(wide(packed[6]), 640 * lax.rem(dp, 2), 1)
    up = up * jnp.where(lax.div(dp, 2) == fs, 1.0, 0.0)
    mixed = wide(packed[7])
    lane = lax.broadcasted_iota(jnp.int32, (1, D), 1)
    row = jnp.zeros((1, D), F32)
    for t in range(3):
        shift = 480 * dp - 960 * t - W * fs
        turned = pltpu.roll(mixed, lax.rem(shift + 4 * D, D), 1)
        mine = (lane >= W * t) & (lane < W * t + W) & (lane >= shift) & (lane < shift + 480)
        row = row + jnp.where(mine, turned, 0.0)
    return jnp.concatenate([rows, up, row], axis=0)


def _marks(pictures, spots, real, s):
    lane = lax.broadcasted_iota(jnp.int32, (3, SUB), 1)
    change = jnp.where((pictures != pltpu.roll(pictures, 1, 1)) & (lane > 0), 1.0, 0.0).astype(BF)
    here = lax.broadcasted_iota(jnp.int32, (SUB, SUB), 0)
    there = lax.broadcasted_iota(jnp.int32, (SUB, SUB), 1)
    upto = jnp.where(here <= there, 1.0, 0.0).astype(BF)
    rank = _nn(change, upto)[s : s + 1, :].astype(jnp.int32)
    spot = lax.rem(here, 32)
    row = (spot < 16) & (spot == spots[0:1, SUB * s : SUB * s + SUB])
    col = (spot >= 16) & (spot - 16 == spots[1:2, SUB * s : SUB * s + SUB])
    once = (here < 96) & (row | col)
    picture = (here >= 96) & (here < 104) & (here - 96 == rank)
    live = (here == 104) & (real[s : s + 1, :] > 0)
    return jnp.where(once | picture | live, 1.0, 0.0).T.astype(BF)


def layer_kernel(
    tok_h, teach_h, mix_h, out_h, wu_h, wd_h, v0, v1, v2, v3, v4, v5, v6, v7, pictures, spots, real, tabs,
    res_h, gtok_h, gd_h, gu_h, ga_h, small_o, loss_o, keep_h,
    tok, aux, w, wo, n1a, n2, gu, gzb, qk, v, o, acc, own, mid, gy, sb, rb,
    gb, xin, zin, fin, vecs, small, ccz, ccx, sta, stx, stz,
    ws, wr, ags, agr, rss, rsr, xs, xr, zs, zr, as_, ar, bs, br, ls, os_, xfree, zfree, gfree, nfree,
):
    place = Place()
    z, x = place.z, place.x
    patches = TOTAL[0]
    mine = _ds(BLK * (2 * z + x), BLK, 32)
    loads = [
        pltpu.make_async_copy(src, dst, ls.at[i])
        for i, (src, dst) in enumerate(
            [(mix_h.at[t], o.at[pl.ds(BLK * t, BLK), :]) for t in range(3)]
            + [(out_h, o.at[pl.ds(3 * BLK, BLK), :]), (tok_h, tok)]
            + [(wu_h, w.at[1, mine, :]), (wd_h, w.at[2, mine, :])]
        )
    ]
    for copy in loads:
        copy.start()
    stz[z, :8, :] = _spread((v0, v1, v2, v3, v4, v5, v6, v7), place)
    place.barrier()

    def over_z(buf, rows, kind):
        there = buf.at[z, rows, :]
        return [_send(there, there, as_.at[kind, k], ar.at[kind, z], place.zn[k]) for k in (1, 2, 3)]

    def from_z(buf, rows, kind):
        for k in (1, 2, 3):
            there = buf.at[place.zs[k], rows, :]
            _send(there, there, as_.at[kind, k], ar.at[kind, place.zs[k]], place.zn[k]).wait_recv()

    def swap_x(buf, rows, kind):
        return _send(buf.at[0, rows, :], buf.at[1, rows, :], bs.at[kind], br.at[kind], place.xnb)

    first8 = pl.ds(0, 8)
    vector_z = over_z(stz, first8, 0)
    for copy in vector_z:
        copy.start()

    shards = (None, wu_h, wd_h)

    def at(piece, zk, xk):
        third, start, size = PIECES[piece]
        return w.at[third, _ds(BLK * (2 * zk + xk), BLK, 32), pl.ds(start, size)]

    def shard(piece):
        third, start, size = PIECES[piece]
        if third == 0:
            return at(piece, z, x)
        return shards[third].at[:, pl.ds(start, size)]

    def first(piece, i):
        peer = (place.xnb, place.up, place.down)[i]
        return _send(shard(piece), at(piece, z, x), ws.at[piece, i], wr.at[piece, 2 * z + x], peer)

    def begin_z(piece):
        pl.when(z < 3)(lambda: first(piece, 1).start())
        pl.when(z > 0)(lambda: first(piece, 2).start())

    def begin_x(piece):
        first(piece, 0).start()

    def hop(piece, d, i):
        zk = jnp.maximum(z - d, 0) if i < 2 else jnp.minimum(z + d, 3)
        peer = (place.up, place.xnb, place.down, place.xnb)[i]
        there = at(piece, zk, x)
        return _send(there, there, ws.at[piece, 4 * d - 1 + i], wr.at[piece, 2 * zk + x], peer)

    def relay(piece, d):
        @pl.when(z >= d)
        def _():
            hop(piece, d, 0).wait_recv()
            pl.when(z < 3)(lambda: hop(piece, d, 0).start())
            hop(piece, d, 1).start()

        @pl.when(z + d <= 3)
        def _():
            hop(piece, d, 2).wait_recv()
            pl.when(z > 0)(lambda: hop(piece, d, 2).start())
            hop(piece, d, 3).start()

    def over_x(piece, zk):
        there = at(piece, zk, 1 - x)
        _send(there, there, ws.at[piece, 0], wr.at[piece, 2 * zk + 1 - x], place.xnb).wait_recv()

    def complete(piece):
        for k in range(4):
            over_x(piece, place.zs[k])

    def sent(piece):
        first(piece, 0).wait_send()
        pl.when(z < 3)(lambda: first(piece, 1).wait_send())
        pl.when(z > 0)(lambda: first(piece, 2).wait_send())
        for d in range(1, 4):

            @pl.when(z >= d)
            def _(d=d):
                pl.when(z < 3)(lambda: hop(piece, d, 0).wait_send())
                hop(piece, d, 1).wait_send()

            @pl.when(z + d <= 3)
            def _(d=d):
                pl.when(z > 0)(lambda: hop(piece, d, 2).wait_send())
                hop(piece, d, 3).wait_send()

    outs = []

    def out(src, dst):
        copy = pltpu.make_async_copy(src, dst, os_.at[len(outs)])
        copy.start()
        outs.append(copy)
        return len(outs) - 1

    for copy in loads[:4]:
        copy.wait()
    w[0, mine, :] = jnp.concatenate([o[pl.ds(BLK * t, BLK), :] for t in range(4)], axis=1)
    begin_z(0)
    begin_x(0)
    agx = Gather(place, aux, ags.at[1], agr.at[1])
    for s in range(3):
        aux[pl.ds(QUAD * s, SUB), :] = _marks(pictures[...], spots[...], real[...], s)
        agx.start(s)
    loads[4].wait()

    def first_norm(i, _):
        rows = _ds(32 * i, 32, 32)
        own[rows, :] = _norm(tok[rows, :].astype(F32))[0]
        return 0

    lax.fori_loop(0, R // 32, first_norm, 0)
    from_z(stz, first8, 0)
    stx[0, :8, :] = (stz[0, :8, :] + stz[1, :8, :]) + (stz[2, :8, :] + stz[3, :8, :])
    vector_x = swap_x(stx, first8, 0)
    vector_x.start()
    vector_x.wait_recv()
    vecs[...] = stx[0, :8, :] + stx[1, :8, :]
    ag1 = Gather(place, n1a, ags.at[0], agr.at[0])
    for s in range(3):

        def scale_rows(i, _, s=s):
            rows = _ds(QUAD * s + 32 * i, 32, 32)
            n1a[rows, :] = (own[_ds(SUB * s + 32 * i, 32, 32), :] * vecs[0:1, :] + vecs[1:2, :]).astype(BF)
            return 0

        lax.fori_loop(0, 4, scale_rows, 0)
        ag1.start(s)
    relay(0, 1)
    for s in range(3):
        agx.pass_on(s)
    relay(0, 2)
    begin_z(1)
    begin_z(2)
    ag1.pass_on(0)
    relay(0, 3)
    begin_x(1)
    for s in range(3):
        agx.ready(s)
    whole = slice(None)
    count_z = over_z(ccz, whole, 1)
    count_x = swap_x(ccx, whole, 1)
    complete(0)
    for copy in vector_z + [vector_x]:
        copy.wait_send()

    side = _head_rows(W, 0)
    first_half = lax.rem(lax.broadcasted_iota(jnp.int32, (1, 2 * W), 1), HD) < HD // 2
    rs1 = Scatter(place, sb, rb, own, rss.at[0], rsr.at[0])

    def attend_part(s, _):
        ag1.ready(s)
        acc[:, : 3 * W] = _nn(n1a[_ds(QUAD * s, QUAD, QUAD), :], w[0, :, : 3 * W]) + vecs[7:8, : 3 * W]

        def attend_rows(i, _):
            here = _ds(SUB * i, SUB, SUB)
            rows = _ds(QUAD * s + SUB * i, SUB, SUB)
            auxb = aux[rows, :]
            angle = _nn(auxb, tabs[...])
            raw = acc[here, : 2 * W]
            flipped = jnp.where(first_half, -pltpu.roll(raw, 2 * W - 40, 1), pltpu.roll(raw, 40, 1))
            turned = raw * angle[:, : 2 * W] + flipped * angle[:, 2 * W :]
            qkb = turned.astype(BF)
            kqb = pltpu.roll(turned, W, 1)[:, :W].astype(BF)
            vb = acc[here, 2 * W : 3 * W].astype(BF)
            qk[rows, :] = qkb
            v[rows, :] = vb
            scores = _nt(qkb[:, :W], _stack(kqb, side)) * HD ** (-0.5)
            probs = _softmax(scores, _allowed(auxb))
            flat = jnp.concatenate([p.astype(BF) for p in probs], axis=1)
            o[rows, :] = _nn(flat, _stack(vb, side)).astype(BF)

            @pl.when((s == 0) & (i == 0))
            def _():
                relay(1, 1)
                ag1.pass_on(1)

            @pl.when((s == 0) & (i == 1))
            def _():
                relay(1, 2)

            @pl.when((s == 0) & (i == 2))
            def _():
                relay(1, 3)
                begin_x(2)

            pl.when((s == 0) & (i == 3))(lambda: relay(2, 1))

            @pl.when((s == 1) & (i == 2))
            def _():
                relay(2, 2)
                begin_z(3)

            @pl.when((s == 2) & (i == 2))
            def _():
                relay(2, 3)
                begin_x(3)

            return 0

        lax.fori_loop(0, 4, attend_rows, 0)

        @pl.when(s == 0)
        def _():
            complete(1)
            wo[...] = w[0, :, 3 * W :]
            ag1.pass_on(2)


        rs1.post(s, lambda rows: o[rows, :], lambda: wo[...])

        @pl.when(s == 0)
        def _():
            ccz[z] = _nn(jnp.ones((8, G), BF), aux[...])
            for copy in count_z:
                copy.start()

        return 0

    lax.fori_loop(0, 3, attend_part, 0)
    n1_kept = out(n1a, keep_h)
    ag2 = Gather(place, n2, ags.at[2], agr.at[2])

    def second_norm(s, _):
        rs1.wait(s)

        def rows_of(i, _):
            rows = _ds(SUB * s + 32 * i, 32, 32)
            middle = tok[rows, :].astype(F32) + rs1.total(s, i, 32) + vecs[2:3, :]
            mid[rows, :] = middle
            normed, _r = _norm(middle)
            n2[_ds(QUAD * s + 32 * i, 32, 32), :] = (normed * vecs[3:4, :] + vecs[4:5, :]).astype(BF)
            return 0

        lax.fori_loop(0, 4, rows_of, 0)
        ag2.start(s)

        @pl.when(s == 1)
        def _():
            from_z(ccz, whole, 1)
            ccx[0] = (ccz[0] + ccz[1]) + (ccz[2] + ccz[3])
            count_x.start()

        return 0

    lax.fori_loop(0, 3, second_norm, 0)
    teach = tok
    teach_load = pltpu.make_async_copy(teach_h, teach, ls.at[7])
    teach_load.start()
    relay(3, 1)
    ag1.end()
    outs[n1_kept].wait()
    loads[5].wait()
    complete(2)

    def up_part(s, _):
        pl.when(s == 1)(lambda: relay(3, 2))
        pl.when(s == 2)(lambda: relay(3, 3))
        ag2.pass_on(s)
        ag2.ready(s)
        acc[...] = _nn(n2[_ds(QUAD * s, QUAD, QUAD), :], w[1]) + vecs[6:7, :]

        def rows_of(i, _):
            upper = acc[_ds(32 * i, 32, 32), :]
            rows = _ds(QUAD * s + 32 * i, 32, 32)
            gate = 0.5 * jnp.tanh(0.851 * upper) + 0.5
            n1a[rows, :] = (upper * gate).astype(BF)
            gu[rows, :] = (gate + 1.702 * upper * gate * (1.0 - gate)).astype(BF)
            return 0

        lax.fori_loop(0, QUAD // 32, rows_of, 0)
        return 0

    lax.fori_loop(0, 3, up_part, 0)
    act = n1a
    rs1.end()
    loads[6].wait()
    teach_load.wait()

    cols = {0: _ds(HALF * place.near, HALF, 128), 1: _ds(HALF * place.far, HALF, 128)}
    count_x.wait_recv()
    real_count = (ccx[0] + ccx[1])[0:1, 104:105]
    factor = 2.0 * patches / real_count
    downs = [Scatter(place, sb, rb, own, rss.at[1 + j], rsr.at[1 + j], cols[j]) for j in range(2)]
    gathers = [Gather(place, gzb, ags.at[3 + j], agr.at[3 + j], cols[j]) for j in range(2)]
    small[...] = jnp.zeros_like(small)

    for j in range(2):
        for k in ((0, 1), (2, 3))[j]:
            over_x(3, place.zs[k])
        half = (place.near, place.far)[j]

        def down_part(s, _, j=j, half=half):
            downs[j].post(s, lambda rows: act[rows, :], lambda: w[2, _ds(HALF * half, HALF, 128), :])
            return 0

        lax.fori_loop(0, 3, down_part, 0)

        def finish_part(s, sums, j=j):
            downs[j].wait(s)

            def rows_of(i, sums):
                rows = _ds(SUB * s + 32 * i, 32, 32)
                result = mid[rows, cols[j]] + downs[j].total(s, i, 32) + vecs[5:6, cols[j]]
                real = aux[_ds(QUAD * s + 32 * i, 32, 32), 104:105].astype(F32)
                difference = result - teach[rows, cols[j]].astype(F32)
                masked = real * difference
                gout = factor * masked
                low = gout.astype(BF)
                gy[rows, cols[j]] = gout
                teach[rows, cols[j]] = result.astype(BF)
                gzb[_ds(QUAD * s + 32 * i, 32, 32), cols[j]] = low
                return (
                    sums[0] + jnp.sum(masked * difference, axis=0, keepdims=True),
                    sums[1] + jnp.sum(low.astype(F32), axis=0, keepdims=True),
                )

            sums = lax.fori_loop(0, 4, rows_of, sums)
            gathers[j].start(s)
            if j == 1:
                gathers[0].pass_on(s)
            return sums

        zero = jnp.zeros((1, HALF), F32)
        sums = lax.fori_loop(0, 3, finish_part, (zero, zero))
        small[6:7, cols[j]] = sums[0]
        small[5:6, cols[j]] = sums[1]
    res_out = out(teach, res_h)

    def xin_at(chunk, slot, k):
        if chunk == 3:
            return n2.at[pl.ds(BLK * k, BLK), pl.ds(256, 256)]
        return xin.at[slot, k, :, pl.ds(0, 1024)] if chunk == 0 else xin.at[slot, k]

    def zin_at(chunk, slot, i):
        if chunk == 3:
            return n2.at[pl.ds(BLK * i, BLK), pl.ds(512, 256)]
        return zin.at[slot, i, :, pl.ds(0, 1024)] if chunk == 0 else zin.at[slot, i]

    def g_rows(chunk, slot, rows):
        if chunk == 3:
            return n2.at[rows, pl.ds(0, 256)]
        return gb.at[slot, rows, pl.ds(0, 1024)] if chunk == 0 else gb.at[slot, rows, :]

    def to_x(chunk, slot, k):
        rows = _ds(BLK * (2 * place.zs[k] + 1 - x), BLK, 32)
        return _send(
            g_rows(chunk, slot, rows), xin_at(chunk, slot, k), xs.at[chunk, k], xr.at[chunk, k], place.xnb
        )

    def block(k):
        return _ds(BLK * (2 * place.zs[k] + x), BLK, 32)

    def to_z(chunk, slot, i):
        k, peer = ((3, place.zn[1]), (1, place.zn[1]), (2, place.zn[2]))[i]
        return _send(g_rows(chunk, slot, block(k)), zin_at(chunk, slot, i), zs.at[chunk, i], zr.at[chunk, i], peer)

    def tile(slot, lhs, rhs, half):
        rows = _ds(HALF * half, HALF, 128)
        for part in range(2):
            cols = pl.ds(HALF * part, HALF)
            gb[slot, rows, cols] = _tn(lhs[:, rows], rhs[:, cols]).astype(BF)

    def add_x(chunk, slot, i):
        k = (3, 1)[i]
        to_x(chunk, slot, k).wait_recv()
        ref = g_rows(chunk, slot, block(k))
        ref[...] = (ref[...].astype(F32) + xin_at(chunk, slot, k)[...].astype(F32)).astype(BF)
        to_z(chunk, slot, i).start()

    def combine(chunk, slot):
        to_x(chunk, slot, 2).wait_recv()
        to_z(chunk, slot, 0).wait_recv()
        ref = g_rows(chunk, slot, block(2))
        ref[...] = (
            (ref[...].astype(F32) + xin_at(chunk, slot, 2)[...].astype(F32)) + zin_at(chunk, slot, 0)[...].astype(F32)
        ).astype(BF)
        to_z(chunk, slot, 2).start()

    def fin_cols(chunk):
        return {0: pl.ds(0, 1024), 3: pl.ds(1024, 256)}.get(chunk, pl.ds(0, D))

    def add_own(chunk, slot):
        to_x(chunk, slot, 0).wait_recv()
        fin[:, fin_cols(chunk)] = g_rows(chunk, slot, block(0))[...].astype(F32) + xin_at(chunk, slot, 0)[...].astype(F32)

    def add_z(chunk, slot):
        to_z(chunk, slot, 1).wait_recv()
        to_z(chunk, slot, 2).wait_recv()
        cols = fin_cols(chunk)
        fin[:, cols] = fin[:, cols] + (
            zin_at(chunk, slot, 1)[...].astype(F32) + zin_at(chunk, slot, 2)[...].astype(F32)
        )

    for s in range(3):
        gathers[0].ready(s)
    tile(0, gzb, act, place.near)
    to_x(2, 0, 1).start()
    to_x(2, 0, 0).start()

    for copy in downs:
        copy.end()
    rs3 = Scatter(place, sb, rb, own, rss.at[3], rsr.at[3])
    up_total = jnp.zeros((1, F), F32)
    for s in range(3):
        gathers[1].pass_on(s)
    gathers[1].ready(0)
    for s in range(3):
        acc[...] = _nn(gzb[pl.ds(QUAD * s, QUAD), :], w[2])

        def gate_rows(i, total, s=s):
            rows = _ds(QUAD * s + 32 * i, 32, 32)
            low = (acc[_ds(32 * i, 32, 32), :] * gu[rows, :].astype(F32)).astype(BF)
            gu[rows, :] = low
            return total + jnp.sum(low.astype(F32), axis=0, keepdims=True)

        up_total = lax.fori_loop(0, QUAD // 32, gate_rows, up_total)
        rs3.post(s, lambda rows: gu[rows, :], lambda: w[1])
        if s == 0:
            for t in (1, 2):
                gathers[1].ready(t)
            tile(0, gzb, act, place.far)
            to_x(2, 0, 3).start()
            to_x(2, 0, 2).start()
    for gather in gathers:
        gather.end()
    for peer in (place.core, place.ynb):
        pl.semaphore_signal(gfree, inc=1, device_id=peer, device_id_type=MESH_ID)
    n1_back = pltpu.make_async_copy(keep_h, n1a, ls.at[8])
    n1_back.start()
    outs[res_out].wait()
    tok_back = pltpu.make_async_copy(tok_h, tok, ls.at[9])
    tok_back.start()
    small[pl.ds(8 + place.fs, 1), :] = up_total
    add_x(2, 0, 1)
    tile(1, n2, gu, place.far)
    to_x(1, 1, 3).start()
    to_x(1, 1, 2).start()
    pl.semaphore_wait(gfree, 2)
    ag3 = Gather(place, gzb, ags.at[5], agr.at[5])

    def norm_rows(s, i, sums, values, gain, terms):
        rows = _ds(SUB * s + 32 * i, 32, 32)
        grad = terms.total(s, i, 32)
        normed, reciprocal = _norm(values[rows, :].astype(F32))
        scaled = grad * gain
        back = (
            scaled
            - jnp.mean(scaled, axis=-1, keepdims=True)
            - normed * jnp.mean(scaled * normed, axis=-1, keepdims=True)
        ) * reciprocal
        total = gy[rows, :] + back
        gy[rows, :] = total
        pair = (
            sums[0] + jnp.sum(grad * normed, axis=0, keepdims=True),
            sums[1] + jnp.sum(grad, axis=0, keepdims=True),
        )
        return total, pair

    zero = jnp.zeros((1, D), F32)

    def second_back(s, sums):
        rs3.wait(s)

        def rows_of(i, sums):
            total, pair = norm_rows(s, i, sums[:2], mid, vecs[3:4, :], rs3)
            low = total.astype(BF)
            gzb[_ds(QUAD * s + 32 * i, 32, 32), :] = low
            return pair + (sums[2] + jnp.sum(low.astype(F32), axis=0, keepdims=True),)

        sums = lax.fori_loop(0, 4, rows_of, sums)
        ag3.start(s)
        return sums

    gain2, shift2, outb = lax.fori_loop(0, 3, second_back, (zero, zero, zero))
    small[2:3, :] = outb
    small[3:4, :] = gain2
    small[4:5, :] = shift2
    tile(1, n2, gu, place.near)
    to_x(1, 1, 1).start()
    to_x(1, 1, 0).start()
    ag2.end()
    for peer in (place.xnb,) + place.zn[1:3]:
        pl.semaphore_signal(nfree, inc=1, device_id=peer, device_id_type=MESH_ID)
    add_x(2, 0, 0)
    add_own(2, 0)
    rs3.end()
    rs4 = Scatter(place, sb, rb, own, rss.at[4], rsr.at[4])

    def attend_back(s, total):
        ag3.pass_on(s)
        ag3.ready(s)

        @pl.when(s == 2)
        def _():
            for half in (place.far, place.near):
                rows = _ds(HALF * half, HALF, 128)
                n2[rows, pl.ds(0, 256)] = _tn(gzb[:, rows], o[:, W - 256 :]).astype(BF)
            pl.semaphore_wait(nfree, 3)
            for k in (3, 2, 1, 0):
                to_x(3, 0, k).start()

        acc[:, :W] = _nn(gzb[_ds(QUAD * s, QUAD, QUAD), :], wo[...])

        def attend_rows(i, total):
            rows = _ds(QUAD * s + SUB * i, SUB, SUB)
            auxb = aux[rows, :]
            qkb = qk[rows, :]
            kqb = pltpu.roll(qkb.astype(F32), W, 1)[:, :W].astype(BF)
            vb = v[rows, :]
            gob = acc[_ds(SUB * i, SUB, SUB), :W].astype(BF)
            keys = _stack(kqb, side)
            scores = _nt(qkb[:, :W], keys) * HD ** (-0.5)
            probs = _softmax(scores, _allowed(auxb))
            gprobs = _nt(gob, _stack(vb, side))
            gscores = []
            for h in range(HEADS_LOCAL):
                gp = gprobs[:, 128 * h : 128 * h + 128]
                delta = jnp.sum(gp * probs[h], axis=-1, keepdims=True)
                gscores.append((probs[h] * (gp - delta)).astype(BF))
            flat = jnp.concatenate(gscores, axis=1)
            tall = jnp.concatenate(gscores, axis=0)
            ptall = jnp.concatenate([p.astype(BF) for p in probs], axis=0)
            gqk = jnp.concatenate([_nn(flat, keys), _tn(tall, _stack(qkb[:, :W], side))], axis=1) * HD ** (-0.5)
            gv = _tn(ptall, _stack(gob, side))
            angle = _nn(auxb, tabs[...])
            sined = gqk * angle[:, 2 * W :]
            shifted = jnp.where(first_half, pltpu.roll(sined, 2 * W - 40, 1), -pltpu.roll(sined, 40, 1))
            turned = gqk * angle[:, : 2 * W] + shifted
            low = jnp.concatenate([turned, gv], axis=1).astype(BF)
            gu[rows, : 3 * W] = low
            return total + jnp.sum(low.astype(F32), axis=0, keepdims=True)

        total = lax.fori_loop(0, 4, attend_rows, total)
        rs4.post(s, lambda rows: gu[rows, : 3 * W], lambda: w[0, :, : 3 * W])


        @pl.when(s == 0)
        def _():
            combine(2, 0)
            pl.semaphore_signal(xfree, inc=1, device_id=place.xnb, device_id_type=MESH_ID)

        pl.when(s == 1)(lambda: add_x(1, 1, 0))

        @pl.when(s == 2)
        def _():
            combine(1, 1)
            add_x(1, 1, 1)

        return total

    mix_total = lax.fori_loop(0, 3, attend_back, jnp.zeros((1, 3 * W), F32))
    small[pl.ds(12 + place.fs, 1), : 3 * W] = mix_total

    for k in range(4):
        to_x(2, 0, k).wait_send()
    for i in range(3):
        to_z(2, 0, i).wait_send()
    n1_back.wait()

    def last_tile(half):
        rows = _ds(HALF * half, HALF, 128)
        gb[0, rows, : 3 * W] = _tn(n1a[:, rows], gu[:, : 3 * W]).astype(BF)
        gb[0, rows, 3 * W : 1024] = _tn(gzb[:, rows], o[:, : W - 256]).astype(BF)

    last_tile(place.far)
    pl.semaphore_wait(xfree, 1)
    to_x(0, 0, 3).start()
    to_x(0, 0, 2).start()
    last_tile(place.near)
    add_z(2, 0)
    down_out = out(fin, gd_h)
    for peer in place.zn[1:3]:
        pl.semaphore_signal(zfree, inc=1, device_id=peer, device_id_type=MESH_ID)

    tok_back.wait()

    def first_back(s, sums):
        rs4.wait(s)

        pl.when(s == 1)(lambda: add_x(3, 0, 0))
        return lax.fori_loop(0, 4, lambda i, t: norm_rows(s, i, t, tok, vecs[0:1, :], rs4)[1], sums)

    gain1, shift1 = lax.fori_loop(0, 3, first_back, (zero, zero))
    out(gy, gtok_h)
    small[0:1, :] = gain1
    small[1:2, :] = shift1

    sta[place.fs] = small[...]
    there = sta.at[place.fs]
    peers = (place.core, place.ynb, place.diagonal)
    small_f = [_send(there, there, as_.at[3, k], ar.at[3, place.fs], peer) for k, peer in enumerate(peers)]
    for copy in small_f:
        copy.start()
    outs[down_out].wait()
    for k, peer in enumerate(peers):
        there = sta.at[place.mates[k]]
        _send(there, there, as_.at[3, k], ar.at[3, place.mates[k]], peer).wait_recv()
    stx[0] = (sta[0] + sta[1]) + (sta[2] + sta[3])
    small_x = swap_x(stx, whole, 2)
    small_x.start()
    to_x(0, 0, 1).start()
    to_x(0, 0, 0).start()
    pl.semaphore_wait(zfree, 2)
    add_x(0, 0, 0)
    combine(3, 0)
    add_x(3, 0, 1)
    add_own(1, 1)
    add_z(1, 1)
    up_out = out(fin, gu_h)
    small_x.wait_recv()
    stz[z] = stx[0] + stx[1]
    small_z = over_z(stz, whole, 2)
    for copy in small_z:
        copy.start()
    combine(0, 0)
    add_x(0, 0, 1)
    outs[up_out].wait()
    add_own(3, 0)
    add_z(3, 0)
    add_own(0, 0)
    from_z(stz, whole, 2)
    total = (stz[0] + stz[1]) + (stz[2] + stz[3])
    small_o[...] = total
    loss_o[...] = jnp.sum(total[6:7, :], axis=-1, keepdims=True) / (real_count * D)
    add_z(0, 0)
    out(fin, ga_h)

    for piece in range(4):
        sent(piece)
    agx.end()
    ag3.end()
    rs4.end()
    for copy in count_z + [count_x] + small_f + [small_x] + small_z:
        copy.wait_send()
    for chunk, slot in ((1, 1), (0, 0), (3, 0)):
        for k in range(4):
            to_x(chunk, slot, k).wait_send()
        for i in range(3):
            to_z(chunk, slot, i).wait_send()
    for i, copy in enumerate(outs):
        if i not in (n1_kept, res_out, down_out, up_out):
            copy.wait()


TOTAL = [0]


def layer_call(*operands):
    any_, vm = pl.ANY, pltpu.VMEM
    outs = [
        ((R, D), BF, any_),
        ((R, D), F32, any_),
        ((BLK, D), F32, any_),
        ((BLK, D), F32, any_),
        ((BLK, D), F32, any_),
        ((16, D), F32, vm),
        ((1, 1), F32, vm),
        ((G, D), BF, any_),
    ]
    dma = pltpu.SemaphoreType.DMA
    scratch = [
        vm((R, D), BF),
        vm((G, 128), BF),
        vm((3, D, D), BF),
        vm((D, W), BF),
        vm((G, D), BF),
        vm((G, D), BF),
        vm((G, F), BF),
        vm((G, D), BF),
        vm((G, 2 * W), BF),
        vm((G, W), BF),
        vm((G, W), BF),
        vm((QUAD, D), F32),
        vm((R, D), F32),
        vm((R, D), F32),
        vm((R, D), F32),
        vm((5, SUB, D), BF),
        vm((3, 3, SUB, D), BF),
        vm((2, D, D), BF),
        vm((2, 4, BLK, D), BF),
        vm((2, 3, BLK, D), BF),
        vm((BLK, D), F32),
        vm((8, D), F32),
        vm((16, D), F32),
        vm((4, 8, 128), F32),
        vm((2, 8, 128), F32),
        vm((4, 16, D), F32),
        vm((2, 16, D), F32),
        vm((4, 16, D), F32),
        dma((4, 15)),
        dma((4, 8)),
        dma((6, 9)),
        dma((6, 9)),
        dma((5, 9)),
        dma((5, 9)),
        dma((4, 4)),
        dma((4, 4)),
        dma((4, 3)),
        dma((4, 3)),
        dma((4, 4)),
        dma((4, 4)),
        dma((3,)),
        dma((3,)),
        dma((10,)),
        dma((8,)),
        pltpu.SemaphoreType.REGULAR,
        pltpu.SemaphoreType.REGULAR,
        pltpu.SemaphoreType.REGULAR,
        pltpu.SemaphoreType.REGULAR,
    ]
    ins = [any_] * 6 + [vm] * 12
    return pl.pallas_call(
        layer_kernel,
        out_shape=[jax.ShapeDtypeStruct(shape, dtype) for shape, dtype, _ in outs],
        in_specs=[pl.BlockSpec(memory_space=space) for space in ins],
        out_specs=[pl.BlockSpec(memory_space=space) for _, _, space in outs],
        scratch_shapes=scratch,
        compiler_params=pltpu.CompilerParams(
            collective_id=1, has_side_effects=True, vmem_limit_bytes=64 << 20
        ),
        name="layer",
    )(*operands)


def turn_tables():
    import ml_dtypes

    quarter = HD // 4
    frequency = (1.0 / np.float32(10000.0) ** (np.arange(quarter, dtype=np.float32) * 4.0 / HD)).astype(np.float32)
    angle = (np.arange(16, dtype=np.float32)[:, None] * frequency[None, :]).astype(np.float32)
    cosine, sine = np.cos(angle.astype(np.float64)), np.sin(angle.astype(np.float64))
    zero = np.zeros_like(cosine)

    def head(first, second):
        top = np.concatenate([first, zero, second, zero], axis=1)
        low = np.concatenate([zero, first, zero, second], axis=1)
        return np.tile(np.concatenate([top, low], axis=0), (1, 2 * HEADS_LOCAL))

    full = np.concatenate([head(cosine, cosine), head(sine, sine)], axis=1).astype(np.float32)
    terms = []
    rest = full
    for _ in range(3):
        term = rest.astype(ml_dtypes.bfloat16)
        terms.append(term)
        rest = rest - term.astype(np.float32)
    terms.append(np.zeros((32, full.shape[1]), ml_dtypes.bfloat16))
    return jnp.asarray(np.concatenate(terms, axis=0))


def finish_kernel(
    res_i, gtok_i, gd_i, gu_i, ga_i, small, loss_i,
    res_o, loss_o, gtok_o, fg_o, fs_o, mix_o, mb_o, vb_o, out_o, ob_o, sg_o, ss_o, up_o, ub_o, down_o, db_o,
    ga, gtok, res, gd, gu, sems,
):
    dp = lax.axis_index("dp")
    copies = [
        pltpu.make_async_copy(src, dst, sems.at[i])
        for i, (src, dst) in enumerate(
            [
                (gtok_i, gtok),
                (ga_i, ga),
                (res_i, res),
                (gd_i, gd),
                (gu_i, gu),
                (gtok, gtok_o),
                (res, res_o),
                (gd, down_o),
                (gu, up_o),
            ]
        )
    ]
    for copy in copies[:5]:
        copy.start()
    loss_o[...] = loss_i[...]
    pieces = pltpu.roll(small[:8, :], lax.rem(D - BLK * dp + D, D), 1)[:, :BLK]
    for i, ref in ((0, fg_o), (1, fs_o), (2, ob_o), (3, sg_o), (4, ss_o), (5, db_o)):
        ref[...] = pieces[i : i + 1, :].reshape(BLK)
    ub_o[...] = small[pl.ds(8 + lax.div(dp, 2), 1), _ds(640 * lax.rem(dp, 2), 640, 128)].reshape(640)
    row = small[pl.ds(12 + lax.rem(dp, 4), 1), :]
    mb_o[...] = pltpu.roll(row, lax.rem(D - W * lax.div(dp, 4), D), 1)[:, :W].reshape(W)
    row = small[pl.ds(12 + lax.div(dp, 2), 1), :]
    vb_o[...] = pltpu.roll(row, 2 * W - BLK * lax.rem(dp, 2), 1)[:, :BLK].reshape(BLK)
    copies[0].wait()
    copies[5].start()
    for i in (2, 3, 4):
        copies[i].wait()
        copies[i + 4].start()
    copies[1].wait()
    for t in range(3):
        mix_o[t] = ga[:, W * t : W * t + W]
    out_o[...] = ga[:, 3 * W :]
    for copy in copies[5:]:
        copy.wait()


def finish_call(*operands):
    any_, vm = pl.ANY, pltpu.VMEM
    outs = [
        ((R, D), BF, any_),
        ((1, 1), F32, vm),
        ((R, D), F32, any_),
        ((BLK,), F32, vm),
        ((BLK,), F32, vm),
        ((3, BLK, W), F32, vm),
        ((W,), F32, vm),
        ((BLK,), F32, vm),
        ((BLK, W), F32, vm),
        ((BLK,), F32, vm),
        ((BLK,), F32, vm),
        ((BLK,), F32, vm),
        ((BLK, D), F32, any_),
        ((640,), F32, vm),
        ((BLK, D), F32, any_),
        ((BLK,), F32, vm),
    ]
    ins = [any_] * 5 + [vm] * 2
    return pl.pallas_call(
        finish_kernel,
        out_shape=[jax.ShapeDtypeStruct(shape, dtype) for shape, dtype, _ in outs],
        in_specs=[pl.BlockSpec(memory_space=space) for space in ins],
        out_specs=[pl.BlockSpec(memory_space=space) for _, _, space in outs],
        scratch_shapes=[
            vm((BLK, D), F32),
            vm((R, D), F32),
            vm((R, D), BF),
            vm((BLK, D), F32),
            vm((BLK, D), F32),
            pltpu.SemaphoreType.DMA((9,)),
        ],
        compiler_params=pltpu.CompilerParams(vmem_limit_bytes=62 << 20),
        name="finish",
    )(*operands)


def on_device_fast(
    tokens,
    teacher,
    picture,
    places,
    validity,
    first_gain,
    first_shift,
    mixer_weight,
    mixer_bias,
    output_weight,
    output_bias,
    second_gain,
    second_shift,
    upward_weight,
    upward_bias,
    downward_weight,
    downward_bias,
):
    TOTAL[0] = float(tokens.shape[0] * lax.axis_size("dp") * lax.axis_size("fsdp"))
    res, gtok, gd, gup, ga, small, loss, _ = layer_call(
        tokens,
        teacher,
        mixer_weight.transpose(1, 0, 2),
        output_weight.T,
        upward_weight,
        downward_weight.T,
        first_gain,
        first_shift,
        output_bias,
        second_gain,
        second_shift,
        downward_bias,
        upward_bias,
        mixer_bias,
        picture.reshape(3, ROW_PATCHES),
        places.T,
        validity.reshape(3, ROW_PATCHES),
        turn_tables(),
    )
    (res, loss, gtok, fg, fs, mix, mb, vb, out, ob, sg, ss, up, ub, down, db) = finish_call(
        res, gtok, gd, gup, ga, small, loss
    )
    return (res, loss.reshape(()), gtok, fg, fs, mix.transpose(1, 0, 2), mb, vb, out.T, ob, sg, ss, up, ub, down.T, db)


def solution(mesh):
    fast = mesh.shape["dp"] == 8 and mesh.shape["fsdp"] == 4
    return jax.shard_map(
        on_device_fast if fast else on_device,
        mesh=mesh,
        in_specs=(
            P(("dp", "fsdp"), None),
            P(("dp", "fsdp"), None),
            P(("dp", "fsdp")),
            P(("dp", "fsdp"), None),
            P(("dp", "fsdp")),
            P("dp"),
            P("dp"),
            P("dp", None, "fsdp"),
            P("dp"),
            P("fsdp", "dp"),
            P("dp"),
            P("dp"),
            P("dp"),
            P("dp", "fsdp"),
            P("dp"),
            P("fsdp", "dp"),
            P("dp"),
        ),
        out_specs=(
            P(("dp", "fsdp"), None),
            P(),
            P(("dp", "fsdp"), None),
            P("dp"),
            P("dp"),
            P("dp", None, "fsdp"),
            P("dp"),
            P("dp"),
            P("fsdp", "dp"),
            P("dp"),
            P("dp"),
            P("dp"),
            P("dp", "fsdp"),
            P("dp"),
            P("fsdp", "dp"),
            P("dp"),
        ),
        check_vma=False,
    )
```

```python
import numpy as np
import jax
import jax.numpy as jnp
from jax import lax
from jax.experimental import pallas as pl
from jax.experimental.pallas import tpu as pltpu
from jax.sharding import PartitionSpec as P

D = 1280
HD = 80
FF = 5120
ROW_PATCHES = 128
MB = 3


EPSILON = 1e-06


def norm_forward(values, scaler, offset):
    average = jnp.mean(values, axis=-1, keepdims=True)
    centered = values - average
    reciprocal = lax.rsqrt(jnp.mean(centered * centered, axis=-1, keepdims=True) + EPSILON)
    normed = centered * reciprocal
    return (normed * scaler.astype(jnp.float32) + offset.astype(jnp.float32), normed, reciprocal)


def norm_backward(gradient, normed, reciprocal, scaler):
    scaled = gradient * scaler.astype(jnp.float32)
    adjusted = (
        scaled
        - jnp.mean(scaled, axis=-1, keepdims=True)
        - normed * jnp.mean(scaled * normed, axis=-1, keepdims=True)
    )
    return (adjusted * reciprocal, jnp.sum(gradient * normed, axis=0), jnp.sum(gradient, axis=0))


def tables(places):
    quarter = HD // 4
    frequency = 1.0 / 10000.0 ** (jnp.arange(quarter, dtype=jnp.float32) * 4.0 / HD)
    row_angle = places[:, 0:1].astype(jnp.float32) * frequency
    col_angle = places[:, 1:2].astype(jnp.float32) * frequency
    angle_all = jnp.concatenate([row_angle, col_angle, row_angle, col_angle], axis=-1)
    return (jnp.cos(angle_all)[:, None, :], jnp.sin(angle_all)[:, None, :])


def rotate(values, cosine, sine):
    halfway = HD // 2
    flipped = jnp.concatenate([-values[..., halfway:], values[..., :halfway]], axis=-1)
    return values * cosine + flipped * sine


def unrotate(gradient, cosine, sine):
    halfway = HD // 2
    shifted = gradient * sine
    return gradient * cosine + jnp.concatenate(
        [shifted[..., halfway:], -shifted[..., :halfway]], axis=-1
    )


def allowed_mask(picture, validity):
    picture_rows = picture.reshape(-1, ROW_PATCHES)
    occupancy_flags = validity.reshape(-1, ROW_PATCHES) > 0
    shared_picture_mask = picture_rows[:, :, None] == picture_rows[:, None, :]
    self_pairs = jnp.eye(ROW_PATCHES, dtype=bool)[None]
    return (shared_picture_mask & occupancy_flags[:, None, :] | self_pairs)[:, None]


def scores_of(query, key_rows, permitted_pairs):
    products = jnp.einsum(
        "bqhd,bkhd->bhqk", query, key_rows, preferred_element_type=jnp.float32
    ) * HD ** (-0.5)
    return jnp.where(permitted_pairs, products, -1e30)


def attend(query, key_rows, value_rows, permitted_pairs):
    scores = scores_of(query, key_rows, permitted_pairs)
    maximum = jnp.max(scores, axis=-1, keepdims=True)
    log_total = maximum + jnp.log(jnp.sum(jnp.exp(scores - maximum), axis=-1, keepdims=True))
    probs = jnp.exp(scores - log_total).astype(jnp.bfloat16)
    attended = jnp.einsum("bhqk,bkhd->bqhd", probs, value_rows, preferred_element_type=jnp.float32)
    return (attended, log_total)


def attend_back(grad_attended, query, key_rows, value_rows, permitted_pairs, log_total):
    scores = scores_of(query, key_rows, permitted_pairs)
    probs = jnp.exp(scores - log_total)
    grad_probs = jnp.einsum(
        "bqhd,bkhd->bhqk", grad_attended, value_rows, preferred_element_type=jnp.float32
    )
    delta = jnp.sum(grad_probs * probs, axis=-1, keepdims=True)
    grad_scores = (probs * (grad_probs - delta)).astype(jnp.bfloat16)
    scaling = HD ** (-0.5)
    grad_query = (
        jnp.einsum("bhqk,bkhd->bqhd", grad_scores, key_rows, preferred_element_type=jnp.float32)
        * scaling
    )
    grad_key = (
        jnp.einsum("bhqk,bqhd->bkhd", grad_scores, query, preferred_element_type=jnp.float32)
        * scaling
    )
    grad_value = jnp.einsum(
        "bhqk,bqhd->bkhd",
        probs.astype(jnp.bfloat16),
        grad_attended,
        preferred_element_type=jnp.float32,
    )
    return (grad_query, grad_key, grad_value)


def quick_gelu_grad(grad_active, upper):
    sigmoid_up = jax.nn.sigmoid(1.702 * upper)
    return (grad_active * (sigmoid_up + 1.702 * upper * sigmoid_up * (1.0 - sigmoid_up))).astype(
        jnp.bfloat16
    )


def own_slice(vector, data_index, data_ways):
    length = vector.shape[0] // data_ways
    return lax.dynamic_slice_in_dim(vector, data_index * length, length, 0)


def on_device(
    tokens,
    teacher,
    picture,
    places,
    validity,
    first_gain,
    first_shift,
    mixer_weight,
    mixer_bias,
    output_weight,
    output_bias,
    second_gain,
    second_shift,
    upward_weight,
    upward_bias,
    downward_weight,
    downward_bias,
):
    data_ways = lax.axis_size("dp")
    split_ways = lax.axis_size("fsdp")
    member = lax.axis_index("fsdp")
    data_index = lax.axis_index("dp")
    occupancy_flags = validity.astype(jnp.float32)
    token_tally = lax.psum(jnp.sum(occupancy_flags), ("dp", "fsdp"))
    factor = tokens.shape[0] * data_ways * split_ways / token_tally
    (
        mixer_local,
        output_local,
        upward_local,
        downward_local,
        gain_one,
        shift_one,
        mixer_shift,
        output_shift,
        gain_two,
        shift_two,
        upward_shift,
        downward_shift,
    ) = (
        lax.all_gather(mixer_weight, "dp", axis=0, tiled=True),
        lax.all_gather(output_weight, "dp", axis=1, tiled=True),
        lax.all_gather(upward_weight, "dp", axis=0, tiled=True),
        lax.all_gather(downward_weight, "dp", axis=1, tiled=True),
        lax.all_gather(first_gain, "dp", axis=0, tiled=True),
        lax.all_gather(first_shift, "dp", axis=0, tiled=True),
        lax.all_gather(mixer_bias, "dp", axis=0, tiled=True),
        lax.all_gather(output_bias, "dp", axis=0, tiled=True),
        lax.all_gather(second_gain, "dp", axis=0, tiled=True),
        lax.all_gather(second_shift, "dp", axis=0, tiled=True),
        lax.all_gather(upward_bias, "dp", axis=0, tiled=True),
        lax.all_gather(downward_bias, "dp", axis=0, tiled=True),
    )
    width_local = output_local.shape[0]
    heads_local = width_local // HD
    hidden_local = upward_local.shape[1]
    mixer_flat = mixer_local.reshape(D, 3 * width_local)
    mixer_piece = lax.dynamic_slice_in_dim(
        mixer_shift.reshape(3, D), member * width_local, width_local, 1
    )
    mixer_piece = mixer_piece.reshape(3 * width_local).astype(jnp.float32)
    upward_piece = lax.dynamic_slice_in_dim(
        upward_shift, member * hidden_local, hidden_local, 0
    ).astype(jnp.float32)
    packed_rows = tokens.shape[0] // MB
    errors = jnp.zeros((), jnp.float32)
    matrix_sums = None
    small_sums = None
    results = []
    input_grads = []
    for micro in range(MB):
        start_offset = micro * packed_rows
        inputs = tokens[start_offset : start_offset + packed_rows].astype(jnp.float32)
        target = teacher[start_offset : start_offset + packed_rows].astype(jnp.float32)
        occupied_rows = occupancy_flags[start_offset : start_offset + packed_rows]
        picture_rows = picture[start_offset : start_offset + packed_rows]
        local_picture = (picture_rows - picture_rows[0]).astype(jnp.bfloat16)
        place_rows = places[start_offset : start_offset + packed_rows].astype(jnp.bfloat16)
        live_marks = validity[start_offset : start_offset + packed_rows].astype(jnp.bfloat16)
        shifted_one, normed_one, recip_one = norm_forward(inputs, gain_one, shift_one)
        lowered_one = shifted_one.astype(jnp.bfloat16)
        group_one, group_picture, group_places, group_live = (
            lax.all_gather(lowered_one, "fsdp", axis=0, tiled=True),
            lax.all_gather(local_picture, "fsdp", axis=0, tiled=True),
            lax.all_gather(place_rows, "fsdp", axis=0, tiled=True),
            lax.all_gather(live_marks, "fsdp", axis=0, tiled=True),
        )
        group_rows = group_one.shape[0]
        mixed = jnp.dot(group_one, mixer_flat, preferred_element_type=jnp.float32) + mixer_piece
        mixed = mixed.reshape(group_rows, 3, heads_local, HD)
        cosine, sine = tables(group_places)
        query = (
            rotate(mixed[:, 0], cosine, sine)
            .astype(jnp.bfloat16)
            .reshape(-1, ROW_PATCHES, heads_local, HD)
        )
        key_rows = (
            rotate(mixed[:, 1], cosine, sine)
            .astype(jnp.bfloat16)
            .reshape(-1, ROW_PATCHES, heads_local, HD)
        )
        value_rows = mixed[:, 2].astype(jnp.bfloat16).reshape(-1, ROW_PATCHES, heads_local, HD)
        permitted_pairs = allowed_mask(group_picture, group_live)
        attended, log_total = attend(query, key_rows, value_rows, permitted_pairs)
        attended = attended.reshape(group_rows, width_local).astype(jnp.bfloat16)
        branch = lax.psum_scatter(
            jnp.dot(attended, output_local, preferred_element_type=jnp.float32).astype(
                jnp.bfloat16
            ),
            "fsdp",
            scatter_dimension=0,
            tiled=True,
        ).astype(jnp.float32)
        middle = inputs + branch + output_shift.astype(jnp.float32)
        shifted_two, normed_two, recip_two = norm_forward(middle, gain_two, shift_two)
        lowered_two = shifted_two.astype(jnp.bfloat16)
        group_two = lax.all_gather(lowered_two, "fsdp", axis=0, tiled=True)
        upper = jnp.dot(group_two, upward_local, preferred_element_type=jnp.float32) + upward_piece
        active = (upper * jax.nn.sigmoid(1.702 * upper)).astype(jnp.bfloat16)
        lowered = lax.psum_scatter(
            jnp.dot(active, downward_local, preferred_element_type=jnp.float32).astype(
                jnp.bfloat16
            ),
            "fsdp",
            scatter_dimension=0,
            tiled=True,
        ).astype(jnp.float32)
        outputs = middle + lowered + downward_shift.astype(jnp.float32)
        difference = outputs - target
        masked = occupied_rows[:, None] * difference
        errors = errors + jnp.sum(masked * difference)
        grad_out = 2.0 * factor * masked
        grad_low = grad_out.astype(jnp.bfloat16)
        down_bias_term = jnp.sum(grad_low.astype(jnp.float32), axis=0)
        group_grad = lax.all_gather(grad_low, "fsdp", axis=0, tiled=True)
        g_down = jnp.einsum("rf,rd->fd", active, group_grad, preferred_element_type=jnp.float32)
        grad_active = jnp.einsum(
            "rd,fd->rf", group_grad, downward_local, preferred_element_type=jnp.float32
        )
        grad_upper = quick_gelu_grad(grad_active, upper)
        g_up = jnp.einsum("rd,rf->df", group_two, grad_upper, preferred_element_type=jnp.float32)
        up_bias_term = lax.dynamic_update_slice_in_dim(
            jnp.zeros((FF,), jnp.float32),
            jnp.sum(grad_upper.astype(jnp.float32), axis=0),
            member * hidden_local,
            0,
        )
        grad_two = lax.psum_scatter(
            jnp.einsum(
                "rf,df->rd", grad_upper, upward_local, preferred_element_type=jnp.float32
            ).astype(jnp.bfloat16),
            "fsdp",
            scatter_dimension=0,
            tiled=True,
        ).astype(jnp.float32)
        back_two, g_gain_two, g_shift_two = norm_backward(grad_two, normed_two, recip_two, gain_two)
        grad_middle = grad_out + back_two
        grad_branch = grad_middle.astype(jnp.bfloat16)
        out_bias_term = jnp.sum(grad_branch.astype(jnp.float32), axis=0)
        group_branch = lax.all_gather(grad_branch, "fsdp", axis=0, tiled=True)
        g_output = jnp.einsum(
            "rd,re->de", attended, group_branch, preferred_element_type=jnp.float32
        )
        grad_attended = jnp.einsum(
            "re,de->rd", group_branch, output_local, preferred_element_type=jnp.float32
        )
        grad_attended = grad_attended.astype(jnp.bfloat16).reshape(-1, ROW_PATCHES, heads_local, HD)
        grad_query, grad_key, grad_value = attend_back(
            grad_attended, query, key_rows, value_rows, permitted_pairs, log_total
        )
        grad_mixed = jnp.stack(
            [
                unrotate(grad_query.reshape(group_rows, heads_local, HD), cosine, sine),
                unrotate(grad_key.reshape(group_rows, heads_local, HD), cosine, sine),
                grad_value.reshape(group_rows, heads_local, HD),
            ],
            axis=1,
        )
        grad_mixed = grad_mixed.reshape(group_rows, 3 * width_local).astype(jnp.bfloat16)
        g_mixer = jnp.einsum("rd,re->de", group_one, grad_mixed, preferred_element_type=jnp.float32)
        g_mixer = g_mixer.reshape(D, 3, width_local)
        mixer_bias_term = lax.dynamic_update_slice_in_dim(
            jnp.zeros((3, D), jnp.float32),
            jnp.sum(grad_mixed.astype(jnp.float32), axis=0).reshape(3, width_local),
            member * width_local,
            1,
        )
        mixer_bias_term = mixer_bias_term.reshape(3 * D)
        grad_one = lax.psum_scatter(
            jnp.einsum(
                "re,de->rd", grad_mixed, mixer_flat, preferred_element_type=jnp.float32
            ).astype(jnp.bfloat16),
            "fsdp",
            scatter_dimension=0,
            tiled=True,
        ).astype(jnp.float32)
        back_one, g_gain_one, g_shift_one = norm_backward(grad_one, normed_one, recip_one, gain_one)
        grad_inputs = grad_middle + back_one
        matrices = (g_mixer, g_output, g_up, g_down)
        smalls = (
            g_gain_one,
            g_shift_one,
            mixer_bias_term,
            out_bias_term,
            g_gain_two,
            g_shift_two,
            up_bias_term,
            down_bias_term,
        )
        matrix_sums = (
            matrices if matrix_sums is None else jax.tree.map(jnp.add, matrix_sums, matrices)
        )
        small_sums = smalls if small_sums is None else jax.tree.map(jnp.add, small_sums, smalls)
        results.append(outputs.astype(jnp.bfloat16))
        input_grads.append(grad_inputs)
    g_mixer_sum, g_output_sum, g_up_sum, g_down_sum = matrix_sums
    reduced = (
        lax.psum_scatter(
            g_mixer_sum.astype(jnp.bfloat16), "dp", scatter_dimension=0, tiled=True
        ).astype(jnp.float32),
        lax.psum_scatter(
            g_output_sum.astype(jnp.bfloat16), "dp", scatter_dimension=1, tiled=True
        ).astype(jnp.float32),
        lax.psum_scatter(
            g_up_sum.astype(jnp.bfloat16), "dp", scatter_dimension=0, tiled=True
        ).astype(jnp.float32),
        lax.psum_scatter(
            g_down_sum.astype(jnp.bfloat16), "dp", scatter_dimension=1, tiled=True
        ).astype(jnp.float32),
    )
    totals = lax.psum(
        (
            small_sums[0],
            small_sums[1],
            small_sums[2],
            small_sums[3],
            small_sums[4],
            small_sums[5],
            small_sums[6],
            small_sums[7],
            errors,
        ),
        ("dp", "fsdp"),
    )
    pieces = [own_slice(totals[index], data_index, data_ways) for index in range(8)]
    query_key_piece = own_slice(totals[2][: 2 * D], data_index, data_ways)
    value_piece = own_slice(totals[2][2 * D :], data_index, data_ways)
    loss = totals[8] / (token_tally * D)
    return (
        jnp.concatenate(results, axis=0),
        loss,
        jnp.concatenate(input_grads, axis=0),
        pieces[0],
        pieces[1],
        reduced[0],
        query_key_piece,
        value_piece,
        reduced[1],
        pieces[3],
        pieces[4],
        pieces[5],
        reduced[2],
        pieces[6],
        reduced[3],
        pieces[7],
    )


BF = jnp.bfloat16
F32 = jnp.float32
HEADS_LOCAL = 4
W = 320
F = 1280
R = 384
G = 1536
BLK = 160
SUB = 128
QUAD = 512
HALF = 640
MESH_ID = pl.DeviceIdType.MESH


def _nn(a, b):
    return lax.dot_general(a, b, (((1,), (0,)), ((), ())), preferred_element_type=F32)


def _nt(a, b):
    return lax.dot_general(a, b, (((1,), (1,)), ((), ())), preferred_element_type=F32)


def _tn(a, b):
    return lax.dot_general(a, b, (((0,), (0,)), ((), ())), preferred_element_type=F32)


def _ds(start, size, step):
    if isinstance(start, int):
        return pl.ds(start, size)
    return pl.ds(pl.multiple_of(start, step), size)


class Place:
    def __init__(self):
        dp = lax.axis_index("dp")
        fs = lax.axis_index("fsdp")
        z, x = lax.div(dp, 2), lax.rem(dp, 2)
        y, c = lax.div(fs, 2), lax.rem(fs, 2)
        self.z, self.x, self.fs, self.dp = z, x, fs, dp
        self.core = (dp, 2 * y + 1 - c)
        self.ynb = (dp, 2 * (1 - y) + c)
        self.diagonal = (dp, 2 * (1 - y) + 1 - c)
        self.mates = (2 * y + 1 - c, 2 * (1 - y) + c, 2 * (1 - y) + 1 - c)
        self.xnb = (2 * z + 1 - x, fs)
        self.zs = (z, z + 1 - 2 * lax.rem(z, 2), lax.rem(z + 2, 4), 3 - z)
        self.zn = tuple((2 * zk + x, fs) for zk in self.zs)
        self.up = (2 * jnp.minimum(z + 1, 3) + x, fs)
        self.down = (2 * jnp.maximum(z - 1, 0) + x, fs)
        self.near = lax.div(z, 2)
        self.far = 1 - self.near

    def barrier(self):
        sem = pltpu.get_barrier_semaphore()
        for peer in (self.core, self.ynb, self.diagonal, self.xnb) + self.zn[1:]:
            pl.semaphore_signal(sem, inc=1, device_id=peer, device_id_type=MESH_ID)
        pl.semaphore_wait(sem, 7)


def _send(src, dst, ss, rs, peer):
    return pltpu.make_async_remote_copy(
        src_ref=src, dst_ref=dst, send_sem=ss, recv_sem=rs, device_id=peer, device_id_type=MESH_ID
    )


class Gather:
    def __init__(self, place, buf, ss, rs, cols=slice(None)):
        self.place, self.buf, self.ss, self.rs, self.cols = place, buf, ss, rs, cols

    def part(self, s, slot):
        return self.buf.at[_ds(QUAD * s + SUB * slot, SUB, SUB), self.cols]

    def to_core(self, s):
        return _send(self.part(s, 0), self.part(s, 1), self.ss.at[s], self.rs.at[s], self.place.core)

    def to_y(self, s):
        return _send(self.part(s, 0), self.part(s, 2), self.ss.at[3 + s], self.rs.at[3 + s], self.place.ynb)

    def on(self, s):
        return _send(self.part(s, 2), self.part(s, 3), self.ss.at[6 + s], self.rs.at[6 + s], self.place.core)

    def start(self, s):
        self.to_y(s).start()
        self.to_core(s).start()

    def pass_on(self, s):
        self.to_y(s).wait_recv()
        self.on(s).start()

    def ready(self, s):
        self.to_core(s).wait_recv()
        self.on(s).wait_recv()

    def end(self):
        for s in range(3):
            self.to_core(s).wait_send()
            self.to_y(s).wait_send()
            self.on(s).wait_send()


class Scatter:
    def __init__(self, place, sb, rb, own, ss, rs, cols=slice(None)):
        self.place, self.sb, self.rb, self.own, self.ss, self.rs, self.cols = place, sb, rb, own, ss, rs, cols

    def copy(self, kind, s):
        peer = self.place.ynb if kind == 1 else self.place.core
        slot = 2 + s if kind == 1 else kind // 2
        return _send(
            self.sb.at[slot, :, self.cols],
            self.rb.at[kind, s, :, self.cols],
            self.ss.at[3 * kind + s],
            self.rs.at[3 * kind + s],
            peer,
        )

    def again(self, kind, s):
        if isinstance(s, int):
            if s > 0:
                self.copy(kind, s - 1).wait_send()
        else:
            pl.when(s > 0)(lambda: self.copy(kind, s - 1).wait_send())

    def post(self, s, lhs, rhs):
        rows = QUAD * s
        term = _nt(lhs(_ds(rows + 2 * SUB, 2 * SUB, SUB)), rhs())
        self.again(0, s)
        self.sb[0, :, self.cols] = term[SUB:].astype(BF)
        self.copy(0, s).start()
        mine = _nt(lhs(_ds(rows, 2 * SUB, SUB)), rhs())
        self.again(2, s)
        self.sb[1, :, self.cols] = mine[SUB:].astype(BF)
        self.copy(2, s).start()
        self.own[_ds(SUB * s, SUB, SUB), self.cols] = mine[:SUB]
        self.copy(0, s).wait_recv()
        self.sb[2 + s, :, self.cols] = (term[:SUB] + self.rb[0, s, :, self.cols].astype(F32)).astype(BF)
        self.copy(1, s).start()

    def wait(self, s):
        self.copy(2, s).wait_recv()
        self.copy(1, s).wait_recv()

    def total(self, s, i, step):
        sub = _ds(step * i, step, step)
        return self.own[_ds(SUB * s + step * i, step, step), self.cols] + (
            self.rb[2, s, sub, self.cols].astype(F32) + self.rb[1, s, sub, self.cols].astype(F32)
        )

    def end(self):
        self.copy(0, 2).wait_send()
        self.copy(2, 2).wait_send()
        for s in range(3):
            self.copy(1, s).wait_send()


def _norm(values):
    average = jnp.mean(values, axis=-1, keepdims=True)
    centered = values - average
    reciprocal = lax.rsqrt(jnp.mean(centered * centered, axis=-1, keepdims=True) + EPSILON)
    return centered * reciprocal, reciprocal


def _head_rows(lanes, offset):
    lane = lax.broadcasted_iota(jnp.int32, (1, lanes), 1) - offset
    return [
        jnp.where((lane >= HD * h) & (lane < HD * h + HD), 1.0, 0.0).astype(BF)
        for h in range(HEADS_LOCAL)
    ]


def _stack(values, heads):
    return jnp.concatenate([values * head for head in heads], axis=0)


def _allowed(auxb):
    lane = lax.broadcasted_iota(jnp.int32, (1, 128), 1)
    picks = (lane >= 96) & (lane < 104)
    left = jnp.where(picks, auxb.astype(F32), jnp.where(lane == 104, 1.0, 0.0)).astype(BF)
    score = _nt(left, auxb)
    here = lax.broadcasted_iota(jnp.int32, (128, 128), 0)
    there = lax.broadcasted_iota(jnp.int32, (128, 128), 1)
    return (score > 1.5) | (here == there)


def _softmax(scores, allowed):
    probs = []
    for h in range(HEADS_LOCAL):
        part = jnp.where(allowed, scores[:, 128 * h : 128 * h + 128], -1e30)
        grown = jnp.exp(part - jnp.max(part, axis=-1, keepdims=True))
        probs.append(grown * (1.0 / jnp.sum(grown, axis=-1, keepdims=True)))
    return probs


PIECES = ((0, 0, 1024), (0, 1024, 256), (1, 0, 1280), (2, 0, 1280))


def _spread(packed, place):
    dp, fs = place.dp, place.fs

    def wide(ref):
        size = ref.shape[0]
        return jnp.concatenate([ref[...].astype(F32).reshape(1, size), jnp.zeros((1, D - size), F32)], axis=1)

    rows = jnp.concatenate([wide(ref) for ref in packed[:6]], axis=0)
    rows = pltpu.roll(rows, BLK * dp, 1)
    up = pltpu.roll(wide(packed[6]), 640 * lax.rem(dp, 2), 1)
    up = up * jnp.where(lax.div(dp, 2) == fs, 1.0, 0.0)
    mixed = wide(packed[7])
    lane = lax.broadcasted_iota(jnp.int32, (1, D), 1)
    row = jnp.zeros((1, D), F32)
    for t in range(3):
        shift = 480 * dp - 960 * t - W * fs
        turned = pltpu.roll(mixed, lax.rem(shift + 4 * D, D), 1)
        mine = (lane >= W * t) & (lane < W * t + W) & (lane >= shift) & (lane < shift + 480)
        row = row + jnp.where(mine, turned, 0.0)
    return jnp.concatenate([rows, up, row], axis=0)


def _marks(pictures, spots, real, s):
    lane = lax.broadcasted_iota(jnp.int32, (3, SUB), 1)
    change = jnp.where((pictures != pltpu.roll(pictures, 1, 1)) & (lane > 0), 1.0, 0.0).astype(BF)
    here = lax.broadcasted_iota(jnp.int32, (SUB, SUB), 0)
    there = lax.broadcasted_iota(jnp.int32, (SUB, SUB), 1)
    upto = jnp.where(here <= there, 1.0, 0.0).astype(BF)
    rank = _nn(change, upto)[s : s + 1, :].astype(jnp.int32)
    spot = lax.rem(here, 32)
    row = (spot < 16) & (spot == spots[0:1, SUB * s : SUB * s + SUB])
    col = (spot >= 16) & (spot - 16 == spots[1:2, SUB * s : SUB * s + SUB])
    once = (here < 96) & (row | col)
    picture = (here >= 96) & (here < 104) & (here - 96 == rank)
    live = (here == 104) & (real[s : s + 1, :] > 0)
    return jnp.where(once | picture | live, 1.0, 0.0).T.astype(BF)


def layer_kernel(
    tok_h, teach_h, mix_h, out_h, wu_h, wd_h, v0, v1, v2, v3, v4, v5, v6, v7, pictures, spots, real, tabs,
    res_h, gtok_h, gd_h, gu_h, ga_h, small_o, loss_o, keep_h,
    tok, aux, w, wo, n1a, n2, gu, gzb, qk, v, o, acc, own, mid, gy, sb, rb,
    gb, xin, zin, fin, vecs, small, ccz, ccx, sta, stx, stz,
    ws, wr, ags, agr, rss, rsr, xs, xr, zs, zr, as_, ar, bs, br, ls, os_, xfree, zfree, gfree, nfree,
):
    place = Place()
    z, x = place.z, place.x
    patches = TOTAL[0]
    mine = _ds(BLK * (2 * z + x), BLK, 32)
    loads = [
        pltpu.make_async_copy(src, dst, ls.at[i])
        for i, (src, dst) in enumerate(
            [(mix_h.at[t], o.at[pl.ds(BLK * t, BLK), :]) for t in range(3)]
            + [(out_h, o.at[pl.ds(3 * BLK, BLK), :]), (tok_h, tok)]
            + [(wu_h, w.at[1, mine, :]), (wd_h, w.at[2, mine, :])]
        )
    ]
    for copy in loads:
        copy.start()
    stz[z, :8, :] = _spread((v0, v1, v2, v3, v4, v5, v6, v7), place)
    place.barrier()

    def over_z(buf, rows, kind):
        there = buf.at[z, rows, :]
        return [_send(there, there, as_.at[kind, k], ar.at[kind, z], place.zn[k]) for k in (1, 2, 3)]

    def from_z(buf, rows, kind):
        for k in (1, 2, 3):
            there = buf.at[place.zs[k], rows, :]
            _send(there, there, as_.at[kind, k], ar.at[kind, place.zs[k]], place.zn[k]).wait_recv()

    def swap_x(buf, rows, kind):
        return _send(buf.at[0, rows, :], buf.at[1, rows, :], bs.at[kind], br.at[kind], place.xnb)

    first8 = pl.ds(0, 8)
    vector_z = over_z(stz, first8, 0)
    for copy in vector_z:
        copy.start()

    shards = (None, wu_h, wd_h)

    def at(piece, zk, xk):
        third, start, size = PIECES[piece]
        return w.at[third, _ds(BLK * (2 * zk + xk), BLK, 32), pl.ds(start, size)]

    def shard(piece):
        third, start, size = PIECES[piece]
        if third == 0:
            return at(piece, z, x)
        return shards[third].at[:, pl.ds(start, size)]

    def first(piece, i):
        peer = (place.xnb, place.up, place.down)[i]
        return _send(shard(piece), at(piece, z, x), ws.at[piece, i], wr.at[piece, 2 * z + x], peer)

    def begin_z(piece):
        pl.when(z < 3)(lambda: first(piece, 1).start())
        pl.when(z > 0)(lambda: first(piece, 2).start())

    def begin_x(piece):
        first(piece, 0).start()

    def hop(piece, d, i):
        zk = jnp.maximum(z - d, 0) if i < 2 else jnp.minimum(z + d, 3)
        peer = (place.up, place.xnb, place.down, place.xnb)[i]
        there = at(piece, zk, x)
        return _send(there, there, ws.at[piece, 4 * d - 1 + i], wr.at[piece, 2 * zk + x], peer)

    def relay(piece, d):
        @pl.when(z >= d)
        def _():
            hop(piece, d, 0).wait_recv()
            pl.when(z < 3)(lambda: hop(piece, d, 0).start())
            hop(piece, d, 1).start()

        @pl.when(z + d <= 3)
        def _():
            hop(piece, d, 2).wait_recv()
            pl.when(z > 0)(lambda: hop(piece, d, 2).start())
            hop(piece, d, 3).start()

    def over_x(piece, zk):
        there = at(piece, zk, 1 - x)
        _send(there, there, ws.at[piece, 0], wr.at[piece, 2 * zk + 1 - x], place.xnb).wait_recv()

    def complete(piece):
        for k in range(4):
            over_x(piece, place.zs[k])

    def sent(piece):
        first(piece, 0).wait_send()
        pl.when(z < 3)(lambda: first(piece, 1).wait_send())
        pl.when(z > 0)(lambda: first(piece, 2).wait_send())
        for d in range(1, 4):

            @pl.when(z >= d)
            def _(d=d):
                pl.when(z < 3)(lambda: hop(piece, d, 0).wait_send())
                hop(piece, d, 1).wait_send()

            @pl.when(z + d <= 3)
            def _(d=d):
                pl.when(z > 0)(lambda: hop(piece, d, 2).wait_send())
                hop(piece, d, 3).wait_send()

    outs = []

    def out(src, dst):
        copy = pltpu.make_async_copy(src, dst, os_.at[len(outs)])
        copy.start()
        outs.append(copy)
        return len(outs) - 1

    for copy in loads[:4]:
        copy.wait()
    w[0, mine, :] = jnp.concatenate([o[pl.ds(BLK * t, BLK), :] for t in range(4)], axis=1)
    begin_z(0)
    begin_x(0)
    agx = Gather(place, aux, ags.at[1], agr.at[1])
    for s in range(3):
        aux[pl.ds(QUAD * s, SUB), :] = _marks(pictures[...], spots[...], real[...], s)
        agx.start(s)
    loads[4].wait()

    def first_norm(i, _):
        rows = _ds(32 * i, 32, 32)
        own[rows, :] = _norm(tok[rows, :].astype(F32))[0]
        return 0

    lax.fori_loop(0, R // 32, first_norm, 0)
    from_z(stz, first8, 0)
    stx[0, :8, :] = (stz[0, :8, :] + stz[1, :8, :]) + (stz[2, :8, :] + stz[3, :8, :])
    vector_x = swap_x(stx, first8, 0)
    vector_x.start()
    vector_x.wait_recv()
    vecs[...] = stx[0, :8, :] + stx[1, :8, :]
    ag1 = Gather(place, n1a, ags.at[0], agr.at[0])
    for s in range(3):

        def scale_rows(i, _, s=s):
            rows = _ds(QUAD * s + 32 * i, 32, 32)
            n1a[rows, :] = (own[_ds(SUB * s + 32 * i, 32, 32), :] * vecs[0:1, :] + vecs[1:2, :]).astype(BF)
            return 0

        lax.fori_loop(0, 4, scale_rows, 0)
        ag1.start(s)
    relay(0, 1)
    for s in range(3):
        agx.pass_on(s)
    relay(0, 2)
    begin_z(1)
    begin_z(2)
    ag1.pass_on(0)
    relay(0, 3)
    begin_x(1)
    for s in range(3):
        agx.ready(s)
    whole = slice(None)
    count_z = over_z(ccz, whole, 1)
    count_x = swap_x(ccx, whole, 1)
    complete(0)
    for copy in vector_z + [vector_x]:
        copy.wait_send()

    side = _head_rows(W, 0)
    first_half = lax.rem(lax.broadcasted_iota(jnp.int32, (1, 2 * W), 1), HD) < HD // 2
    rs1 = Scatter(place, sb, rb, own, rss.at[0], rsr.at[0])

    def attend_part(s, _):
        ag1.ready(s)
        acc[:, : 3 * W] = _nn(n1a[_ds(QUAD * s, QUAD, QUAD), :], w[0, :, : 3 * W]) + vecs[7:8, : 3 * W]

        def attend_rows(i, _):
            here = _ds(SUB * i, SUB, SUB)
            rows = _ds(QUAD * s + SUB * i, SUB, SUB)
            auxb = aux[rows, :]
            angle = _nn(auxb, tabs[...])
            raw = acc[here, : 2 * W]
            flipped = jnp.where(first_half, -pltpu.roll(raw, 2 * W - 40, 1), pltpu.roll(raw, 40, 1))
            turned = raw * angle[:, : 2 * W] + flipped * angle[:, 2 * W :]
            qkb = turned.astype(BF)
            kqb = pltpu.roll(turned, W, 1)[:, :W].astype(BF)
            vb = acc[here, 2 * W : 3 * W].astype(BF)
            qk[rows, :] = qkb
            v[rows, :] = vb
            scores = _nt(qkb[:, :W], _stack(kqb, side)) * HD ** (-0.5)
            probs = _softmax(scores, _allowed(auxb))
            flat = jnp.concatenate([p.astype(BF) for p in probs], axis=1)
            o[rows, :] = _nn(flat, _stack(vb, side)).astype(BF)

            @pl.when((s == 0) & (i == 0))
            def _():
                relay(1, 1)
                ag1.pass_on(1)

            @pl.when((s == 0) & (i == 1))
            def _():
                relay(1, 2)

            @pl.when((s == 0) & (i == 2))
            def _():
                relay(1, 3)
                begin_x(2)

            pl.when((s == 0) & (i == 3))(lambda: relay(2, 1))

            @pl.when((s == 1) & (i == 2))
            def _():
                relay(2, 2)
                begin_z(3)

            @pl.when((s == 2) & (i == 2))
            def _():
                relay(2, 3)
                begin_x(3)

            return 0

        lax.fori_loop(0, 4, attend_rows, 0)

        @pl.when(s == 0)
        def _():
            complete(1)
            wo[...] = w[0, :, 3 * W :]
            ag1.pass_on(2)


        rs1.post(s, lambda rows: o[rows, :], lambda: wo[...])

        @pl.when(s == 0)
        def _():
            ccz[z] = _nn(jnp.ones((8, G), BF), aux[...])
            for copy in count_z:
                copy.start()

        return 0

    lax.fori_loop(0, 3, attend_part, 0)
    n1_kept = out(n1a, keep_h)
    ag2 = Gather(place, n2, ags.at[2], agr.at[2])

    def second_norm(s, _):
        rs1.wait(s)

        def rows_of(i, _):
            rows = _ds(SUB * s + 32 * i, 32, 32)
            middle = tok[rows, :].astype(F32) + rs1.total(s, i, 32) + vecs[2:3, :]
            mid[rows, :] = middle
            normed, _r = _norm(middle)
            n2[_ds(QUAD * s + 32 * i, 32, 32), :] = (normed * vecs[3:4, :] + vecs[4:5, :]).astype(BF)
            return 0

        lax.fori_loop(0, 4, rows_of, 0)
        ag2.start(s)

        @pl.when(s == 1)
        def _():
            from_z(ccz, whole, 1)
            ccx[0] = (ccz[0] + ccz[1]) + (ccz[2] + ccz[3])
            count_x.start()

        return 0

    lax.fori_loop(0, 3, second_norm, 0)
    teach = tok
    teach_load = pltpu.make_async_copy(teach_h, teach, ls.at[7])
    teach_load.start()
    relay(3, 1)
    ag1.end()
    outs[n1_kept].wait()
    loads[5].wait()
    complete(2)

    def up_part(s, _):
        pl.when(s == 1)(lambda: relay(3, 2))
        pl.when(s == 2)(lambda: relay(3, 3))
        ag2.pass_on(s)
        ag2.ready(s)
        acc[...] = _nn(n2[_ds(QUAD * s, QUAD, QUAD), :], w[1]) + vecs[6:7, :]

        def rows_of(i, _):
            upper = acc[_ds(32 * i, 32, 32), :]
            rows = _ds(QUAD * s + 32 * i, 32, 32)
            gate = 0.5 * jnp.tanh(0.851 * upper) + 0.5
            n1a[rows, :] = (upper * gate).astype(BF)
            gu[rows, :] = (gate + 1.702 * upper * gate * (1.0 - gate)).astype(BF)
            return 0

        lax.fori_loop(0, QUAD // 32, rows_of, 0)
        return 0

    lax.fori_loop(0, 3, up_part, 0)
    act = n1a
    rs1.end()
    loads[6].wait()
    teach_load.wait()

    cols = {0: _ds(HALF * place.near, HALF, 128), 1: _ds(HALF * place.far, HALF, 128)}
    count_x.wait_recv()
    real_count = (ccx[0] + ccx[1])[0:1, 104:105]
    factor = 2.0 * patches / real_count
    downs = [Scatter(place, sb, rb, own, rss.at[1 + j], rsr.at[1 + j], cols[j]) for j in range(2)]
    gathers = [Gather(place, gzb, ags.at[3 + j], agr.at[3 + j], cols[j]) for j in range(2)]
    small[...] = jnp.zeros_like(small)

    for j in range(2):
        for k in ((0, 1), (2, 3))[j]:
            over_x(3, place.zs[k])
        half = (place.near, place.far)[j]

        def down_part(s, _, j=j, half=half):
            downs[j].post(s, lambda rows: act[rows, :], lambda: w[2, _ds(HALF * half, HALF, 128), :])
            return 0

        lax.fori_loop(0, 3, down_part, 0)

        def finish_part(s, sums, j=j):
            downs[j].wait(s)

            def rows_of(i, sums):
                rows = _ds(SUB * s + 32 * i, 32, 32)
                result = mid[rows, cols[j]] + downs[j].total(s, i, 32) + vecs[5:6, cols[j]]
                real = aux[_ds(QUAD * s + 32 * i, 32, 32), 104:105].astype(F32)
                difference = result - teach[rows, cols[j]].astype(F32)
                masked = real * difference
                gout = factor * masked
                low = gout.astype(BF)
                gy[rows, cols[j]] = gout
                teach[rows, cols[j]] = result.astype(BF)
                gzb[_ds(QUAD * s + 32 * i, 32, 32), cols[j]] = low
                return (
                    sums[0] + jnp.sum(masked * difference, axis=0, keepdims=True),
                    sums[1] + jnp.sum(low.astype(F32), axis=0, keepdims=True),
                )

            sums = lax.fori_loop(0, 4, rows_of, sums)
            gathers[j].start(s)
            if j == 1:
                gathers[0].pass_on(s)
            return sums

        zero = jnp.zeros((1, HALF), F32)
        sums = lax.fori_loop(0, 3, finish_part, (zero, zero))
        small[6:7, cols[j]] = sums[0]
        small[5:6, cols[j]] = sums[1]
    res_out = out(teach, res_h)

    def xin_at(chunk, slot, k):
        if chunk == 3:
            return n2.at[pl.ds(BLK * k, BLK), pl.ds(256, 256)]
        return xin.at[slot, k, :, pl.ds(0, 1024)] if chunk == 0 else xin.at[slot, k]

    def zin_at(chunk, slot, i):
        if chunk == 3:
            return n2.at[pl.ds(BLK * i, BLK), pl.ds(512, 256)]
        return zin.at[slot, i, :, pl.ds(0, 1024)] if chunk == 0 else zin.at[slot, i]

    def g_rows(chunk, slot, rows):
        if chunk == 3:
            return n2.at[rows, pl.ds(0, 256)]
        return gb.at[slot, rows, pl.ds(0, 1024)] if chunk == 0 else gb.at[slot, rows, :]

    def to_x(chunk, slot, k):
        rows = _ds(BLK * (2 * place.zs[k] + 1 - x), BLK, 32)
        return _send(
            g_rows(chunk, slot, rows), xin_at(chunk, slot, k), xs.at[chunk, k], xr.at[chunk, k], place.xnb
        )

    def block(k):
        return _ds(BLK * (2 * place.zs[k] + x), BLK, 32)

    def to_z(chunk, slot, i):
        k, peer = ((3, place.zn[1]), (1, place.zn[1]), (2, place.zn[2]))[i]
        return _send(g_rows(chunk, slot, block(k)), zin_at(chunk, slot, i), zs.at[chunk, i], zr.at[chunk, i], peer)

    def tile(slot, lhs, rhs, half):
        rows = _ds(HALF * half, HALF, 128)
        for part in range(2):
            cols = pl.ds(HALF * part, HALF)
            gb[slot, rows, cols] = _tn(lhs[:, rows], rhs[:, cols]).astype(BF)

    def add_x(chunk, slot, i):
        k = (3, 1)[i]
        to_x(chunk, slot, k).wait_recv()
        ref = g_rows(chunk, slot, block(k))
        ref[...] = (ref[...].astype(F32) + xin_at(chunk, slot, k)[...].astype(F32)).astype(BF)
        to_z(chunk, slot, i).start()

    def combine(chunk, slot):
        to_x(chunk, slot, 2).wait_recv()
        to_z(chunk, slot, 0).wait_recv()
        ref = g_rows(chunk, slot, block(2))
        ref[...] = (
            (ref[...].astype(F32) + xin_at(chunk, slot, 2)[...].astype(F32)) + zin_at(chunk, slot, 0)[...].astype(F32)
        ).astype(BF)
        to_z(chunk, slot, 2).start()

    def fin_cols(chunk):
        return {0: pl.ds(0, 1024), 3: pl.ds(1024, 256)}.get(chunk, pl.ds(0, D))

    def add_own(chunk, slot):
        to_x(chunk, slot, 0).wait_recv()
        fin[:, fin_cols(chunk)] = g_rows(chunk, slot, block(0))[...].astype(F32) + xin_at(chunk, slot, 0)[...].astype(F32)

    def add_z(chunk, slot):
        to_z(chunk, slot, 1).wait_recv()
        to_z(chunk, slot, 2).wait_recv()
        cols = fin_cols(chunk)
        fin[:, cols] = fin[:, cols] + (
            zin_at(chunk, slot, 1)[...].astype(F32) + zin_at(chunk, slot, 2)[...].astype(F32)
        )

    for s in range(3):
        gathers[0].ready(s)
    tile(0, gzb, act, place.near)
    to_x(2, 0, 1).start()
    to_x(2, 0, 0).start()

    for copy in downs:
        copy.end()
    rs3 = Scatter(place, sb, rb, own, rss.at[3], rsr.at[3])
    up_total = jnp.zeros((1, F), F32)
    for s in range(3):
        gathers[1].pass_on(s)
    gathers[1].ready(0)
    for s in range(3):
        acc[...] = _nn(gzb[pl.ds(QUAD * s, QUAD), :], w[2])

        def gate_rows(i, total, s=s):
            rows = _ds(QUAD * s + 32 * i, 32, 32)
            low = (acc[_ds(32 * i, 32, 32), :] * gu[rows, :].astype(F32)).astype(BF)
            gu[rows, :] = low
            return total + jnp.sum(low.astype(F32), axis=0, keepdims=True)

        up_total = lax.fori_loop(0, QUAD // 32, gate_rows, up_total)
        rs3.post(s, lambda rows: gu[rows, :], lambda: w[1])
        if s == 0:
            for t in (1, 2):
                gathers[1].ready(t)
            tile(0, gzb, act, place.far)
            to_x(2, 0, 3).start()
            to_x(2, 0, 2).start()
    for gather in gathers:
        gather.end()
    for peer in (place.core, place.ynb):
        pl.semaphore_signal(gfree, inc=1, device_id=peer, device_id_type=MESH_ID)
    n1_back = pltpu.make_async_copy(keep_h, n1a, ls.at[8])
    n1_back.start()
    outs[res_out].wait()
    tok_back = pltpu.make_async_copy(tok_h, tok, ls.at[9])
    tok_back.start()
    small[pl.ds(8 + place.fs, 1), :] = up_total
    add_x(2, 0, 1)
    pl.semaphore_wait(gfree, 2)
    ag3 = Gather(place, gzb, ags.at[5], agr.at[5])

    def norm_rows(s, i, sums, values, gain, terms):
        rows = _ds(SUB * s + 32 * i, 32, 32)
        grad = terms.total(s, i, 32)
        normed, reciprocal = _norm(values[rows, :].astype(F32))
        scaled = grad * gain
        back = (
            scaled
            - jnp.mean(scaled, axis=-1, keepdims=True)
            - normed * jnp.mean(scaled * normed, axis=-1, keepdims=True)
        ) * reciprocal
        total = gy[rows, :] + back
        gy[rows, :] = total
        pair = (
            sums[0] + jnp.sum(grad * normed, axis=0, keepdims=True),
            sums[1] + jnp.sum(grad, axis=0, keepdims=True),
        )
        return total, pair

    zero = jnp.zeros((1, D), F32)

    def second_back(s, sums):
        rs3.wait(s)

        def rows_of(i, sums):
            total, pair = norm_rows(s, i, sums[:2], mid, vecs[3:4, :], rs3)
            low = total.astype(BF)
            gzb[_ds(QUAD * s + 32 * i, 32, 32), :] = low
            return pair + (sums[2] + jnp.sum(low.astype(F32), axis=0, keepdims=True),)

        sums = lax.fori_loop(0, 4, rows_of, sums)
        ag3.start(s)

        @pl.when(s == 1)
        def _():
            tile(1, n2, gu, place.far)
            to_x(1, 1, 3).start()
            to_x(1, 1, 2).start()

        return sums

    gain2, shift2, outb = lax.fori_loop(0, 3, second_back, (zero, zero, zero))
    small[2:3, :] = outb
    small[3:4, :] = gain2
    small[4:5, :] = shift2
    tile(1, n2, gu, place.near)
    to_x(1, 1, 1).start()
    to_x(1, 1, 0).start()
    ag2.end()
    for peer in (place.xnb,) + place.zn[1:3]:
        pl.semaphore_signal(nfree, inc=1, device_id=peer, device_id_type=MESH_ID)
    add_x(2, 0, 0)
    add_own(2, 0)
    rs3.end()
    rs4 = Scatter(place, sb, rb, own, rss.at[4], rsr.at[4])

    def attend_back(s, total):
        ag3.pass_on(s)
        ag3.ready(s)

        @pl.when(s == 2)
        def _():
            for half in (place.far, place.near):
                rows = _ds(HALF * half, HALF, 128)
                n2[rows, pl.ds(0, 256)] = _tn(gzb[:, rows], o[:, W - 256 :]).astype(BF)
            pl.semaphore_wait(nfree, 3)
            for k in (3, 2, 1, 0):
                to_x(3, 0, k).start()

        acc[:, :W] = _nn(gzb[_ds(QUAD * s, QUAD, QUAD), :], wo[...])

        def attend_rows(i, total):
            rows = _ds(QUAD * s + SUB * i, SUB, SUB)
            auxb = aux[rows, :]
            qkb = qk[rows, :]
            kqb = pltpu.roll(qkb.astype(F32), W, 1)[:, :W].astype(BF)
            vb = v[rows, :]
            gob = acc[_ds(SUB * i, SUB, SUB), :W].astype(BF)
            keys = _stack(kqb, side)
            scores = _nt(qkb[:, :W], keys) * HD ** (-0.5)
            probs = _softmax(scores, _allowed(auxb))
            gprobs = _nt(gob, _stack(vb, side))
            gscores = []
            for h in range(HEADS_LOCAL):
                gp = gprobs[:, 128 * h : 128 * h + 128]
                delta = jnp.sum(gp * probs[h], axis=-1, keepdims=True)
                gscores.append((probs[h] * (gp - delta)).astype(BF))
            flat = jnp.concatenate(gscores, axis=1)
            tall = jnp.concatenate(gscores, axis=0)
            ptall = jnp.concatenate([p.astype(BF) for p in probs], axis=0)
            gqk = jnp.concatenate([_nn(flat, keys), _tn(tall, _stack(qkb[:, :W], side))], axis=1) * HD ** (-0.5)
            gv = _tn(ptall, _stack(gob, side))
            angle = _nn(auxb, tabs[...])
            sined = gqk * angle[:, 2 * W :]
            shifted = jnp.where(first_half, pltpu.roll(sined, 2 * W - 40, 1), -pltpu.roll(sined, 40, 1))
            turned = gqk * angle[:, : 2 * W] + shifted
            low = jnp.concatenate([turned, gv], axis=1).astype(BF)
            gu[rows, : 3 * W] = low
            return total + jnp.sum(low.astype(F32), axis=0, keepdims=True)

        total = lax.fori_loop(0, 4, attend_rows, total)
        rs4.post(s, lambda rows: gu[rows, : 3 * W], lambda: w[0, :, : 3 * W])


        @pl.when(s == 0)
        def _():
            combine(2, 0)
            pl.semaphore_signal(xfree, inc=1, device_id=place.xnb, device_id_type=MESH_ID)

        pl.when(s == 1)(lambda: add_x(1, 1, 0))

        @pl.when(s == 2)
        def _():
            combine(1, 1)
            add_x(1, 1, 1)

        return total

    mix_total = lax.fori_loop(0, 3, attend_back, jnp.zeros((1, 3 * W), F32))
    small[pl.ds(12 + place.fs, 1), : 3 * W] = mix_total

    for k in range(4):
        to_x(2, 0, k).wait_send()
    for i in range(3):
        to_z(2, 0, i).wait_send()
    n1_back.wait()

    def last_tile(half):
        rows = _ds(HALF * half, HALF, 128)
        gb[0, rows, : 3 * W] = _tn(n1a[:, rows], gu[:, : 3 * W]).astype(BF)
        gb[0, rows, 3 * W : 1024] = _tn(gzb[:, rows], o[:, : W - 256]).astype(BF)

    last_tile(place.far)
    pl.semaphore_wait(xfree, 1)
    to_x(0, 0, 3).start()
    to_x(0, 0, 2).start()
    last_tile(place.near)
    add_z(2, 0)
    down_out = out(fin, gd_h)
    for peer in place.zn[1:3]:
        pl.semaphore_signal(zfree, inc=1, device_id=peer, device_id_type=MESH_ID)

    tok_back.wait()

    def first_back(s, sums):
        rs4.wait(s)

        pl.when(s == 1)(lambda: add_x(3, 0, 0))
        return lax.fori_loop(0, 4, lambda i, t: norm_rows(s, i, t, tok, vecs[0:1, :], rs4)[1], sums)

    gain1, shift1 = lax.fori_loop(0, 3, first_back, (zero, zero))
    out(gy, gtok_h)
    small[0:1, :] = gain1
    small[1:2, :] = shift1

    sta[place.fs] = small[...]
    there = sta.at[place.fs]
    peers = (place.core, place.ynb, place.diagonal)
    small_f = [_send(there, there, as_.at[3, k], ar.at[3, place.fs], peer) for k, peer in enumerate(peers)]
    for copy in small_f:
        copy.start()
    outs[down_out].wait()
    for k, peer in enumerate(peers):
        there = sta.at[place.mates[k]]
        _send(there, there, as_.at[3, k], ar.at[3, place.mates[k]], peer).wait_recv()
    stx[0] = (sta[0] + sta[1]) + (sta[2] + sta[3])
    small_x = swap_x(stx, whole, 2)
    small_x.start()
    to_x(0, 0, 1).start()
    to_x(0, 0, 0).start()
    pl.semaphore_wait(zfree, 2)
    add_x(0, 0, 0)
    combine(3, 0)
    add_x(3, 0, 1)
    add_own(1, 1)
    add_z(1, 1)
    up_out = out(fin, gu_h)
    small_x.wait_recv()
    stz[z] = stx[0] + stx[1]
    small_z = over_z(stz, whole, 2)
    for copy in small_z:
        copy.start()
    combine(0, 0)
    add_x(0, 0, 1)
    outs[up_out].wait()
    add_own(3, 0)
    add_z(3, 0)
    add_own(0, 0)
    from_z(stz, whole, 2)
    total = (stz[0] + stz[1]) + (stz[2] + stz[3])
    small_o[...] = total
    loss_o[...] = jnp.sum(total[6:7, :], axis=-1, keepdims=True) / (real_count * D)
    add_z(0, 0)
    out(fin, ga_h)

    for piece in range(4):
        sent(piece)
    agx.end()
    ag3.end()
    rs4.end()
    for copy in count_z + [count_x] + small_f + [small_x] + small_z:
        copy.wait_send()
    for chunk, slot in ((1, 1), (0, 0), (3, 0)):
        for k in range(4):
            to_x(chunk, slot, k).wait_send()
        for i in range(3):
            to_z(chunk, slot, i).wait_send()
    for i, copy in enumerate(outs):
        if i not in (n1_kept, res_out, down_out, up_out):
            copy.wait()


TOTAL = [0]


def layer_call(*operands):
    any_, vm = pl.ANY, pltpu.VMEM
    outs = [
        ((R, D), BF, any_),
        ((R, D), F32, any_),
        ((BLK, D), F32, any_),
        ((BLK, D), F32, any_),
        ((BLK, D), F32, any_),
        ((16, D), F32, vm),
        ((1, 1), F32, vm),
        ((G, D), BF, any_),
    ]
    dma = pltpu.SemaphoreType.DMA
    scratch = [
        vm((R, D), BF),
        vm((G, 128), BF),
        vm((3, D, D), BF),
        vm((D, W), BF),
        vm((G, D), BF),
        vm((G, D), BF),
        vm((G, F), BF),
        vm((G, D), BF),
        vm((G, 2 * W), BF),
        vm((G, W), BF),
        vm((G, W), BF),
        vm((QUAD, D), F32),
        vm((R, D), F32),
        vm((R, D), F32),
        vm((R, D), F32),
        vm((5, SUB, D), BF),
        vm((3, 3, SUB, D), BF),
        vm((2, D, D), BF),
        vm((2, 4, BLK, D), BF),
        vm((2, 3, BLK, D), BF),
        vm((BLK, D), F32),
        vm((8, D), F32),
        vm((16, D), F32),
        vm((4, 8, 128), F32),
        vm((2, 8, 128), F32),
        vm((4, 16, D), F32),
        vm((2, 16, D), F32),
        vm((4, 16, D), F32),
        dma((4, 15)),
        dma((4, 8)),
        dma((6, 9)),
        dma((6, 9)),
        dma((5, 9)),
        dma((5, 9)),
        dma((4, 4)),
        dma((4, 4)),
        dma((4, 3)),
        dma((4, 3)),
        dma((4, 4)),
        dma((4, 4)),
        dma((3,)),
        dma((3,)),
        dma((10,)),
        dma((8,)),
        pltpu.SemaphoreType.REGULAR,
        pltpu.SemaphoreType.REGULAR,
        pltpu.SemaphoreType.REGULAR,
        pltpu.SemaphoreType.REGULAR,
    ]
    ins = [any_] * 6 + [vm] * 12
    return pl.pallas_call(
        layer_kernel,
        out_shape=[jax.ShapeDtypeStruct(shape, dtype) for shape, dtype, _ in outs],
        in_specs=[pl.BlockSpec(memory_space=space) for space in ins],
        out_specs=[pl.BlockSpec(memory_space=space) for _, _, space in outs],
        scratch_shapes=scratch,
        compiler_params=pltpu.CompilerParams(
            collective_id=1, has_side_effects=True, vmem_limit_bytes=64 << 20
        ),
        name="layer",
    )(*operands)


def turn_tables():
    import ml_dtypes

    quarter = HD // 4
    frequency = (1.0 / np.float32(10000.0) ** (np.arange(quarter, dtype=np.float32) * 4.0 / HD)).astype(np.float32)
    angle = (np.arange(16, dtype=np.float32)[:, None] * frequency[None, :]).astype(np.float32)
    cosine, sine = np.cos(angle.astype(np.float64)), np.sin(angle.astype(np.float64))
    zero = np.zeros_like(cosine)

    def head(first, second):
        top = np.concatenate([first, zero, second, zero], axis=1)
        low = np.concatenate([zero, first, zero, second], axis=1)
        return np.tile(np.concatenate([top, low], axis=0), (1, 2 * HEADS_LOCAL))

    full = np.concatenate([head(cosine, cosine), head(sine, sine)], axis=1).astype(np.float32)
    terms = []
    rest = full
    for _ in range(3):
        term = rest.astype(ml_dtypes.bfloat16)
        terms.append(term)
        rest = rest - term.astype(np.float32)
    terms.append(np.zeros((32, full.shape[1]), ml_dtypes.bfloat16))
    return jnp.asarray(np.concatenate(terms, axis=0))


def finish_kernel(
    res_i, gtok_i, gd_i, gu_i, ga_i, small, loss_i,
    res_o, loss_o, gtok_o, fg_o, fs_o, mix_o, mb_o, vb_o, out_o, ob_o, sg_o, ss_o, up_o, ub_o, down_o, db_o,
    ga, gtok, res, gd, gu, sems,
):
    dp = lax.axis_index("dp")
    copies = [
        pltpu.make_async_copy(src, dst, sems.at[i])
        for i, (src, dst) in enumerate(
            [
                (gtok_i, gtok),
                (ga_i, ga),
                (res_i, res),
                (gd_i, gd),
                (gu_i, gu),
                (gtok, gtok_o),
                (res, res_o),
                (gd, down_o),
                (gu, up_o),
            ]
        )
    ]
    for copy in copies[:5]:
        copy.start()
    loss_o[...] = loss_i[...]
    pieces = pltpu.roll(small[:8, :], lax.rem(D - BLK * dp + D, D), 1)[:, :BLK]
    for i, ref in ((0, fg_o), (1, fs_o), (2, ob_o), (3, sg_o), (4, ss_o), (5, db_o)):
        ref[...] = pieces[i : i + 1, :].reshape(BLK)
    ub_o[...] = small[pl.ds(8 + lax.div(dp, 2), 1), _ds(640 * lax.rem(dp, 2), 640, 128)].reshape(640)
    row = small[pl.ds(12 + lax.rem(dp, 4), 1), :]
    mb_o[...] = pltpu.roll(row, lax.rem(D - W * lax.div(dp, 4), D), 1)[:, :W].reshape(W)
    row = small[pl.ds(12 + lax.div(dp, 2), 1), :]
    vb_o[...] = pltpu.roll(row, 2 * W - BLK * lax.rem(dp, 2), 1)[:, :BLK].reshape(BLK)
    copies[0].wait()
    copies[5].start()
    for i in (2, 3, 4):
        copies[i].wait()
        copies[i + 4].start()
    copies[1].wait()
    for t in range(3):
        mix_o[t] = ga[:, W * t : W * t + W]
    out_o[...] = ga[:, 3 * W :]
    for copy in copies[5:]:
        copy.wait()


def finish_call(*operands):
    any_, vm = pl.ANY, pltpu.VMEM
    outs = [
        ((R, D), BF, any_),
        ((1, 1), F32, vm),
        ((R, D), F32, any_),
        ((BLK,), F32, vm),
        ((BLK,), F32, vm),
        ((3, BLK, W), F32, vm),
        ((W,), F32, vm),
        ((BLK,), F32, vm),
        ((BLK, W), F32, vm),
        ((BLK,), F32, vm),
        ((BLK,), F32, vm),
        ((BLK,), F32, vm),
        ((BLK, D), F32, any_),
        ((640,), F32, vm),
        ((BLK, D), F32, any_),
        ((BLK,), F32, vm),
    ]
    ins = [any_] * 5 + [vm] * 2
    return pl.pallas_call(
        finish_kernel,
        out_shape=[jax.ShapeDtypeStruct(shape, dtype) for shape, dtype, _ in outs],
        in_specs=[pl.BlockSpec(memory_space=space) for space in ins],
        out_specs=[pl.BlockSpec(memory_space=space) for _, _, space in outs],
        scratch_shapes=[
            vm((BLK, D), F32),
            vm((R, D), F32),
            vm((R, D), BF),
            vm((BLK, D), F32),
            vm((BLK, D), F32),
            pltpu.SemaphoreType.DMA((9,)),
        ],
        compiler_params=pltpu.CompilerParams(vmem_limit_bytes=62 << 20),
        name="finish",
    )(*operands)


def on_device_fast(
    tokens,
    teacher,
    picture,
    places,
    validity,
    first_gain,
    first_shift,
    mixer_weight,
    mixer_bias,
    output_weight,
    output_bias,
    second_gain,
    second_shift,
    upward_weight,
    upward_bias,
    downward_weight,
    downward_bias,
):
    TOTAL[0] = float(tokens.shape[0] * lax.axis_size("dp") * lax.axis_size("fsdp"))
    res, gtok, gd, gup, ga, small, loss, _ = layer_call(
        tokens,
        teacher,
        mixer_weight.transpose(1, 0, 2),
        output_weight.T,
        upward_weight,
        downward_weight.T,
        first_gain,
        first_shift,
        output_bias,
        second_gain,
        second_shift,
        downward_bias,
        upward_bias,
        mixer_bias,
        picture.reshape(3, ROW_PATCHES),
        places.T,
        validity.reshape(3, ROW_PATCHES),
        turn_tables(),
    )
    (res, loss, gtok, fg, fs, mix, mb, vb, out, ob, sg, ss, up, ub, down, db) = finish_call(
        res, gtok, gd, gup, ga, small, loss
    )
    return (res, loss.reshape(()), gtok, fg, fs, mix.transpose(1, 0, 2), mb, vb, out.T, ob, sg, ss, up, ub, down.T, db)


def solution(mesh):
    fast = mesh.shape["dp"] == 8 and mesh.shape["fsdp"] == 4
    return jax.shard_map(
        on_device_fast if fast else on_device,
        mesh=mesh,
        in_specs=(
            P(("dp", "fsdp"), None),
            P(("dp", "fsdp"), None),
            P(("dp", "fsdp")),
            P(("dp", "fsdp"), None),
            P(("dp", "fsdp")),
            P("dp"),
            P("dp"),
            P("dp", None, "fsdp"),
            P("dp"),
            P("fsdp", "dp"),
            P("dp"),
            P("dp"),
            P("dp"),
            P("dp", "fsdp"),
            P("dp"),
            P("fsdp", "dp"),
            P("dp"),
        ),
        out_specs=(
            P(("dp", "fsdp"), None),
            P(),
            P(("dp", "fsdp"), None),
            P("dp"),
            P("dp"),
            P("dp", None, "fsdp"),
            P("dp"),
            P("dp"),
            P("fsdp", "dp"),
            P("dp"),
            P("dp"),
            P("dp"),
            P("dp", "fsdp"),
            P("dp"),
            P("fsdp", "dp"),
            P("dp"),
        ),
        check_vma=False,
    )
```
